32 devices in a mesh: gz: 2 (over x), gy: 4 (over z), gx: 4 (over y, core).
Axes of the slice: x: 2, y: 2, z: 4, core: 2. Of those that a mesh axis runs over, the one named last changes fastest.
Arguments:
- density: float32 [16, 32, 512], P('gz', 'gy', 'gx'), may hold values from 0.3 to 3
- velocity: float32 [3, 16, 32, 512], P(None, 'gz', 'gy', 'gx'), may hold values from -3 to 3
- pressure: float32 [16, 32, 512], P('gz', 'gy', 'gx'), may hold values from 0.3 to 3
- field: float32 [3, 16, 32, 512], P(None, 'gz', 'gy', 'gx'), may hold values from -3 to 3
- corona: int32 [16], replicated, may hold values from 0 to 1, as said below
Outputs:
- conserved: float32 [5, 16, 32, 512], P(None, 'gz', 'gy', 'gx')
- faces_new: float32 [3, 16, 32, 512], P(None, 'gz', 'gy', 'gx')
The draws below stay inside these ranges and needn't reach their ends.
Inputs may be any that keep to these rules, and one draw needn't show every extreme that they name: `corona`: 1 marks a cooled slab; every slab farther from the midplane than a drawn height (one for each half of z) is cooled, and some other slabs are cooled too.
All inputs are finite; a program needn't handle non-finite values.
Results may differ from the reference program's by a relative error of at most 0.00002.
Values sent between devices are 32-bit elements; how exact they have to be, the bound alone decides.
A program may use at most 64 MiB of HBM per device.

```python
import math
import jax
import jax.numpy as jnp

COOL_STEPS = 8
NX = 512
NY = 32
NZ = 16


def draw_corona(key, part):
    lower_key = jax.random.fold_in(key, 11)
    upper_key = jax.random.fold_in(key, 23)
    extra_key = jax.random.fold_in(key, 37)
    lower_height = jax.random.randint(lower_key, (), NZ // 4, 3 * NZ // 8 + 1)
    upper_height = jax.random.randint(upper_key, (), NZ // 4, 3 * NZ // 8 + 1)
    index = jnp.arange(NZ, dtype=jnp.int32)
    offsets = jnp.abs(2 * index + 1 - NZ)
    threshold = jnp.where(2 * index < NZ, lower_height, upper_height)
    outer = offsets > 2 * threshold
    extra = jax.random.randint(extra_key, (NZ,), 0, 4) == 0
    return jnp.logical_or(outer, extra).astype(jnp.int32)


def shard_levels(own_key, dims, split, least, largest):
    def one(axis_at, shards_of):
        draws = jax.random.uniform(jax.random.fold_in(jax.random.fold_in(own_key, 6), axis_at), (shards_of,), jnp.float32, least / len(split), largest / len(split))
        return jnp.repeat(jnp.exp(draws), dims[axis_at] // shards_of).reshape((-1,) + (1,) * (len(dims) - axis_at - 1))

    level = one(*split[0])
    for cut in split[1:]:
        level = level * one(*cut)
    return level


def noise(stream_key, extent, scale, limit, cuts=(), kind=jnp.bfloat16):
    level = shard_levels(stream_key, extent, cuts, -0.22, 0.18) if cuts else 1.0
    values = jax.random.normal(stream_key, extent, jnp.float32) * scale * level
    return jnp.minimum(jnp.maximum(values, -limit), limit).astype(kind)


def setup_inputs(seed: int = 0) -> dict:
    splits = jax.random.split(jax.random.key(seed), 6)
    density = jnp.clip(jnp.exp(math.log(3.0) - 2.3025851 * jax.random.uniform(splits[0], (NZ, NY, NX), jnp.float32) ** shard_levels(splits[0], (NZ, NY, NX), ((0, 2), (1, 4), (2, 4)), -0.2, 0.2)), 0.3, 3.0)
    velocity = noise(splits[1], (3, NZ, NY, NX), 0.5, 3.0, ((1, 2), (2, 4), (3, 4)), jnp.float32)
    pressure = jnp.clip(jnp.exp(math.log(3.0) - 2.3025851 * jax.random.uniform(splits[2], (NZ, NY, NX), jnp.float32) ** shard_levels(splits[2], (NZ, NY, NX), ((0, 2), (1, 4), (2, 4)), -0.2, 0.2)), 0.3, 3.0)
    field = noise(splits[3], (3, NZ, NY, NX), 0.5, 3.0, ((1, 2), (2, 4), (3, 4)), jnp.float32)
    corona = draw_corona(jax.random.fold_in(splits[5], 71), 0)
    return {"density": density, "velocity": velocity, "pressure": pressure, "field": field, "corona": corona}


adiabatic = 5.0 / 3.0
courant = 0.08
cool_rate = 0.03
gravity = 1.0
cyclic_pairs = ((2, 1), (0, 2), (1, 0))

def shift_up(values, along):
    return jnp.roll(values, -1, along)

def shift_down(values, along):
    return jnp.roll(values, 1, along)

def cool_cells(density, pressure):
    for subcycle in range(COOL_STEPS):
        pressure = pressure / (1.0 + cool_rate * jnp.sqrt(density * pressure))
    return pressure

def state_terms(density, velocity, pressure, magnetic, normal_axis):
    others = [component for component in range(3) if component != normal_axis]
    normal_field = magnetic[normal_axis]
    transverse = magnetic[others[0]] * magnetic[others[0]] + magnetic[others[1]] * magnetic[others[1]]
    squared = transverse + normal_field * normal_field
    total_pressure = pressure + 0.5 * squared
    kinetic = velocity[0] * velocity[0] + velocity[1] * velocity[1] + velocity[2] * velocity[2]
    alignment = velocity[0] * magnetic[0] + velocity[1] * magnetic[1] + velocity[2] * magnetic[2]
    energy = pressure / (adiabatic - 1.0) + 0.5 * density * kinetic + 0.5 * squared
    sound = adiabatic * pressure / density
    along_field = normal_field * normal_field / density
    across_field = transverse / density
    fast_speed = jnp.sqrt(0.5 * (sound + along_field + across_field + jnp.sqrt((sound - along_field - across_field) ** 2 + 4.0 * sound * across_field)))
    normal_speed = velocity[normal_axis]
    conserved = [density] + [density * velocity[component] for component in range(3)] + [energy] + [magnetic[component] for component in others]
    fluxes = [density * normal_speed]
    for component in range(3):
        moment = density * velocity[component] * normal_speed - magnetic[component] * normal_field
        if component == normal_axis:
            moment = moment + total_pressure
        fluxes.append(moment)
    fluxes.append((energy + total_pressure) * normal_speed - normal_field * alignment)
    for component in others:
        fluxes.append(normal_speed * magnetic[component] - velocity[component] * normal_field)
    return (normal_speed, fast_speed, conserved, fluxes)

def interface_flux(density, velocity, pressure, centre, normal_face, normal_axis):
    lower_field = [shift_down(member, normal_axis) for member in centre]
    lower_field[normal_axis] = normal_face
    upper_field = list(centre)
    upper_field[normal_axis] = normal_face
    lower_terms = state_terms(shift_down(density, normal_axis), [shift_down(member, normal_axis) for member in velocity], shift_down(pressure, normal_axis), lower_field, normal_axis)
    upper_terms = state_terms(density, velocity, pressure, upper_field, normal_axis)
    slowest = jnp.minimum(jnp.minimum(lower_terms[0] - lower_terms[1], upper_terms[0] - upper_terms[1]), 0.0)
    fastest = jnp.maximum(jnp.maximum(lower_terms[0] + lower_terms[1], upper_terms[0] + upper_terms[1]), 0.0)
    inverse = 1.0 / (fastest - slowest)
    result = []
    for member in range(7):
        lower_flux = lower_terms[3][member]
        upper_flux = upper_terms[3][member]
        jump = upper_terms[2][member] - lower_terms[2][member]
        result.append((fastest * lower_flux - slowest * upper_flux + slowest * fastest * jump) * inverse)
    return result

def advance(extended, height):
    density = extended[0]
    velocity = [extended[1], extended[2], extended[3]]
    pressure = extended[4]
    faces = [extended[5], extended[6], extended[7]]
    centre = [0.5 * (faces[component] + shift_up(faces[component], component)) for component in range(3)]
    fluxes = [interface_flux(density, velocity, pressure, centre, faces[direction], direction) for direction in range(3)]
    kinetic = velocity[0] * velocity[0] + velocity[1] * velocity[1] + velocity[2] * velocity[2]
    squared = centre[0] * centre[0] + centre[1] * centre[1] + centre[2] * centre[2]
    energy = pressure / (adiabatic - 1.0) + 0.5 * density * kinetic + 0.5 * squared
    conserved = [density, density * velocity[0], density * velocity[1], density * velocity[2], energy]
    inner = (slice(2, -2), slice(2, -2), slice(2, -2))
    updated = []
    for member in range(5):
        change = jnp.zeros_like(density)
        for direction in range(3):
            change = change + shift_up(fluxes[direction][member], direction) - fluxes[direction][member]
        updated.append((conserved[member] - courant * change)[inner])
    pull = -gravity * height[:, None, None]
    updated[1] = updated[1] + courant * density[inner] * pull
    updated[4] = updated[4] + courant * density[inner] * velocity[0][inner] * pull
    electric = []
    for edge in range(3):
        first, second = cyclic_pairs[edge]
        first_others = [component for component in range(3) if component != first]
        second_others = [component for component in range(3) if component != second]
        first_flux = fluxes[first][5 + first_others.index(second)]
        second_flux = fluxes[second][5 + second_others.index(first)]
        electric.append(0.25 * (second_flux + shift_down(second_flux, first) - first_flux - shift_down(first_flux, second)))
    new_faces = []
    for component in range(3):
        across, beyond = cyclic_pairs[component]
        curl = shift_up(electric[beyond], across) - electric[beyond] - (shift_up(electric[across], beyond) - electric[across])
        new_faces.append((faces[component] - courant * curl)[inner])
    return (jnp.stack(updated), jnp.stack(new_faces))

def reference(density, velocity, pressure, field, corona):
    cooled = jnp.where(corona[:, None, None] == 1, cool_cells(density, pressure), pressure)
    stacked = jnp.concatenate([density[None], velocity, cooled[None], field], 0)
    extended = jnp.pad(stacked, ((0, 0), (0, 0), (0, 0), (2, 2)), mode='wrap')
    extended = jnp.pad(extended, ((0, 0), (0, 0), (2, 2), (0, 0)), mode='edge')
    extended = jnp.pad(extended, ((0, 0), (2, 2), (0, 0), (0, 0)), mode='edge')
    height = (2 * jnp.arange(NZ, dtype=jnp.int32) + 1 - NZ).astype(jnp.float32) / NZ
    return advance(extended, height)
```

```python
import functools

import jax
import jax.numpy as jnp
from jax import lax
from jax.experimental import pallas as pl
from jax.experimental.pallas import tpu as pltpu
from jax.sharding import PartitionSpec as P

COOL_STEPS = 8
adiabatic = 5.0 / 3.0
courant = 0.08
cool_rate = 0.03
gravity = 1.0

MESH = pl.DeviceIdType.MESH
DIRS = ((0, -1), (0, 1), (-1, 0), (1, 0), (-1, -1), (-1, 1), (1, -1), (1, 1))
ALL = ((0, 0),) + DIRS
SKIP = ((-1, -1, -1), (1, 1, 1))
FIELDS = 8
FZ, FY, FX = 5, 6, 7
TINY = 1e-36


def root(values):
    return values * lax.rsqrt(values)


def fast_speed(half_sound, half_squared, transverse_sq, half_inverse):
    both = half_squared * (2.0 * half_inverse)
    gap = half_sound - both
    inner = gap * gap + (4.0 * half_sound) * (transverse_sq * half_inverse)
    return root(half_sound + both + root(jnp.maximum(inner, TINY)))


def state_terms(cell, velocity, pressure, magnetic, axis):
    rho, half_inverse, half_sound, hydro, momenta = cell
    one, two = [c for c in range(3) if c != axis]
    normal = magnetic[axis]
    normal_sq = normal * normal
    transverse_sq = magnetic[one] * magnetic[one] + magnetic[two] * magnetic[two]
    half = 0.5 * (transverse_sq + normal_sq)
    energy = hydro + half
    tension = pressure + half - normal_sq
    align = velocity[one] * magnetic[one] + velocity[two] * magnetic[two]
    speed = fast_speed(half_sound, half, transverse_sq, half_inverse)
    va = velocity[axis]
    conserved = [rho] + list(momenta) + [energy]
    work = tension * va - normal * align
    return va, speed, conserved, tension, work, velocity, magnetic


def cell_terms(rho, velocity, pressure):
    half_inverse = 0.5 / rho
    momenta = [rho * v for v in velocity]
    kinetic = momenta[0] * velocity[0] + momenta[1] * velocity[1] + momenta[2] * velocity[2]
    hydro = pressure * (1.0 / (adiabatic - 1.0)) + 0.5 * kinetic
    return rho, half_inverse, adiabatic * pressure * half_inverse, hydro, momenta


def hll(lower, upper, axis, want=range(7)):
    low, high = lower[0] - lower[1], lower[0] + lower[1]
    slow = jnp.minimum(jnp.minimum(low, upper[0] - upper[1]), 0.0)
    fast = jnp.maximum(jnp.maximum(high, upper[0] + upper[1]), 0.0)
    inverse = 1.0 / (fast - slow)
    wl = fast * inverse
    wu = -slow * inverse
    wj = slow * wl
    al = wl * lower[0] - wj
    au = wu * upper[0] + wj
    normal = upper[6][axis]
    bl, bu = wl * normal, wu * normal
    others = [c for c in range(3) if c != axis]

    def carried(one, two):
        return al * one + au * two

    def member(m):
        if m == 0:
            return carried(lower[2][0], upper[2][0])
        if m <= 3:
            c = m - 1
            value = carried(lower[2][m], upper[2][m])
            if c == axis:
                return value + (wl * lower[3] + wu * upper[3])
            return value - (bl * lower[6][c] + bu * upper[6][c])
        if m == 4:
            return carried(lower[2][4], upper[2][4]) + (wl * lower[4] + wu * upper[4])
        c = others[m - 5]
        return carried(lower[6][c], upper[6][c]) - (bl * lower[5][c] + bu * upper[5][c])

    return {m: member(m) for m in want}


def kernel(
    sizes, rho_hbm, vel_hbm, pre_hbm, fld_hbm, corona_hbm, res,
    stack, raw, marks, sbuf, rbuf, pad, ext, xsend, xrecv, flux, edge, turned, load_sem, send_sem, recv_sem, ready,
):
    nz, ny, nx, gz, gy, gx = sizes
    plane = nz * ny
    wide = ny + 3
    tall = nx + 16
    iz, iy, ix = lax.axis_index("gz"), lax.axis_index("gy"), lax.axis_index("gx")
    left = lax.rem(ix + gx - 1, gx)
    right = lax.rem(ix + 1, gx)

    has_z = {-1: iz > 0, 0: None, 1: iz < gz - 1}
    has_y = {-1: iy > 0, 0: None, 1: iy < gy - 1}

    def exists(dz, dy):
        if dz == 0:
            return has_y[dy]
        if dy == 0:
            return has_z[dz]
        return jnp.logical_and(has_z[dz], has_y[dy])

    loads = [
        pltpu.make_async_copy(src, dst, load_sem.at[i])
        for i, (src, dst) in enumerate((
            (rho_hbm, stack.at[pl.ds(0, plane)]),
            (pre_hbm, raw),
            (corona_hbm, marks),
            (fld_hbm, stack.at[pl.ds(FZ * plane, 3 * plane)]),
            (vel_hbm, stack.at[pl.ds(plane, 3 * plane)]),
        ))
    ]
    for load in loads:
        load.start()

    def when(dz, dy, run):
        if dz == 0 and dy == 0:
            run()
        else:
            pl.when(exists(dz, dy))(run)

    def steps(dz, dy):
        return [dx for dx in (0, -1, 1) if (dz, dy, dx) not in SKIP and (dz, dy, dx) != (0, 0, 0)]

    def place(dz, dy, dx):
        where = {}
        if dz != 0:
            where["gz"] = iz + dz
        if dy != 0:
            where["gy"] = iy + dy
        if dx != 0:
            where["gx"] = left if dx < 0 else right
        return where

    barrier = pltpu.get_barrier_semaphore()
    for dz, dy in ALL:
        if dy >= 0:
            def greet():
                for dx in steps(dz, dy):
                    pl.semaphore_signal(
                        barrier, inc=1, device_id=place(dz, dy, dx), device_id_type=MESH
                    )
            when(dz, dy, greet)

    for load in loads[:3]:
        load.wait()
    for z in range(nz):
        rows = pl.ds(z * ny, ny)
        rho = stack[rows, :]
        start = raw[rows, :]
        p = start
        for _ in range(COOL_STEPS):
            p = p / (1.0 + cool_rate * jnp.sqrt(rho * p))
        mark = jnp.full(p.shape, marks[iz * nz + z], jnp.int32)
        stack[pl.ds(4 * plane + z * ny, ny), :] = jnp.where(mark == 1, p, start)

    for load in loads[3:]:
        load.wait()

    def y_rows(f, y):
        return stack[pl.ds(f * plane + y, nz, stride=ny), :]

    def z_rows(f, z):
        return stack[pl.ds(f * plane + z * ny, ny), :]

    def one_row(f, z, y):
        return stack[pl.ds(f * plane + z * ny + y, 1), :]

    zf, yf = FIELDS * ny, FIELDS * nz
    for f in range(FIELDS):
        for d, at in ((0, 0), (1, ny - 1)):
            sbuf[d, pl.ds(f * nz, nz), :] = y_rows(f, at)
        for d, at in ((2, 0), (3, nz - 1)):
            sbuf[d, pl.ds(f * ny, ny), :] = z_rows(f, at)
        for d in range(4, 8):
            dz, dy = DIRS[d]
            sbuf[d, pl.ds(f, 1), :] = one_row(f, 0 if dz < 0 else nz - 1, 0 if dy < 0 else ny - 1)
    sbuf[0, pl.ds(yf, nz), :] = y_rows(FY, 1)
    sbuf[2, pl.ds(zf, ny), :] = z_rows(FZ, 1)
    sbuf[5, pl.ds(FIELDS, 1), :] = one_row(FZ, 1, ny - 1)
    sbuf[6, pl.ds(FIELDS, 1), :] = one_row(FY, nz - 1, 1)
    size = (yf + nz, yf, zf + ny, zf, 16, 16, 16, 16)

    pl.semaphore_wait(
        barrier,
        2 + sum(
            exists(dz, dy).astype(jnp.int32) * len(steps(dz, dy)) for dz, dy in DIRS if dy <= 0
        ),
    )

    def ready_at(dz, dx):
        return ready.at[3 * (dz + 1) + dx + 1]

    for dz, dy in DIRS:
        if dy < 0:
            def answer():
                for dx in steps(dz, dy):
                    pl.semaphore_signal(
                        ready_at(dz, dx), inc=1, device_id=place(dz, dy, dx), device_id_type=MESH
                    )
            when(dz, dy, answer)

    def message(dz, dy, dx):
        d = ALL.index((dz, dy))
        if dx == 0:
            rows = pl.ds(0, size[d - 1])
            src, dst = sbuf.at[d - 1, rows], rbuf.at[d - 1, rows]
        else:
            rows = pl.ds(0, 9) if dx < 0 else pl.ds(16, 8)
            src, dst = xsend.at[rows], xrecv.at[d, rows]
        return pltpu.make_async_remote_copy(
            src_ref=src,
            dst_ref=dst,
            send_sem=send_sem.at[3 * d + dx + 1],
            recv_sem=recv_sem.at[3 * d + dx + 1],
            device_id=place(dz, dy, dx),
            device_id_type=MESH,
        )

    def post(want, sides):
        for dz, dy in ALL:
            if dy == want:
                def go():
                    for dx in steps(dz, dy):
                        if dx in sides:
                            if dy > 0:
                                pl.semaphore_wait(ready_at(-dz, -dx), 1)
                            message(dz, dy, dx).start()
                when(dz, dy, go)

    post(-1, (0,))
    post(0, (0,))

    for f in range(FIELDS):
        for z in range(nz):
            pad[pl.ds(f * 128 + (z + 1) * wide + 1, ny), :] = z_rows(f, z)

    for d in range(4):
        dz, dy = DIRS[d]
        own = DIRS.index((-dz, -dy))
        step = nz if dz == 0 else ny

        @pl.when(jnp.logical_not(exists(-dz, -dy)))
        def _():
            for f in range(FIELDS):
                rbuf[d, pl.ds(f * step, step), :] = sbuf[own, pl.ds(f * step, step), :]
            if dz + dy < 0:
                f = FY if dz == 0 else FZ
                rbuf[d, pl.ds(FIELDS * step, step), :] = sbuf[own, pl.ds(f * step, step), :]

    for f in range(FIELDS):
        ext[pl.ds(f * tall + 8, nx), :] = pad[pl.ds(f * 128, 128), :].T
    xsend[pl.ds(0, FIELDS), :] = ext[pl.ds(8, FIELDS, stride=tall), :]
    xsend[pl.ds(FIELDS, 1), :] = ext[pl.ds(FX * tall + 9, 1), :]
    xsend[pl.ds(16, FIELDS), :] = ext[pl.ds(7 + nx, FIELDS, stride=tall), :]

    post(-1, (-1, 1))
    post(0, (-1, 1))
    def aside(values, by):
        return pltpu.roll(values, by % nx, 1)

    def tiers(values, by):
        return pltpu.roll(values, by % ny, 0)

    def keep(axis, start, count, stride, found):
        for m, value in found.items():
            flux[7 * axis + m, pl.ds(start, count, stride=stride), :] = value

    def start_of(z, y):
        return (z + 1) * wide + y + 1

    past = None
    for z in range(nz):
        rho, vel, pre = z_rows(0, z), [z_rows(1 + c, z) for c in range(3)], z_rows(4, z)
        faces = [z_rows(5 + c, z) for c in range(3)]
        cell = cell_terms(rho, vel, pre)
        centre = [
            0.5 * (faces[0] + z_rows(FZ, z + 1)) if z < nz - 1 else None,
            0.5 * (faces[1] + tiers(faces[1], -1)),
            0.5 * (faces[2] + aside(faces[2], -1)),
        ]
        if z > 0:
            lower = state_terms(past[0], past[1], past[2], [faces[0]] + past[3][1:], 0)
            upper = state_terms(cell, vel, pre, [faces[0]] + centre[1:], 0)
            keep(0, start_of(z, 0), ny, 1, hll(lower, upper, 0))
        if z < nz - 1:
            for axis, below in ((1, lambda v: tiers(v, 1)), (2, lambda v: aside(v, 1))):
                lrho, lvel = below(rho), [below(v) for v in vel]
                lcell = (
                    lrho, below(cell[1]), below(cell[2]), below(cell[3]),
                    [lrho * v for v in lvel],
                )
                lmag = [faces[c] if c == axis else below(centre[c]) for c in range(3)]
                umag = [faces[c] if c == axis else centre[c] for c in range(3)]
                lower = state_terms(lcell, lvel, below(pre), lmag, axis)
                upper = state_terms(cell, vel, pre, umag, axis)
                keep(axis, start_of(z, 0), ny, 1, hll(lower, upper, axis))
        past = (cell, vel, pre, centre)

    post(1, (0,))
    post(1, (-1, 1))

    for d in range(8):
        dz, dy = DIRS[d]

        @pl.when(exists(-dz, -dy))
        def _():
            message(dz, dy, 0).wait_recv()

    for f in range(FIELDS):
        base = f * 128
        pad[pl.ds(base + wide, nz, stride=wide), :] = rbuf[1, pl.ds(f * nz, nz), :]
        pad[pl.ds(base + wide + ny + 1, nz, stride=wide), :] = rbuf[0, pl.ds(f * nz, nz), :]
        pad[pl.ds(base + 1, ny), :] = rbuf[3, pl.ds(f * ny, ny), :]
        pad[pl.ds(base + (nz + 1) * wide + 1, ny), :] = rbuf[2, pl.ds(f * ny, ny), :]
    pad[pl.ds(FY * 128 + wide + ny + 2, nz, stride=wide), :] = rbuf[0, pl.ds(yf, nz), :]
    pad[pl.ds(FZ * 128 + (nz + 2) * wide + 1, ny), :] = rbuf[2, pl.ds(zf, ny), :]

    def spot(z, y):
        return (z + 1) * wide + y + 1

    for d in range(4, 8):
        dz, dy = DIRS[d]
        zg, yg = (nz if dz < 0 else -1), (ny if dy < 0 else -1)
        zc, yc = min(max(zg, 0), nz - 1), min(max(yg, 0), ny - 1)
        both = exists(-dz, -dy)
        extra = {5: (FZ, 1, 0), 6: (FY, 0, 1)}.get(d)

        @pl.when(both)
        def _():
            pad[pl.ds(spot(zg, yg), FIELDS, stride=128), :] = rbuf[d, pl.ds(0, FIELDS), :]
            if extra:
                f, ez, ey = extra
                pad[pl.ds(f * 128 + spot(zg + ez, yg + ey), 1), :] = rbuf[d, pl.ds(FIELDS, 1), :]

        def copy_rows(zs, ys):
            pad[pl.ds(spot(zg, yg), FIELDS, stride=128), :] = pad[
                pl.ds(spot(zs, ys), FIELDS, stride=128), :
            ]

        @pl.when(jnp.logical_not(has_z[-dz]))
        def _():
            copy_rows(zc, yg)
            if extra:
                f, ez, ey = extra
                pad[pl.ds(f * 128 + spot(zg + ez, yg + ey), 1), :] = pad[
                    pl.ds(f * 128 + spot(zc, yg + ey), 1), :
                ]

        @pl.when(jnp.logical_and(has_z[-dz], jnp.logical_not(has_y[-dy])))
        def _():
            copy_rows(zg, yc)
            if extra:
                f, ez, ey = extra
                pad[pl.ds(f * 128 + spot(zg + ez, yg + ey), 1), :] = pad[
                    pl.ds(f * 128 + spot(zg + ez, yc), 1), :
                ]

    away = (wide, 1)

    def border(axis, start, count, stride, want):
        def load(f, at):
            return pad[pl.ds(f * 128 + at, count, stride=stride), :]

        def state(at):
            vel = [load(1 + c, at) for c in range(3)]
            pre = load(4, at)
            cell = cell_terms(load(0, at), vel, pre)
            centre = [None] * 3
            for c in range(3):
                if c != axis:
                    face = load(5 + c, at)
                    after = aside(face, -1) if c == 2 else load(5 + c, at + away[c])
                    centre[c] = 0.5 * (face + after)
            return cell, vel, pre, centre

        normal = load(5 + axis, start)
        cell, vel, pre, centre = state(start)
        if axis == 2:
            lvel = [aside(v, 1) for v in vel]
            lrho = aside(cell[0], 1)
            lcell = (
                lrho, aside(cell[1], 1), aside(cell[2], 1), aside(cell[3], 1),
                [lrho * v for v in lvel],
            )
            lpre = aside(pre, 1)
            lcentre = [aside(centre[0], 1), aside(centre[1], 1), None]
        else:
            lcell, lvel, lpre, lcentre = state(start - away[axis])
        lcentre[axis] = centre[axis] = normal
        lower = state_terms(lcell, lvel, lpre, lcentre, axis)
        upper = state_terms(cell, vel, pre, centre, axis)
        keep(axis, start, count, stride, hll(lower, upper, axis, want))

    def across(z):
        return start_of(z, 0), ny, 1

    def along(y):
        return start_of(0, y), nz, wide

    every = range(7)
    border(0, *across(0), every)
    border(0, *across(nz), every)
    border(0, *along(ny - 1), every)
    border(0, start_of(0, -1), nz + 1, wide, (5,))
    border(0, *along(ny), (5,))
    border(1, *along(0), every)
    border(1, *along(ny), every)
    border(1, *across(nz - 1), every)
    border(1, start_of(-1, 0), ny + 1, 1, (5,))
    border(1, *across(nz), (5,))
    border(2, *along(ny - 1), every)
    border(2, *across(nz - 1), every)
    border(2, *along(-1), (6,))
    border(2, *along(ny), (6,))
    border(2, *across(-1), (5,))
    border(2, *across(nz), (5,))

    for dz, dy in ALL:
        def arrived():
            for dx in steps(-dz, -dy):
                if dx != 0:
                    message(-dz, -dy, dx).wait_recv()
        when(dz, dy, arrived)

    for f in range(FIELDS):
        ext[pl.ds(f * tall + 8, nx), :] = pad[pl.ds(f * 128, 128), :].T
    lane = lax.broadcasted_iota(jnp.int32, (8, 128), 1)
    slab = iz * nz - 1
    zglobal = jnp.zeros((8, 128), jnp.int32) + slab
    for j in range(1, nz + 3):
        zglobal = zglobal + (lane >= j * wide).astype(jnp.int32)
    height = (2 * zglobal + 1 - nz * gz).astype(jnp.float32) * (1.0 / (nz * gz))
    pull = -gravity * courant * height

    zat = jnp.zeros((8, 128), jnp.int32) - 1
    for j in range(1, nz + 3):
        zat = zat + (lane >= j * wide).astype(jnp.int32)
    yat = lane - (zat + 1) * wide - 1

    def turn(values, by):
        return pltpu.roll(values, by % 128, 1)

    def gather(dx, row):
        def taken(dz, dy):
            return xrecv[ALL.index((-dz, -dy)), pl.ds(row, 8), :]

        def line(dz):
            shift = dz * nz * wide
            mid = turn(taken(dz, 0), shift)
            low, high = turn(mid, -1), turn(mid, 1)
            if (dz, -1, dx) not in SKIP:
                low = jnp.where(has_y[-1], turn(taken(dz, -1), shift - ny), low)
            beyond = turn(mid, 2)
            if (dz, 1, dx) not in SKIP:
                over = turn(taken(dz, 1), shift + ny)
                high = jnp.where(has_y[1], over, high)
                beyond = jnp.where(has_y[1], over, beyond)
            out = jnp.where(yat < 0, low, mid)
            return jnp.where(yat == ny, high, jnp.where(yat > ny, beyond, out))

        mid = line(0)
        low = jnp.where(has_z[-1], line(-1), turn(mid, -wide))
        over = line(1)
        high = jnp.where(has_z[1], over, turn(mid, wide))
        beyond = jnp.where(has_z[1], over, turn(mid, 2 * wide))
        out = jnp.where(zat < 0, low, mid)
        return jnp.where(zat == nz, high, jnp.where(zat > nz, beyond, out))

    ext[pl.ds(8 + nx, FIELDS, stride=tall), :] = gather(1, 0)
    ext[pl.ds(FX * tall + 9 + nx, 1), :] = gather(1, FIELDS)[:1]
    ext[pl.ds(7, FIELDS, stride=tall), :] = gather(-1, 16)
    def up(values, axis):
        return pltpu.roll(values, 128 - (wide if axis == 0 else 1), 1)

    def down(values, axis):
        return pltpu.roll(values, wide if axis == 0 else 1, 1)

    def side(x):
        r = 8 + x
        now = [ext[pl.ds(f * tall + r, 8), :] for f in range(FIELDS)]
        below = [ext[pl.ds(f * tall + r - 1, 8), :] for f in range(7)]
        rho, vel, pre, faces = now[0], now[1:4], now[4], now[5:8]
        centre = [
            0.5 * (faces[0] + up(faces[0], 0)),
            0.5 * (faces[1] + up(faces[1], 1)),
            0.5 * (faces[2] + ext[pl.ds(FX * tall + r + 1, 8), :]),
        ]
        cell = cell_terms(rho, vel, pre)
        fluxes = []
        for axis in range(3):
            if axis == 2:
                lrho, lvel, lpre = below[0], below[1:4], below[4]
                lcell = cell_terms(lrho, lvel, lpre)
                lmag = [
                    0.5 * (below[5] + up(below[5], 0)),
                    0.5 * (below[6] + up(below[6], 1)),
                    faces[2],
                ]
            else:
                lrho, lpre = down(rho, axis), down(pre, axis)
                lvel = [down(v, axis) for v in vel]
                lcell = (
                    lrho, down(cell[1], axis), down(cell[2], axis), down(cell[3], axis),
                    [lrho * v for v in lvel],
                )
                lmag = [faces[c] if c == axis else down(centre[c], axis) for c in range(3)]
            umag = [faces[c] if c == axis else centre[c] for c in range(3)]
            lower = state_terms(lcell, lvel, lpre, lmag, axis)
            upper = state_terms(cell, vel, pre, umag, axis)
            fluxes.append(hll(lower, upper, axis))
        squared = centre[0] * centre[0] + centre[1] * centre[1] + centre[2] * centre[2]
        base = [rho] + list(cell[4]) + [cell[3] + 0.5 * squared]
        fz, fy, fx = fluxes

        def after(values):
            return pltpu.roll(values, 7, 0)

        def before(values):
            return pltpu.roll(values, 1, 0)

        outs = []
        for m in range(5):
            change = up(fz[m], 0) - fz[m] + up(fy[m], 1) - fy[m] + after(fx[m]) - fx[m]
            value = base[m] - courant * change
            if m == 1:
                value = value + rho * pull
            if m == 4:
                value = value + cell[4][0] * pull
            outs.append(value)
        ex = 0.25 * (fz[5] + down(fz[5], 1) - fy[5] - down(fy[5], 0))
        ey = 0.25 * (fx[5] + down(fx[5], 0) - fz[6] - before(fz[6]))
        ez = 0.25 * (fy[6] + before(fy[6]) - fx[6] - down(fx[6], 1))
        outs.append(faces[0] - courant * ((after(ey) - ey) - (up(ex, 1) - ex)))
        outs.append(faces[1] - courant * ((up(ex, 0) - ex) - (after(ez) - ez)))
        outs.append(faces[2] - courant * ((up(ez, 1) - ez) - (up(ey, 0) - ey)))
        return outs

    first, last = side(-1), side(nx - 6)
    for m in range(FIELDS):
        edge[pl.ds(3 * m, 2), :] = last[m][4:6]
        edge[pl.ds(3 * m + 2, 1), :] = first[m][1:2]
    turned[...] = edge[...].T

    def got(axis, m, at):
        return flux[7 * axis + m, pl.ds(at, ny), :]

    def ex_at(at):
        return 0.25 * (got(0, 5, at) + got(0, 5, at - 1) - got(1, 5, at) - got(1, 5, at - wide))

    def ey_at(at):
        one = got(0, 6, at)
        return 0.25 * (got(2, 5, at) + got(2, 5, at - wide) - one - aside(one, 1))

    def ez_at(at):
        one = got(1, 6, at)
        return 0.25 * (one + aside(one, 1) - got(2, 6, at) - got(2, 6, at - 1))

    column = lax.broadcasted_iota(jnp.int32, (ny, nx), 1)
    ends = jnp.logical_or(column == 0, column >= nx - 2)
    ex_here, ey_here = ex_at(start_of(0, 0)), ey_at(start_of(0, 0))
    for z in range(nz):
        at = start_of(z, 0)
        rho, vel, pre = z_rows(0, z), [z_rows(1 + c, z) for c in range(3)], z_rows(4, z)
        faces = [z_rows(5 + c, z) for c in range(3)]
        above = pad[pl.ds(FZ * 128 + at + wide, ny), :]
        beside = pad[pl.ds(FY * 128 + at + 1, ny), :]
        centre = [
            0.5 * (faces[0] + above), 0.5 * (faces[1] + beside),
            0.5 * (faces[2] + aside(faces[2], -1)),
        ]
        cell = cell_terms(rho, vel, pre)
        squared = centre[0] * centre[0] + centre[1] * centre[1] + centre[2] * centre[2]
        start = [rho] + list(cell[4]) + [cell[3] + 0.5 * squared]
        level = jnp.zeros((ny, nx), jnp.int32) + (2 * (iz * nz + z) + 1 - nz * gz)
        force = -gravity * courant * (level.astype(jnp.float32) * (1.0 / (nz * gz)))
        values = []
        for m in range(5):
            fx, fy, fz = got(2, m, at), got(1, m, at), got(0, m, at)
            change = (
                aside(fx, -1) - fx + got(1, m, at + 1) - fy + got(0, m, at + wide) - fz
            )
            value = start[m] - courant * change
            if m == 1:
                value = value + rho * force
            if m == 4:
                value = value + cell[4][0] * force
            values.append(value)
        ex, ey, ez = ex_here, ey_here, ez_at(at)
        ex_here, ey_here = ex_at(at + wide), ey_at(at + wide)
        values.append(faces[0] - courant * ((aside(ey, -1) - ey) - (ex_at(at + 1) - ex)))
        values.append(faces[1] - courant * ((ex_here - ex) - (aside(ez, -1) - ez)))
        values.append(faces[2] - courant * ((ez_at(at + 1) - ez) - (ey_here - ey)))
        ring = turned[pl.ds(at, ny), :]
        for m in range(FIELDS):
            res[pl.ds(m * plane + z * ny, ny), :] = jnp.where(
                ends, pltpu.roll(ring, (nx - 2 - 3 * m) % nx, 1), values[m]
            )
    for dz, dy in ALL:
        def sent():
            for dx in steps(dz, dy):
                message(dz, dy, dx).wait_send()
        when(dz, dy, sent)


def unload_kernel(sizes, res, cons_ref, face_ref, sem):
    nz, ny = sizes
    plane = nz * ny
    copies = [
        pltpu.make_async_copy(res.at[pl.ds(0, 5 * plane)], cons_ref, sem.at[0]),
        pltpu.make_async_copy(res.at[pl.ds(5 * plane, 3 * plane)], face_ref, sem.at[1]),
    ]
    for copy in copies:
        copy.start()
    for copy in copies:
        copy.wait()


def on_device(sizes, density, velocity, pressure, field, corona):
    nz, ny, nx = density.shape
    gz, gy, gx = sizes
    plane = nz * ny
    hbm = pl.BlockSpec(memory_space=pltpu.HBM)
    vmem = pl.BlockSpec(memory_space=pltpu.VMEM)
    f32 = jnp.float32
    rows = FIELDS * max(nz, ny) + max(nz, ny)
    result = pl.pallas_call(
        functools.partial(kernel, (nz, ny, nx, gz, gy, gx)),
        out_shape=pltpu.VMEM((FIELDS * plane, nx), f32),
        in_specs=[hbm] * 5,
        out_specs=vmem,
        scratch_shapes=[
            pltpu.VMEM((FIELDS * plane, nx), f32),
            pltpu.VMEM((plane, nx), f32),
            pltpu.SMEM(corona.shape, jnp.int32),
            pltpu.VMEM((8, rows, nx), f32),
            pltpu.VMEM((8, rows, nx), f32),
            pltpu.VMEM((FIELDS * 128, nx), f32),
            pltpu.VMEM((FIELDS * (nx + 16), 128), f32),
            pltpu.VMEM((24, 128), f32),
            pltpu.VMEM((9, 24, 128), f32),
            pltpu.VMEM((21, 128, nx), f32),
            pltpu.VMEM((128, 128), f32),
            pltpu.VMEM((128, 128), f32),
            pltpu.SemaphoreType.DMA((5,)),
            pltpu.SemaphoreType.DMA((27,)),
            pltpu.SemaphoreType.DMA((27,)),
            pltpu.SemaphoreType.REGULAR((9,)),
        ],
        compiler_params=pltpu.CompilerParams(
            collective_id=0, has_side_effects=True, vmem_limit_bytes=16 << 20
        ),
    )(
        *(
            pltpu.with_memory_space_constraint(x, pltpu.HBM)
            for x in (
                density.reshape(plane, nx),
                velocity.reshape(3 * plane, nx),
                pressure.reshape(plane, nx),
                field.reshape(3 * plane, nx),
                corona,
            )
        )
    )
    conserved, faces = pl.pallas_call(
        functools.partial(unload_kernel, (nz, ny)),
        out_shape=(
            jax.ShapeDtypeStruct((5 * plane, nx), f32),
            jax.ShapeDtypeStruct((3 * plane, nx), f32),
        ),
        in_specs=[vmem],
        out_specs=(hbm, hbm),
        scratch_shapes=[
            pltpu.SemaphoreType.DMA((2,)),
        ],
        compiler_params=pltpu.CompilerParams(vmem_limit_bytes=16 << 20),
    )(result)
    return conserved.reshape(5, nz, ny, nx), faces.reshape(3, nz, ny, nx)


def solution(mesh):
    sizes = tuple(mesh.shape[axis] for axis in ("gz", "gy", "gx"))
    return jax.shard_map(
        functools.partial(on_device, sizes),
        mesh=mesh,
        in_specs=(
            P("gz", "gy", "gx"),
            P(None, "gz", "gy", "gx"),
            P("gz", "gy", "gx"),
            P(None, "gz", "gy", "gx"),
            P(),
        ),
        out_specs=(P(None, "gz", "gy", "gx"), P(None, "gz", "gy", "gx")),
        check_vma=False,
    )
```

```python
import functools

import jax
import jax.numpy as jnp
from jax import lax
from jax.experimental import pallas as pl
from jax.experimental.pallas import tpu as pltpu
from jax.sharding import PartitionSpec as P

COOL_STEPS = 8
adiabatic = 5.0 / 3.0
courant = 0.08
cool_rate = 0.03
gravity = 1.0

MESH = pl.DeviceIdType.MESH
DIRS = ((0, -1), (0, 1), (-1, 0), (1, 0), (-1, -1), (-1, 1), (1, -1), (1, 1))
ALL = ((0, 0),) + DIRS
SKIP = ((-1, -1, -1), (1, 1, 1))
FIELDS = 8
FZ, FY, FX = 5, 6, 7
TINY = 1e-36


def root(values):
    return values * lax.rsqrt(values)


def fast_speed(half_sound, half_squared, transverse_sq, half_inverse):
    both = half_squared * (2.0 * half_inverse)
    gap = half_sound - both
    inner = gap * gap + (4.0 * half_sound) * (transverse_sq * half_inverse)
    return root(half_sound + both + root(jnp.maximum(inner, TINY)))


def state_terms(cell, velocity, pressure, magnetic, axis):
    rho, half_inverse, half_sound, hydro, momenta = cell
    one, two = [c for c in range(3) if c != axis]
    normal = magnetic[axis]
    normal_sq = normal * normal
    transverse_sq = magnetic[one] * magnetic[one] + magnetic[two] * magnetic[two]
    half = 0.5 * (transverse_sq + normal_sq)
    energy = hydro + half
    tension = pressure + half - normal_sq
    align = velocity[one] * magnetic[one] + velocity[two] * magnetic[two]
    speed = fast_speed(half_sound, half, transverse_sq, half_inverse)
    va = velocity[axis]
    conserved = [rho] + list(momenta) + [energy]
    work = tension * va - normal * align
    return va, speed, conserved, tension, work, velocity, magnetic


def cell_terms(rho, velocity, pressure):
    half_inverse = 0.5 / rho
    momenta = [rho * v for v in velocity]
    kinetic = momenta[0] * velocity[0] + momenta[1] * velocity[1] + momenta[2] * velocity[2]
    hydro = pressure * (1.0 / (adiabatic - 1.0)) + 0.5 * kinetic
    return rho, half_inverse, adiabatic * pressure * half_inverse, hydro, momenta


def hll(lower, upper, axis, want=range(7)):
    low, high = lower[0] - lower[1], lower[0] + lower[1]
    slow = jnp.minimum(jnp.minimum(low, upper[0] - upper[1]), 0.0)
    fast = jnp.maximum(jnp.maximum(high, upper[0] + upper[1]), 0.0)
    inverse = 1.0 / (fast - slow)
    wl = fast * inverse
    wu = -slow * inverse
    wj = slow * wl
    al = wl * lower[0] - wj
    au = wu * upper[0] + wj
    normal = upper[6][axis]
    bl, bu = wl * normal, wu * normal
    others = [c for c in range(3) if c != axis]

    def carried(one, two):
        return al * one + au * two

    def member(m):
        if m == 0:
            return carried(lower[2][0], upper[2][0])
        if m <= 3:
            c = m - 1
            value = carried(lower[2][m], upper[2][m])
            if c == axis:
                return value + (wl * lower[3] + wu * upper[3])
            return value - (bl * lower[6][c] + bu * upper[6][c])
        if m == 4:
            return carried(lower[2][4], upper[2][4]) + (wl * lower[4] + wu * upper[4])
        c = others[m - 5]
        return carried(lower[6][c], upper[6][c]) - (bl * lower[5][c] + bu * upper[5][c])

    return {m: member(m) for m in want}


def kernel(
    sizes, rho_hbm, vel_hbm, pre_hbm, fld_hbm, corona_hbm, res, turned,
    stack, raw, marks, sbuf, rbuf, pad, ext, xsend, xrecv, esend, erecv, flux, edge, load_sem, send_sem, recv_sem, ready,
):
    nz, ny, nx, gz, gy, gx = sizes
    plane = nz * ny
    wide = ny + 3
    tall = nx + 16
    iz, iy, ix = lax.axis_index("gz"), lax.axis_index("gy"), lax.axis_index("gx")
    left = lax.rem(ix + gx - 1, gx)
    right = lax.rem(ix + 1, gx)

    has_z = {-1: iz > 0, 0: None, 1: iz < gz - 1}
    has_y = {-1: iy > 0, 0: None, 1: iy < gy - 1}

    def exists(dz, dy):
        if dz == 0:
            return has_y[dy]
        if dy == 0:
            return has_z[dz]
        return jnp.logical_and(has_z[dz], has_y[dy])

    loads = [
        pltpu.make_async_copy(src, dst, load_sem.at[i])
        for i, (src, dst) in enumerate((
            (rho_hbm, stack.at[pl.ds(0, plane)]),
            (pre_hbm, raw),
            (corona_hbm, marks),
            (fld_hbm, stack.at[pl.ds(FZ * plane, 3 * plane)]),
            (vel_hbm, stack.at[pl.ds(plane, 3 * plane)]),
        ))
    ]
    for load in loads:
        load.start()

    def when(dz, dy, run):
        if dz == 0 and dy == 0:
            run()
        else:
            pl.when(exists(dz, dy))(run)

    def steps(dz, dy):
        return [dx for dx in (0, -1, 1) if (dz, dy, dx) not in SKIP and (dz, dy, dx) != (0, 0, 0)]

    def place(dz, dy, dx):
        where = {}
        if dz != 0:
            where["gz"] = iz + dz
        if dy != 0:
            where["gy"] = iy + dy
        if dx != 0:
            where["gx"] = left if dx < 0 else right
        return where

    barrier = pltpu.get_barrier_semaphore()
    for dz, dy in ALL:
        if dy >= 0:
            def greet():
                for dx in steps(dz, dy):
                    pl.semaphore_signal(
                        barrier, inc=1, device_id=place(dz, dy, dx), device_id_type=MESH
                    )
            when(dz, dy, greet)

    for load in loads[:3]:
        load.wait()
    for z in range(nz):
        rows = pl.ds(z * ny, ny)
        rho = stack[rows, :]
        start = raw[rows, :]
        p = start
        for _ in range(COOL_STEPS):
            p = p / (1.0 + cool_rate * jnp.sqrt(rho * p))
        mark = jnp.full(p.shape, marks[iz * nz + z], jnp.int32)
        stack[pl.ds(4 * plane + z * ny, ny), :] = jnp.where(mark == 1, p, start)

    for load in loads[3:]:
        load.wait()

    def y_rows(f, y):
        return stack[pl.ds(f * plane + y, nz, stride=ny), :]

    def z_rows(f, z):
        return stack[pl.ds(f * plane + z * ny, ny), :]

    def one_row(f, z, y):
        return stack[pl.ds(f * plane + z * ny + y, 1), :]

    zf, yf = FIELDS * ny, FIELDS * nz
    for f in range(FIELDS):
        for d, at in ((0, 0), (1, ny - 1)):
            sbuf[d, pl.ds(f * nz, nz), :] = y_rows(f, at)
        for d, at in ((2, 0), (3, nz - 1)):
            sbuf[d, pl.ds(f * ny, ny), :] = z_rows(f, at)
        for d in range(4, 8):
            dz, dy = DIRS[d]
            sbuf[d, pl.ds(f, 1), :] = one_row(f, 0 if dz < 0 else nz - 1, 0 if dy < 0 else ny - 1)
    sbuf[0, pl.ds(yf, nz), :] = y_rows(FY, 1)
    sbuf[2, pl.ds(zf, ny), :] = z_rows(FZ, 1)
    sbuf[5, pl.ds(FIELDS, 1), :] = one_row(FZ, 1, ny - 1)
    sbuf[6, pl.ds(FIELDS, 1), :] = one_row(FY, nz - 1, 1)
    size = (yf + nz, yf, zf + ny, zf, 16, 16, 16, 16)

    pl.semaphore_wait(
        barrier,
        2 + sum(
            exists(dz, dy).astype(jnp.int32) * len(steps(dz, dy)) for dz, dy in DIRS if dy <= 0
        ),
    )

    def ready_at(dz, dx):
        return ready.at[3 * (dz + 1) + dx + 1]

    for dz, dy in DIRS:
        if dy < 0:
            def answer():
                for dx in steps(dz, dy):
                    pl.semaphore_signal(
                        ready_at(dz, dx), inc=1, device_id=place(dz, dy, dx), device_id_type=MESH
                    )
            when(dz, dy, answer)

    def message(dz, dy, dx):
        d = ALL.index((dz, dy))
        if dx == 0:
            rows = pl.ds(0, size[d - 1])
            src, dst = sbuf.at[d - 1, rows], rbuf.at[d - 1, rows]
        elif d == 0:
            rows = pl.ds(0, 9) if dx < 0 else pl.ds(16, 8)
            src, dst = xsend.at[rows], xrecv.at[rows]
        else:
            at = 2 * d + (dx > 0)
            src, dst = esend.at[at, pl.ds(0, 1)], erecv.at[at, pl.ds(0, 1)]
        return pltpu.make_async_remote_copy(
            src_ref=src,
            dst_ref=dst,
            send_sem=send_sem.at[3 * d + dx + 1],
            recv_sem=recv_sem.at[3 * d + dx + 1],
            device_id=place(dz, dy, dx),
            device_id_type=MESH,
        )

    def post(want, sides):
        for dz, dy in ALL:
            if dy == want:
                def go():
                    for dx in steps(dz, dy):
                        if dx in sides:
                            if dy > 0:
                                pl.semaphore_wait(ready_at(-dz, -dx), 1)
                            message(dz, dy, dx).start()
                when(dz, dy, go)

    post(-1, (0,))
    post(0, (0,))

    for f in range(FIELDS):
        for z in range(nz):
            pad[pl.ds(f * 128 + (z + 1) * wide + 1, ny), :] = z_rows(f, z)

    for d in range(4):
        dz, dy = DIRS[d]
        own = DIRS.index((-dz, -dy))
        step = nz if dz == 0 else ny

        @pl.when(jnp.logical_not(exists(-dz, -dy)))
        def _():
            for f in range(FIELDS):
                rbuf[d, pl.ds(f * step, step), :] = sbuf[own, pl.ds(f * step, step), :]
            if dz + dy < 0:
                f = FY if dz == 0 else FZ
                rbuf[d, pl.ds(FIELDS * step, step), :] = sbuf[own, pl.ds(f * step, step), :]

    for f in range(FIELDS):
        ext[pl.ds((FIELDS - 1 - f) * tall + 8, nx), :] = pad[pl.ds(f * 128, 128), :].T
    lane = lax.broadcasted_iota(jnp.int32, (8, 128), 1)
    member = lax.broadcasted_iota(jnp.int32, (8, 128), 0)
    zat = jnp.zeros((8, 128), jnp.int32) - 1
    for j in range(1, nz + 3):
        zat = zat + (lane >= j * wide).astype(jnp.int32)
    yat = lane - (zat + 1) * wide - 1
    far = 4 * 128
    low_y, high_y = jnp.where(has_y[-1], 0, -far), jnp.where(has_y[1], ny, far)
    low_z, high_z = jnp.where(has_z[-1], 0, -far), jnp.where(has_z[1], nz, far)

    def turn(values, by):
        return pltpu.roll(values, by % 128, 1)

    def slant(values, by, step):
        by = by % 128
        if by + (FIELDS - 1) * step > 128:
            values, by = turn(values, by), 0
        return pltpu.roll(values, by, 1, stride=step, stride_axis=0)

    def clamped(values):
        n = values.shape[0]
        y, z = yat[:n], zat[:n]
        over = jnp.where(y == ny, turn(values, 1), turn(values, 2))
        out = jnp.where(y < 0, turn(values, -1), jnp.where(y < ny, values, over))
        out = jnp.where(jnp.logical_or(y < low_y, y >= high_y), values, out)
        over = jnp.where(z == nz, turn(out, wide), turn(out, 2 * wide))
        ends = jnp.where(z < 0, turn(out, -wide), jnp.where(z < nz, out, over))
        return jnp.where(jnp.logical_or(z < low_z, z >= high_z), out, ends)

    def folded(values, extra, dz, dy, dx):
        y0, z0 = (0 if dy < 0 else ny - 1), (0 if dz < 0 else nz - 1)
        if dz == 0:
            from_, step, slot, next_ = y0 + 1, 1, yat + 1, FY
        elif dy == 0:
            from_, step, slot, next_ = (z0 + 1) * wide, wide, zat + 1, FZ
        else:
            from_, step, slot, next_ = (z0 + 1) * wide + y0 + 1, 1, lane, None
        picked = jnp.where(slot == member + 1, slant(values, step - from_, step), 0.0)
        row = jnp.sum(picked, axis=0, keepdims=True)
        if dx < 0:
            return jnp.where(slot[:1] == 0, turn(extra, -from_), row)
        if dz + dy < 0 and dz * dy == 0:
            second = values[FIELDS - 1 - next_:FIELDS - next_]
            return jnp.where(slot[:1] == 0, turn(second, -from_ - step), row)
        return row

    def unfolded(dz, dy, dx):
        row = erecv[2 * ALL.index((-dz, -dy)) + (dx < 0), pl.ds(0, 1), :]
        yt, zt = (-1 if dy < 0 else ny), (-1 if dz < 0 else nz)
        if dz == 0:
            to, step = yt + 1, 1
        elif dy == 0:
            to, step = (zt + 1) * wide, wide
        else:
            to, step = (zt + 1) * wide + yt + 1, 1
        out = slant(jnp.broadcast_to(row, (FIELDS, 128)), to - FIELDS * step, step)
        if dx < 0 and (dz, dy) in ((0, 1), (1, 0)):
            f, second = (FY, yat > ny) if dz == 0 else (FZ, zat > nz)
            chosen = jnp.logical_and(second, member == f)
            out = jnp.where(chosen, turn(row, to + step), out)
        return out, turn(row, to)

    to_left = clamped(ext[pl.ds(8, FIELDS, stride=tall), :])
    to_right = clamped(ext[pl.ds(7 + nx, FIELDS, stride=tall), :])
    extra = clamped(ext[pl.ds((FIELDS - 1 - FX) * tall + 9, 1), :])
    for f in range(FIELDS):
        r = FIELDS - 1 - f
        xsend[pl.ds(f, 1), :] = to_left[r:r + 1]
        xsend[pl.ds(16 + f, 1), :] = to_right[r:r + 1]
    xsend[pl.ds(FIELDS, 1), :] = extra
    for dz, dy in DIRS:
        at = 2 * ALL.index((dz, dy))
        esend[at, pl.ds(0, 1), :] = folded(to_left, extra, dz, dy, -1)
        esend[at + 1, pl.ds(0, 1), :] = folded(to_right, extra, dz, dy, 1)

    post(-1, (-1, 1))
    post(0, (-1, 1))
    def aside(values, by):
        return pltpu.roll(values, by % nx, 1)

    def tiers(values, by):
        return pltpu.roll(values, by % ny, 0)

    def keep(axis, start, count, stride, found):
        for m, value in found.items():
            flux[7 * axis + m, pl.ds(start, count, stride=stride), :] = value

    def start_of(z, y):
        return (z + 1) * wide + y + 1

    past = None
    for z in range(nz):
        rho, vel, pre = z_rows(0, z), [z_rows(1 + c, z) for c in range(3)], z_rows(4, z)
        faces = [z_rows(5 + c, z) for c in range(3)]
        cell = cell_terms(rho, vel, pre)
        centre = [
            0.5 * (faces[0] + z_rows(FZ, z + 1)) if z < nz - 1 else None,
            0.5 * (faces[1] + tiers(faces[1], -1)),
            0.5 * (faces[2] + aside(faces[2], -1)),
        ]
        if z > 0:
            lower = state_terms(past[0], past[1], past[2], [faces[0]] + past[3][1:], 0)
            upper = state_terms(cell, vel, pre, [faces[0]] + centre[1:], 0)
            keep(0, start_of(z, 0), ny, 1, hll(lower, upper, 0))
        if z < nz - 1:
            for axis, below in ((1, lambda v: tiers(v, 1)), (2, lambda v: aside(v, 1))):
                lrho, lvel = below(rho), [below(v) for v in vel]
                lcell = (
                    lrho, below(cell[1]), below(cell[2]), below(cell[3]),
                    [lrho * v for v in lvel],
                )
                lmag = [faces[c] if c == axis else below(centre[c]) for c in range(3)]
                umag = [faces[c] if c == axis else centre[c] for c in range(3)]
                lower = state_terms(lcell, lvel, below(pre), lmag, axis)
                upper = state_terms(cell, vel, pre, umag, axis)
                keep(axis, start_of(z, 0), ny, 1, hll(lower, upper, axis))
        past = (cell, vel, pre, centre)

    post(1, (0,))
    post(1, (-1, 1))

    for d in range(8):
        dz, dy = DIRS[d]

        @pl.when(exists(-dz, -dy))
        def _():
            message(dz, dy, 0).wait_recv()

    for f in range(FIELDS):
        base = f * 128
        pad[pl.ds(base + wide, nz, stride=wide), :] = rbuf[1, pl.ds(f * nz, nz), :]
        pad[pl.ds(base + wide + ny + 1, nz, stride=wide), :] = rbuf[0, pl.ds(f * nz, nz), :]
        pad[pl.ds(base + 1, ny), :] = rbuf[3, pl.ds(f * ny, ny), :]
        pad[pl.ds(base + (nz + 1) * wide + 1, ny), :] = rbuf[2, pl.ds(f * ny, ny), :]
    pad[pl.ds(FY * 128 + wide + ny + 2, nz, stride=wide), :] = rbuf[0, pl.ds(yf, nz), :]
    pad[pl.ds(FZ * 128 + (nz + 2) * wide + 1, ny), :] = rbuf[2, pl.ds(zf, ny), :]

    def spot(z, y):
        return (z + 1) * wide + y + 1

    for d in range(4, 8):
        dz, dy = DIRS[d]
        zg, yg = (nz if dz < 0 else -1), (ny if dy < 0 else -1)
        zc, yc = min(max(zg, 0), nz - 1), min(max(yg, 0), ny - 1)
        both = exists(-dz, -dy)
        extra = {5: (FZ, 1, 0), 6: (FY, 0, 1)}.get(d)

        @pl.when(both)
        def _():
            pad[pl.ds(spot(zg, yg), FIELDS, stride=128), :] = rbuf[d, pl.ds(0, FIELDS), :]
            if extra:
                f, ez, ey = extra
                pad[pl.ds(f * 128 + spot(zg + ez, yg + ey), 1), :] = rbuf[d, pl.ds(FIELDS, 1), :]

        def copy_rows(zs, ys):
            pad[pl.ds(spot(zg, yg), FIELDS, stride=128), :] = pad[
                pl.ds(spot(zs, ys), FIELDS, stride=128), :
            ]

        @pl.when(jnp.logical_not(has_z[-dz]))
        def _():
            copy_rows(zc, yg)
            if extra:
                f, ez, ey = extra
                pad[pl.ds(f * 128 + spot(zg + ez, yg + ey), 1), :] = pad[
                    pl.ds(f * 128 + spot(zc, yg + ey), 1), :
                ]

        @pl.when(jnp.logical_and(has_z[-dz], jnp.logical_not(has_y[-dy])))
        def _():
            copy_rows(zg, yc)
            if extra:
                f, ez, ey = extra
                pad[pl.ds(f * 128 + spot(zg + ez, yg + ey), 1), :] = pad[
                    pl.ds(f * 128 + spot(zg + ez, yc), 1), :
                ]

    away = (wide, 1)

    def border(axis, start, count, stride, want):
        def load(f, at):
            return pad[pl.ds(f * 128 + at, count, stride=stride), :]

        def state(at):
            vel = [load(1 + c, at) for c in range(3)]
            pre = load(4, at)
            cell = cell_terms(load(0, at), vel, pre)
            centre = [None] * 3
            for c in range(3):
                if c != axis:
                    face = load(5 + c, at)
                    after = aside(face, -1) if c == 2 else load(5 + c, at + away[c])
                    centre[c] = 0.5 * (face + after)
            return cell, vel, pre, centre

        normal = load(5 + axis, start)
        cell, vel, pre, centre = state(start)
        if axis == 2:
            lvel = [aside(v, 1) for v in vel]
            lrho = aside(cell[0], 1)
            lcell = (
                lrho, aside(cell[1], 1), aside(cell[2], 1), aside(cell[3], 1),
                [lrho * v for v in lvel],
            )
            lpre = aside(pre, 1)
            lcentre = [aside(centre[0], 1), aside(centre[1], 1), None]
        else:
            lcell, lvel, lpre, lcentre = state(start - away[axis])
        lcentre[axis] = centre[axis] = normal
        lower = state_terms(lcell, lvel, lpre, lcentre, axis)
        upper = state_terms(cell, vel, pre, centre, axis)
        keep(axis, start, count, stride, hll(lower, upper, axis, want))

    def across(z):
        return start_of(z, 0), ny, 1

    def along(y):
        return start_of(0, y), nz, wide

    every = range(7)
    border(0, *across(0), every)
    border(0, *across(nz), every)
    border(0, *along(ny - 1), every)
    border(0, start_of(0, -1), nz + 1, wide, (5,))
    border(0, *along(ny), (5,))
    border(1, *along(0), every)
    border(1, *along(ny), every)
    border(1, *across(nz - 1), every)
    border(1, start_of(-1, 0), ny + 1, 1, (5,))
    border(1, *across(nz), (5,))
    border(2, *along(ny - 1), every)
    border(2, *across(nz - 1), every)
    border(2, *along(-1), (6,))
    border(2, *along(ny), (6,))
    border(2, *across(-1), (5,))
    border(2, *across(nz), (5,))

    def got(axis, m, at):
        return flux[7 * axis + m, pl.ds(at, ny), :]

    def ex_at(at):
        return 0.25 * (got(0, 5, at) + got(0, 5, at - 1) - got(1, 5, at) - got(1, 5, at - wide))

    def ey_at(at):
        one = got(0, 6, at)
        return 0.25 * (got(2, 5, at) + got(2, 5, at - wide) - one - aside(one, 1))

    def ez_at(at):
        one = got(1, 6, at)
        return 0.25 * (one + aside(one, 1) - got(2, 6, at) - got(2, 6, at - 1))

    ex_here, ey_here = ex_at(start_of(0, 0)), ey_at(start_of(0, 0))
    for z in range(nz):
        at = start_of(z, 0)
        rho, vel, pre = z_rows(0, z), [z_rows(1 + c, z) for c in range(3)], z_rows(4, z)
        faces = [z_rows(5 + c, z) for c in range(3)]
        above = pad[pl.ds(FZ * 128 + at + wide, ny), :]
        beside = pad[pl.ds(FY * 128 + at + 1, ny), :]
        centre = [
            0.5 * (faces[0] + above), 0.5 * (faces[1] + beside),
            0.5 * (faces[2] + aside(faces[2], -1)),
        ]
        cell = cell_terms(rho, vel, pre)
        squared = centre[0] * centre[0] + centre[1] * centre[1] + centre[2] * centre[2]
        start = [rho] + list(cell[4]) + [cell[3] + 0.5 * squared]
        level = jnp.zeros((ny, nx), jnp.int32) + (2 * (iz * nz + z) + 1 - nz * gz)
        force = -gravity * courant * (level.astype(jnp.float32) * (1.0 / (nz * gz)))
        values = []
        for m in range(5):
            fx, fy, fz = got(2, m, at), got(1, m, at), got(0, m, at)
            change = (
                aside(fx, -1) - fx + got(1, m, at + 1) - fy + got(0, m, at + wide) - fz
            )
            value = start[m] - courant * change
            if m == 1:
                value = value + rho * force
            if m == 4:
                value = value + cell[4][0] * force
            values.append(value)
        ex, ey, ez = ex_here, ey_here, ez_at(at)
        ex_here, ey_here = ex_at(at + wide), ey_at(at + wide)
        values.append(faces[0] - courant * ((aside(ey, -1) - ey) - (ex_at(at + 1) - ex)))
        values.append(faces[1] - courant * ((ex_here - ex) - (aside(ez, -1) - ez)))
        values.append(faces[2] - courant * ((ez_at(at + 1) - ez) - (ey_here - ey)))
        for m in range(FIELDS):
            res[pl.ds(m * plane + z * ny, ny), :] = values[m]

    for f in range(FIELDS):
        ext[pl.ds(f * tall + 8, nx), :] = pad[pl.ds(f * 128, 128), :].T

    for dz, dy in ALL:
        def arrived():
            for dx in steps(-dz, -dy):
                if dx != 0:
                    message(-dz, -dy, dx).wait_recv()
        when(dz, dy, arrived)

    slab = iz * nz - 1
    zglobal = zat[:8] + (slab + 1)
    height = (2 * zglobal + 1 - nz * gz).astype(jnp.float32) * (1.0 / (nz * gz))
    pull = -gravity * courant * height

    def gather(dx):
        out, extra = (0, 8) if dx > 0 else (16, 16)
        out, extra = xrecv[pl.ds(out, FIELDS), :], xrecv[pl.ds(extra, 1), :]
        in_y, in_z = {-1: yat < low_y, 1: yat >= high_y}, {-1: zat < low_z, 1: zat >= high_z}
        for dz, dy in DIRS:
            if (dz, dy, dx) not in SKIP:
                if dz == 0:
                    zone = in_y[dy]
                elif dy == 0:
                    zone = in_z[dz]
                else:
                    zone = jnp.logical_and(in_y[dy], in_z[dz])
                values, more = unfolded(dz, dy, dx)
                out = jnp.where(zone, values, out)
                extra = jnp.where(zone[:1], more, extra)
        return out, extra

    members, extra = gather(1)
    ext[pl.ds(8 + nx, FIELDS, stride=tall), :] = members
    ext[pl.ds(FX * tall + 9 + nx, 1), :] = extra
    ext[pl.ds(7, FIELDS, stride=tall), :] = gather(-1)[0]

    def up(values, axis):
        return pltpu.roll(values, 128 - (wide if axis == 0 else 1), 1)

    def down(values, axis):
        return pltpu.roll(values, wide if axis == 0 else 1, 1)

    def side(x):
        r = 8 + x
        now = [ext[pl.ds(f * tall + r, 8), :] for f in range(FIELDS)]
        below = [ext[pl.ds(f * tall + r - 1, 8), :] for f in range(7)]
        rho, vel, pre, faces = now[0], now[1:4], now[4], now[5:8]
        centre = [
            0.5 * (faces[0] + up(faces[0], 0)),
            0.5 * (faces[1] + up(faces[1], 1)),
            0.5 * (faces[2] + ext[pl.ds(FX * tall + r + 1, 8), :]),
        ]
        cell = cell_terms(rho, vel, pre)
        fluxes = []
        for axis in range(3):
            if axis == 2:
                lrho, lvel, lpre = below[0], below[1:4], below[4]
                lcell = cell_terms(lrho, lvel, lpre)
                lmag = [
                    0.5 * (below[5] + up(below[5], 0)),
                    0.5 * (below[6] + up(below[6], 1)),
                    faces[2],
                ]
            else:
                lrho, lpre = down(rho, axis), down(pre, axis)
                lvel = [down(v, axis) for v in vel]
                lcell = (
                    lrho, down(cell[1], axis), down(cell[2], axis), down(cell[3], axis),
                    [lrho * v for v in lvel],
                )
                lmag = [faces[c] if c == axis else down(centre[c], axis) for c in range(3)]
            umag = [faces[c] if c == axis else centre[c] for c in range(3)]
            lower = state_terms(lcell, lvel, lpre, lmag, axis)
            upper = state_terms(cell, vel, pre, umag, axis)
            fluxes.append(hll(lower, upper, axis))
        squared = centre[0] * centre[0] + centre[1] * centre[1] + centre[2] * centre[2]
        base = [rho] + list(cell[4]) + [cell[3] + 0.5 * squared]
        fz, fy, fx = fluxes

        def after(values):
            return pltpu.roll(values, 7, 0)

        def before(values):
            return pltpu.roll(values, 1, 0)

        outs = []
        for m in range(5):
            change = up(fz[m], 0) - fz[m] + up(fy[m], 1) - fy[m] + after(fx[m]) - fx[m]
            value = base[m] - courant * change
            if m == 1:
                value = value + rho * pull
            if m == 4:
                value = value + cell[4][0] * pull
            outs.append(value)
        ex = 0.25 * (fz[5] + down(fz[5], 1) - fy[5] - down(fy[5], 0))
        ey = 0.25 * (fx[5] + down(fx[5], 0) - fz[6] - before(fz[6]))
        ez = 0.25 * (fy[6] + before(fy[6]) - fx[6] - down(fx[6], 1))
        outs.append(faces[0] - courant * ((after(ey) - ey) - (up(ex, 1) - ex)))
        outs.append(faces[1] - courant * ((up(ex, 0) - ex) - (after(ez) - ez)))
        outs.append(faces[2] - courant * ((up(ez, 1) - ez) - (up(ey, 0) - ey)))
        return outs

    first, last = side(-1), side(nx - 6)
    for m in range(FIELDS):
        edge[pl.ds(3 * m, 2), :] = last[m][4:6]
        edge[pl.ds(3 * m + 2, 1), :] = first[m][1:2]
    turned[...] = edge[...].T

    for dz, dy in ALL:
        def sent():
            for dx in steps(dz, dy):
                message(dz, dy, dx).wait_send()
        when(dz, dy, sent)


def unload_kernel(sizes, res, turned, cons_ref, face_ref, out, sem):
    nz, ny, nx = sizes
    plane, wide = nz * ny, ny + 3
    column = lax.broadcasted_iota(jnp.int32, (ny, nx), 1)
    ends = jnp.logical_or(column == 0, column >= nx - 2)
    copies = []
    for m in range(FIELDS):
        for z in range(nz):
            rows = pl.ds(m * plane + z * ny, ny)
            ring = turned[pl.ds((z + 1) * wide + 1, ny), :]
            out[rows, :] = jnp.where(
                ends, pltpu.roll(ring, (nx - 2 - 3 * m) % nx, 1), res[rows, :]
            )
        target, base = (cons_ref, m * plane) if m < 5 else (face_ref, (m - 5) * plane)
        copies.append(pltpu.make_async_copy(
            out.at[pl.ds(m * plane, plane)], target.at[pl.ds(base, plane)], sem.at[m]
        ))
        copies[-1].start()
    for copy in copies:
        copy.wait()


def on_device(sizes, density, velocity, pressure, field, corona):
    nz, ny, nx = density.shape
    gz, gy, gx = sizes
    plane = nz * ny
    hbm = pl.BlockSpec(memory_space=pltpu.HBM)
    vmem = pl.BlockSpec(memory_space=pltpu.VMEM)
    f32 = jnp.float32
    rows = FIELDS * max(nz, ny) + max(nz, ny)
    result, ends = pl.pallas_call(
        functools.partial(kernel, (nz, ny, nx, gz, gy, gx)),
        out_shape=(pltpu.VMEM((FIELDS * plane, nx), f32), pltpu.VMEM((128, 128), f32)),
        in_specs=[hbm] * 5,
        out_specs=(vmem, vmem),
        scratch_shapes=[
            pltpu.VMEM((FIELDS * plane, nx), f32),
            pltpu.VMEM((plane, nx), f32),
            pltpu.SMEM(corona.shape, jnp.int32),
            pltpu.VMEM((8, rows, nx), f32),
            pltpu.VMEM((8, rows, nx), f32),
            pltpu.VMEM((FIELDS * 128, nx), f32),
            pltpu.VMEM((FIELDS * (nx + 16), 128), f32),
            pltpu.VMEM((24, 128), f32),
            pltpu.VMEM((24, 128), f32),
            pltpu.VMEM((18, 8, 128), f32),
            pltpu.VMEM((18, 8, 128), f32),
            pltpu.VMEM((21, 128, nx), f32),
            pltpu.VMEM((128, 128), f32),
            pltpu.SemaphoreType.DMA((5,)),
            pltpu.SemaphoreType.DMA((27,)),
            pltpu.SemaphoreType.DMA((27,)),
            pltpu.SemaphoreType.REGULAR((9,)),
        ],
        compiler_params=pltpu.CompilerParams(
            collective_id=0, has_side_effects=True, vmem_limit_bytes=16 << 20
        ),
    )(
        *(
            pltpu.with_memory_space_constraint(x, pltpu.HBM)
            for x in (
                density.reshape(plane, nx),
                velocity.reshape(3 * plane, nx),
                pressure.reshape(plane, nx),
                field.reshape(3 * plane, nx),
                corona,
            )
        )
    )
    conserved, faces = pl.pallas_call(
        functools.partial(unload_kernel, (nz, ny, nx)),
        out_shape=(
            jax.ShapeDtypeStruct((5 * plane, nx), f32),
            jax.ShapeDtypeStruct((3 * plane, nx), f32),
        ),
        in_specs=[vmem, vmem],
        out_specs=(hbm, hbm),
        scratch_shapes=[
            pltpu.VMEM((FIELDS * plane, nx), f32),
            pltpu.SemaphoreType.DMA((FIELDS,)),
        ],
        compiler_params=pltpu.CompilerParams(vmem_limit_bytes=16 << 20),
    )(result, ends)
    return conserved.reshape(5, nz, ny, nx), faces.reshape(3, nz, ny, nx)


def solution(mesh):
    sizes = tuple(mesh.shape[axis] for axis in ("gz", "gy", "gx"))
    return jax.shard_map(
        functools.partial(on_device, sizes),
        mesh=mesh,
        in_specs=(
            P("gz", "gy", "gx"),
            P(None, "gz", "gy", "gx"),
            P("gz", "gy", "gx"),
            P(None, "gz", "gy", "gx"),
            P(),
        ),
        out_specs=(P(None, "gz", "gy", "gx"), P(None, "gz", "gy", "gx")),
        check_vma=False,
    )
```

```python
import functools

import jax
import jax.numpy as jnp
from jax import lax
from jax.experimental import pallas as pl
from jax.experimental.pallas import tpu as pltpu
from jax.sharding import PartitionSpec as P

COOL_STEPS = 8
adiabatic = 5.0 / 3.0
courant = 0.08
cool_rate = 0.03
gravity = 1.0

MESH = pl.DeviceIdType.MESH
DIRS = ((0, -1), (0, 1), (-1, 0), (1, 0), (-1, -1), (-1, 1), (1, -1), (1, 1))
ALL = ((0, 0),) + DIRS
SKIP = ((-1, -1, -1), (1, 1, 1))
FIELDS = 8
FZ, FY, FX = 5, 6, 7
TINY = 1e-36


def root(values):
    return values * lax.rsqrt(values)


def fast_speed(half_sound, half_squared, transverse_sq, half_inverse):
    both = half_squared * (2.0 * half_inverse)
    gap = half_sound - both
    inner = gap * gap + (4.0 * half_sound) * (transverse_sq * half_inverse)
    return root(half_sound + both + root(jnp.maximum(inner, TINY)))


def state_terms(cell, velocity, pressure, magnetic, axis):
    rho, half_inverse, half_sound, hydro, momenta = cell
    one, two = [c for c in range(3) if c != axis]
    normal = magnetic[axis]
    normal_sq = normal * normal
    transverse_sq = magnetic[one] * magnetic[one] + magnetic[two] * magnetic[two]
    half = 0.5 * (transverse_sq + normal_sq)
    energy = hydro + half
    tension = pressure + half - normal_sq
    align = velocity[one] * magnetic[one] + velocity[two] * magnetic[two]
    speed = fast_speed(half_sound, half, transverse_sq, half_inverse)
    va = velocity[axis]
    conserved = [rho] + list(momenta) + [energy]
    work = tension * va - normal * align
    return va, speed, conserved, tension, work, velocity, magnetic


def cell_terms(rho, velocity, pressure):
    half_inverse = 0.5 / rho
    momenta = [rho * v for v in velocity]
    kinetic = momenta[0] * velocity[0] + momenta[1] * velocity[1] + momenta[2] * velocity[2]
    hydro = pressure * (1.0 / (adiabatic - 1.0)) + 0.5 * kinetic
    return rho, half_inverse, adiabatic * pressure * half_inverse, hydro, momenta


def hll(lower, upper, axis, want=range(7)):
    low, high = lower[0] - lower[1], lower[0] + lower[1]
    slow = jnp.minimum(jnp.minimum(low, upper[0] - upper[1]), 0.0)
    fast = jnp.maximum(jnp.maximum(high, upper[0] + upper[1]), 0.0)
    inverse = 1.0 / (fast - slow)
    wl = fast * inverse
    wu = -slow * inverse
    wj = slow * wl
    al = wl * lower[0] - wj
    au = wu * upper[0] + wj
    normal = upper[6][axis]
    bl, bu = wl * normal, wu * normal
    others = [c for c in range(3) if c != axis]

    def carried(one, two):
        return al * one + au * two

    def member(m):
        if m == 0:
            return carried(lower[2][0], upper[2][0])
        if m <= 3:
            c = m - 1
            value = carried(lower[2][m], upper[2][m])
            if c == axis:
                return value + (wl * lower[3] + wu * upper[3])
            return value - (bl * lower[6][c] + bu * upper[6][c])
        if m == 4:
            return carried(lower[2][4], upper[2][4]) + (wl * lower[4] + wu * upper[4])
        c = others[m - 5]
        return carried(lower[6][c], upper[6][c]) - (bl * lower[5][c] + bu * upper[5][c])

    return {m: member(m) for m in want}


def kernel(
    sizes, rho_hbm, vel_hbm, pre_hbm, fld_hbm, corona_hbm, res, turned,
    stack, raw, marks, sbuf, rbuf, pad, ext, flat, xsend, xrecv, esend, erecv, flux, edge, load_sem, send_sem, recv_sem, ready,
):
    nz, ny, nx, gz, gy, gx = sizes
    plane = nz * ny
    wide = ny + 3
    iz, iy, ix = lax.axis_index("gz"), lax.axis_index("gy"), lax.axis_index("gx")
    left = lax.rem(ix + gx - 1, gx)
    right = lax.rem(ix + 1, gx)

    has_z = {-1: iz > 0, 0: None, 1: iz < gz - 1}
    has_y = {-1: iy > 0, 0: None, 1: iy < gy - 1}

    def exists(dz, dy):
        if dz == 0:
            return has_y[dy]
        if dy == 0:
            return has_z[dz]
        return jnp.logical_and(has_z[dz], has_y[dy])

    loads = [
        pltpu.make_async_copy(src, dst, load_sem.at[i])
        for i, (src, dst) in enumerate((
            (rho_hbm, stack.at[pl.ds(0, plane)]),
            (pre_hbm, raw),
            (corona_hbm, marks),
            (fld_hbm, stack.at[pl.ds(FZ * plane, 3 * plane)]),
            (vel_hbm, stack.at[pl.ds(plane, 3 * plane)]),
        ))
    ]
    for load in loads:
        load.start()

    def when(dz, dy, run):
        if dz == 0 and dy == 0:
            run()
        else:
            pl.when(exists(dz, dy))(run)

    def steps(dz, dy):
        return [dx for dx in (0, -1, 1) if (dz, dy, dx) not in SKIP and (dz, dy, dx) != (0, 0, 0)]

    def place(dz, dy, dx):
        where = {}
        if dz != 0:
            where["gz"] = iz + dz
        if dy != 0:
            where["gy"] = iy + dy
        if dx != 0:
            where["gx"] = left if dx < 0 else right
        return where

    barrier = pltpu.get_barrier_semaphore()
    for dz, dy in ALL:
        if dy >= 0:
            def greet():
                for dx in steps(dz, dy):
                    pl.semaphore_signal(
                        barrier, inc=1, device_id=place(dz, dy, dx), device_id_type=MESH
                    )
            when(dz, dy, greet)

    for load in loads[:3]:
        load.wait()
    for z in range(nz):
        rows = pl.ds(z * ny, ny)
        rho = stack[rows, :]
        start = raw[rows, :]
        p = start
        for _ in range(COOL_STEPS):
            p = p / (1.0 + cool_rate * jnp.sqrt(rho * p))
        mark = jnp.full(p.shape, marks[iz * nz + z], jnp.int32)
        stack[pl.ds(4 * plane + z * ny, ny), :] = jnp.where(mark == 1, p, start)

    for load in loads[3:]:
        load.wait()

    def y_rows(f, y):
        return stack[pl.ds(f * plane + y, nz, stride=ny), :]

    def z_rows(f, z):
        return stack[pl.ds(f * plane + z * ny, ny), :]

    def one_row(f, z, y):
        return stack[pl.ds(f * plane + z * ny + y, 1), :]

    zf, yf = FIELDS * ny, FIELDS * nz
    for f in range(FIELDS):
        for d, at in ((0, 0), (1, ny - 1)):
            sbuf[d, pl.ds(f * nz, nz), :] = y_rows(f, at)
        for d, at in ((2, 0), (3, nz - 1)):
            sbuf[d, pl.ds(f * ny, ny), :] = z_rows(f, at)
        for d in range(4, 8):
            dz, dy = DIRS[d]
            sbuf[d, pl.ds(f, 1), :] = one_row(f, 0 if dz < 0 else nz - 1, 0 if dy < 0 else ny - 1)
    sbuf[0, pl.ds(yf, nz), :] = y_rows(FY, 1)
    sbuf[2, pl.ds(zf, ny), :] = z_rows(FZ, 1)
    sbuf[5, pl.ds(FIELDS, 1), :] = one_row(FZ, 1, ny - 1)
    sbuf[6, pl.ds(FIELDS, 1), :] = one_row(FY, nz - 1, 1)
    size = (yf + nz, yf, zf + ny, zf, 16, 16, 16, 16)

    pl.semaphore_wait(
        barrier,
        2 + sum(
            exists(dz, dy).astype(jnp.int32) * len(steps(dz, dy)) for dz, dy in DIRS if dy <= 0
        ),
    )

    def ready_at(dz, dx):
        return ready.at[3 * (dz + 1) + dx + 1]

    for dz, dy in DIRS:
        if dy < 0:
            def answer():
                for dx in steps(dz, dy):
                    pl.semaphore_signal(
                        ready_at(dz, dx), inc=1, device_id=place(dz, dy, dx), device_id_type=MESH
                    )
            when(dz, dy, answer)

    def message(dz, dy, dx):
        d = ALL.index((dz, dy))
        if dx == 0:
            rows = pl.ds(0, size[d - 1])
            src, dst = sbuf.at[d - 1, rows], rbuf.at[d - 1, rows]
        elif d == 0:
            rows = pl.ds(0, 9) if dx < 0 else pl.ds(16, 8)
            src, dst = xsend.at[rows], xrecv.at[rows]
        else:
            at = 2 * d + (dx > 0)
            src, dst = esend.at[at, pl.ds(0, 1)], erecv.at[at, pl.ds(0, 1)]
        return pltpu.make_async_remote_copy(
            src_ref=src,
            dst_ref=dst,
            send_sem=send_sem.at[3 * d + dx + 1],
            recv_sem=recv_sem.at[3 * d + dx + 1],
            device_id=place(dz, dy, dx),
            device_id_type=MESH,
        )

    def post(want, sides):
        for dz, dy in ALL:
            if dy == want:
                def go():
                    for dx in steps(dz, dy):
                        if dx in sides:
                            if dy > 0:
                                pl.semaphore_wait(ready_at(-dz, -dx), 1)
                            message(dz, dy, dx).start()
                when(dz, dy, go)

    post(-1, (0,))
    post(0, (0,))

    for f in range(FIELDS):
        for z in range(nz):
            pad[pl.ds(f * 128 + (z + 1) * wide + 1, ny), :] = z_rows(f, z)

    for d in range(4):
        dz, dy = DIRS[d]
        own = DIRS.index((-dz, -dy))
        step = nz if dz == 0 else ny

        @pl.when(jnp.logical_not(exists(-dz, -dy)))
        def _():
            for f in range(FIELDS):
                rbuf[d, pl.ds(f * step, step), :] = sbuf[own, pl.ds(f * step, step), :]
            if dz + dy < 0:
                f = FY if dz == 0 else FZ
                rbuf[d, pl.ds(FIELDS * step, step), :] = sbuf[own, pl.ds(f * step, step), :]

    lane = lax.broadcasted_iota(jnp.int32, (8, 128), 1)
    member = lax.broadcasted_iota(jnp.int32, (8, 128), 0)

    def ends(place_of):
        for g in range(16):
            found = None
            for f in range(FIELDS):
                at = 8 * place_of(f)
                moved = pltpu.roll(pad[pl.ds(f * 128 + 8 * g, 8), :], (at + 3) % nx, 1)
                if found is None:
                    found = moved
                else:
                    found = jnp.where(jnp.logical_and(lane >= at, lane < at + 8), moved, found)
            edge[pl.ds(8 * g, 8), :] = found
        flat[...] = edge[...].T
        for row, at in enumerate((0, 1, 2, 5, 6, 7)):
            ext[pl.ds(at, FIELDS, stride=8), :] = flat[pl.ds(row, FIELDS, stride=8), :]

    ends(lambda f: FIELDS - 1 - f)
    zat = jnp.zeros((8, 128), jnp.int32) - 1
    for j in range(1, nz + 3):
        zat = zat + (lane >= j * wide).astype(jnp.int32)
    yat = lane - (zat + 1) * wide - 1
    far = 4 * 128
    low_y, high_y = jnp.where(has_y[-1], 0, -far), jnp.where(has_y[1], ny, far)
    low_z, high_z = jnp.where(has_z[-1], 0, -far), jnp.where(has_z[1], nz, far)

    def turn(values, by):
        return pltpu.roll(values, by % 128, 1)

    def slant(values, by, step):
        by = by % 128
        if by + (FIELDS - 1) * step > 128:
            values, by = turn(values, by), 0
        return pltpu.roll(values, by, 1, stride=step, stride_axis=0)

    def clamped(values):
        n = values.shape[0]
        y, z = yat[:n], zat[:n]
        over = jnp.where(y == ny, turn(values, 1), turn(values, 2))
        out = jnp.where(y < 0, turn(values, -1), jnp.where(y < ny, values, over))
        out = jnp.where(jnp.logical_or(y < low_y, y >= high_y), values, out)
        over = jnp.where(z == nz, turn(out, wide), turn(out, 2 * wide))
        ends = jnp.where(z < 0, turn(out, -wide), jnp.where(z < nz, out, over))
        return jnp.where(jnp.logical_or(z < low_z, z >= high_z), out, ends)

    def folded(values, extra, dz, dy, dx):
        y0, z0 = (0 if dy < 0 else ny - 1), (0 if dz < 0 else nz - 1)
        if dz == 0:
            from_, step, slot, next_ = y0 + 1, 1, yat + 1, FY
        elif dy == 0:
            from_, step, slot, next_ = (z0 + 1) * wide, wide, zat + 1, FZ
        else:
            from_, step, slot, next_ = (z0 + 1) * wide + y0 + 1, 1, lane, None
        picked = jnp.where(slot == member + 1, slant(values, step - from_, step), 0.0)
        row = jnp.sum(picked, axis=0, keepdims=True)
        if dx < 0:
            return jnp.where(slot[:1] == 0, turn(extra, -from_), row)
        if dz + dy < 0 and dz * dy == 0:
            second = values[FIELDS - 1 - next_:FIELDS - next_]
            return jnp.where(slot[:1] == 0, turn(second, -from_ - step), row)
        return row

    def unfolded(dz, dy, dx):
        row = erecv[2 * ALL.index((-dz, -dy)) + (dx < 0), pl.ds(0, 1), :]
        yt, zt = (-1 if dy < 0 else ny), (-1 if dz < 0 else nz)
        if dz == 0:
            to, step = yt + 1, 1
        elif dy == 0:
            to, step = (zt + 1) * wide, wide
        else:
            to, step = (zt + 1) * wide + yt + 1, 1
        out = slant(jnp.broadcast_to(row, (FIELDS, 128)), to - FIELDS * step, step)
        if dx < 0 and (dz, dy) in ((0, 1), (1, 0)):
            f, second = (FY, yat > ny) if dz == 0 else (FZ, zat > nz)
            chosen = jnp.logical_and(second, member == f)
            out = jnp.where(chosen, turn(row, to + step), out)
        return out, turn(row, to)

    to_left = clamped(ext[pl.ds(5, FIELDS, stride=8), :])
    to_right = clamped(ext[pl.ds(2, FIELDS, stride=8), :])
    extra = clamped(ext[pl.ds((FIELDS - 1 - FX) * 8 + 6, 1), :])
    for f in range(FIELDS):
        r = FIELDS - 1 - f
        xsend[pl.ds(f, 1), :] = to_left[r:r + 1]
        xsend[pl.ds(16 + f, 1), :] = to_right[r:r + 1]
    xsend[pl.ds(FIELDS, 1), :] = extra
    for dz, dy in DIRS:
        at = 2 * ALL.index((dz, dy))
        esend[at, pl.ds(0, 1), :] = folded(to_left, extra, dz, dy, -1)
        esend[at + 1, pl.ds(0, 1), :] = folded(to_right, extra, dz, dy, 1)

    post(-1, (-1, 1))
    post(0, (-1, 1))
    def aside(values, by):
        return pltpu.roll(values, by % nx, 1)

    def tiers(values, by):
        return pltpu.roll(values, by % ny, 0)

    def keep(axis, start, count, stride, found):
        for m, value in found.items():
            flux[7 * axis + m, pl.ds(start, count, stride=stride), :] = value

    def start_of(z, y):
        return (z + 1) * wide + y + 1

    past = None
    for z in range(nz):
        rho, vel, pre = z_rows(0, z), [z_rows(1 + c, z) for c in range(3)], z_rows(4, z)
        faces = [z_rows(5 + c, z) for c in range(3)]
        cell = cell_terms(rho, vel, pre)
        centre = [
            0.5 * (faces[0] + z_rows(FZ, z + 1)) if z < nz - 1 else None,
            0.5 * (faces[1] + tiers(faces[1], -1)),
            0.5 * (faces[2] + aside(faces[2], -1)),
        ]
        if z > 0:
            lower = state_terms(past[0], past[1], past[2], [faces[0]] + past[3][1:], 0)
            upper = state_terms(cell, vel, pre, [faces[0]] + centre[1:], 0)
            keep(0, start_of(z, 0), ny, 1, hll(lower, upper, 0))
        if z < nz - 1:
            for axis, below in ((1, lambda v: tiers(v, 1)), (2, lambda v: aside(v, 1))):
                lrho, lvel = below(rho), [below(v) for v in vel]
                lcell = (
                    lrho, below(cell[1]), below(cell[2]), below(cell[3]),
                    [lrho * v for v in lvel],
                )
                lmag = [faces[c] if c == axis else below(centre[c]) for c in range(3)]
                umag = [faces[c] if c == axis else centre[c] for c in range(3)]
                lower = state_terms(lcell, lvel, below(pre), lmag, axis)
                upper = state_terms(cell, vel, pre, umag, axis)
                keep(axis, start_of(z, 0), ny, 1, hll(lower, upper, axis))
        past = (cell, vel, pre, centre)

    post(1, (0,))
    post(1, (-1, 1))

    for dz, dy in ALL:
        def sent():
            for dx in steps(dz, dy):
                message(dz, dy, dx).wait_send()
        when(dz, dy, sent)

    for d in range(8):
        dz, dy = DIRS[d]

        @pl.when(exists(-dz, -dy))
        def _():
            message(dz, dy, 0).wait_recv()

    for f in range(FIELDS):
        base = f * 128
        pad[pl.ds(base + wide, nz, stride=wide), :] = rbuf[1, pl.ds(f * nz, nz), :]
        pad[pl.ds(base + wide + ny + 1, nz, stride=wide), :] = rbuf[0, pl.ds(f * nz, nz), :]
        pad[pl.ds(base + 1, ny), :] = rbuf[3, pl.ds(f * ny, ny), :]
        pad[pl.ds(base + (nz + 1) * wide + 1, ny), :] = rbuf[2, pl.ds(f * ny, ny), :]
    pad[pl.ds(FY * 128 + wide + ny + 2, nz, stride=wide), :] = rbuf[0, pl.ds(yf, nz), :]
    pad[pl.ds(FZ * 128 + (nz + 2) * wide + 1, ny), :] = rbuf[2, pl.ds(zf, ny), :]

    def spot(z, y):
        return (z + 1) * wide + y + 1

    for d in range(4, 8):
        dz, dy = DIRS[d]
        zg, yg = (nz if dz < 0 else -1), (ny if dy < 0 else -1)
        zc, yc = min(max(zg, 0), nz - 1), min(max(yg, 0), ny - 1)
        ydir, zdir = DIRS.index((0, dy)), DIRS.index((dz, 0))

        def chosen(corner, along_y, along_z):
            edge_of = jnp.where(has_z[-dz], along_z, along_y)
            return jnp.where(jnp.logical_and(has_z[-dz], has_y[-dy]), corner, edge_of)

        pad[pl.ds(spot(zg, yg), FIELDS, stride=128), :] = chosen(
            rbuf[d, pl.ds(0, FIELDS), :],
            rbuf[ydir, pl.ds(zc, FIELDS, stride=nz), :],
            rbuf[zdir, pl.ds(yc, FIELDS, stride=ny), :],
        )
        if d == 5:
            pad[pl.ds(FZ * 128 + spot(nz + 1, -1), 1), :] = chosen(
                rbuf[d, pl.ds(FIELDS, 1), :],
                rbuf[ydir, pl.ds(FZ * nz + zc, 1), :],
                rbuf[zdir, pl.ds(zf + yc, 1), :],
            )
        if d == 6:
            pad[pl.ds(FY * 128 + spot(-1, ny + 1), 1), :] = chosen(
                rbuf[d, pl.ds(FIELDS, 1), :],
                rbuf[ydir, pl.ds(yf + zc, 1), :],
                rbuf[zdir, pl.ds(FY * ny + yc, 1), :],
            )

    ends(lambda f: f)

    away = (wide, 1)

    def border(axis, start, count, stride, want):
        def load(f, at):
            return pad[pl.ds(f * 128 + at, count, stride=stride), :]

        def state(at):
            vel = [load(1 + c, at) for c in range(3)]
            pre = load(4, at)
            cell = cell_terms(load(0, at), vel, pre)
            centre = [None] * 3
            for c in range(3):
                if c != axis:
                    face = load(5 + c, at)
                    after = aside(face, -1) if c == 2 else load(5 + c, at + away[c])
                    centre[c] = 0.5 * (face + after)
            return cell, vel, pre, centre

        normal = load(5 + axis, start)
        cell, vel, pre, centre = state(start)
        if axis == 2:
            lvel = [aside(v, 1) for v in vel]
            lrho = aside(cell[0], 1)
            lcell = (
                lrho, aside(cell[1], 1), aside(cell[2], 1), aside(cell[3], 1),
                [lrho * v for v in lvel],
            )
            lpre = aside(pre, 1)
            lcentre = [aside(centre[0], 1), aside(centre[1], 1), None]
        else:
            lcell, lvel, lpre, lcentre = state(start - away[axis])
        lcentre[axis] = centre[axis] = normal
        lower = state_terms(lcell, lvel, lpre, lcentre, axis)
        upper = state_terms(cell, vel, pre, centre, axis)
        keep(axis, start, count, stride, hll(lower, upper, axis, want))

    def across(z):
        return start_of(z, 0), ny, 1

    def along(y):
        return start_of(0, y), nz, wide

    every = range(7)
    border(0, *across(0), every)
    border(0, *across(nz), every)
    border(0, *along(ny - 1), every)
    border(0, start_of(0, -1), nz + 1, wide, (5,))
    border(0, *along(ny), (5,))
    border(1, *along(0), every)
    border(1, *along(ny), every)
    border(1, *across(nz - 1), every)
    border(1, start_of(-1, 0), ny + 1, 1, (5,))
    border(1, *across(nz), (5,))
    border(2, *along(ny - 1), every)
    border(2, *across(nz - 1), every)
    border(2, *along(-1), (6,))
    border(2, *along(ny), (6,))
    border(2, *across(-1), (5,))
    border(2, *across(nz), (5,))

    for dz, dy in ALL:
        def arrived():
            for dx in steps(-dz, -dy):
                if dx != 0:
                    message(-dz, -dy, dx).wait_recv()
        when(dz, dy, arrived)

    slab = iz * nz - 1
    zglobal = zat[:8] + (slab + 1)
    height = (2 * zglobal + 1 - nz * gz).astype(jnp.float32) * (1.0 / (nz * gz))
    pull = -gravity * courant * height

    def gather(dx):
        out, extra = (0, 8) if dx > 0 else (16, 16)
        out, extra = xrecv[pl.ds(out, FIELDS), :], xrecv[pl.ds(extra, 1), :]
        in_y, in_z = {-1: yat < low_y, 1: yat >= high_y}, {-1: zat < low_z, 1: zat >= high_z}
        for dz, dy in DIRS:
            if (dz, dy, dx) not in SKIP:
                if dz == 0:
                    zone = in_y[dy]
                elif dy == 0:
                    zone = in_z[dz]
                else:
                    zone = jnp.logical_and(in_y[dy], in_z[dz])
                values, more = unfolded(dz, dy, dx)
                out = jnp.where(zone, values, out)
                extra = jnp.where(zone[:1], more, extra)
        return out, extra

    members, extra = gather(1)
    ext[pl.ds(3, FIELDS, stride=8), :] = members
    ext[pl.ds(4, FIELDS, stride=8), :] = gather(-1)[0]

    def up(values, axis):
        if axis == 2:
            return pltpu.roll(values, 7, 0)
        return pltpu.roll(values, 128 - (wide if axis == 0 else 1), 1)

    def down(values, axis):
        if axis == 2:
            return pltpu.roll(values, 1, 0)
        return pltpu.roll(values, wide if axis == 0 else 1, 1)

    def outer():
        now = [ext[pl.ds(8 * f, 8), :] for f in range(FIELDS)]
        rho, vel, pre, faces = now[0], now[1:4], now[4], now[5:8]
        centre = [
            0.5 * (faces[0] + up(faces[0], 0)),
            0.5 * (faces[1] + up(faces[1], 1)),
            0.5 * (faces[2] + jnp.where(member == 3, extra, up(faces[2], 2))),
        ]
        cell = cell_terms(rho, vel, pre)
        fluxes = []
        for axis in range(3):
            lrho, lvel = down(rho, axis), [down(v, axis) for v in vel]
            lcell = (
                lrho, down(cell[1], axis), down(cell[2], axis), down(cell[3], axis),
                [lrho * v for v in lvel],
            )
            lmag = [faces[c] if c == axis else down(centre[c], axis) for c in range(3)]
            umag = [faces[c] if c == axis else centre[c] for c in range(3)]
            lower = state_terms(lcell, lvel, down(pre, axis), lmag, axis)
            upper = state_terms(cell, vel, pre, umag, axis)
            fluxes.append(hll(lower, upper, axis))
        squared = centre[0] * centre[0] + centre[1] * centre[1] + centre[2] * centre[2]
        base = [rho] + list(cell[4]) + [cell[3] + 0.5 * squared]
        fz, fy, fx = fluxes

        def after(values):
            return up(values, 2)

        def before(values):
            return down(values, 2)

        outs = []
        for m in range(5):
            change = up(fz[m], 0) - fz[m] + up(fy[m], 1) - fy[m] + after(fx[m]) - fx[m]
            value = base[m] - courant * change
            if m == 1:
                value = value + rho * pull
            if m == 4:
                value = value + cell[4][0] * pull
            outs.append(value)
        ex = 0.25 * (fz[5] + down(fz[5], 1) - fy[5] - down(fy[5], 0))
        ey = 0.25 * (fx[5] + down(fx[5], 0) - fz[6] - before(fz[6]))
        ez = 0.25 * (fy[6] + before(fy[6]) - fx[6] - down(fx[6], 1))
        outs.append(faces[0] - courant * ((after(ey) - ey) - (up(ex, 1) - ex)))
        outs.append(faces[1] - courant * ((up(ex, 0) - ex) - (after(ez) - ez)))
        outs.append(faces[2] - courant * ((up(ez, 1) - ez) - (up(ey, 0) - ey)))
        return outs

    for m, value in enumerate(outer()):
        edge[pl.ds(3 * m, 2), :] = value[1:3]
        edge[pl.ds(3 * m + 2, 1), :] = value[5:6]
    turned[...] = edge[...].T

    def got(axis, m, at):
        return flux[7 * axis + m, pl.ds(at, ny), :]

    def ex_at(at):
        return 0.25 * (got(0, 5, at) + got(0, 5, at - 1) - got(1, 5, at) - got(1, 5, at - wide))

    def ey_at(at):
        one = got(0, 6, at)
        return 0.25 * (got(2, 5, at) + got(2, 5, at - wide) - one - aside(one, 1))

    def ez_at(at):
        one = got(1, 6, at)
        return 0.25 * (one + aside(one, 1) - got(2, 6, at) - got(2, 6, at - 1))

    ex_here, ey_here = ex_at(start_of(0, 0)), ey_at(start_of(0, 0))
    for z in range(nz):
        at = start_of(z, 0)
        rho, vel, pre = z_rows(0, z), [z_rows(1 + c, z) for c in range(3)], z_rows(4, z)
        faces = [z_rows(5 + c, z) for c in range(3)]
        above = pad[pl.ds(FZ * 128 + at + wide, ny), :]
        beside = pad[pl.ds(FY * 128 + at + 1, ny), :]
        centre = [
            0.5 * (faces[0] + above), 0.5 * (faces[1] + beside),
            0.5 * (faces[2] + aside(faces[2], -1)),
        ]
        cell = cell_terms(rho, vel, pre)
        squared = centre[0] * centre[0] + centre[1] * centre[1] + centre[2] * centre[2]
        start = [rho] + list(cell[4]) + [cell[3] + 0.5 * squared]
        level = jnp.zeros((ny, nx), jnp.int32) + (2 * (iz * nz + z) + 1 - nz * gz)
        force = -gravity * courant * (level.astype(jnp.float32) * (1.0 / (nz * gz)))
        values = []
        for m in range(5):
            fx, fy, fz = got(2, m, at), got(1, m, at), got(0, m, at)
            change = (
                aside(fx, -1) - fx + got(1, m, at + 1) - fy + got(0, m, at + wide) - fz
            )
            value = start[m] - courant * change
            if m == 1:
                value = value + rho * force
            if m == 4:
                value = value + cell[4][0] * force
            values.append(value)
        ex, ey, ez = ex_here, ey_here, ez_at(at)
        ex_here, ey_here = ex_at(at + wide), ey_at(at + wide)
        values.append(faces[0] - courant * ((aside(ey, -1) - ey) - (ex_at(at + 1) - ex)))
        values.append(faces[1] - courant * ((ex_here - ex) - (aside(ez, -1) - ez)))
        values.append(faces[2] - courant * ((ez_at(at + 1) - ez) - (ey_here - ey)))
        for m in range(FIELDS):
            res[pl.ds(m * plane + z * ny, ny), :] = values[m]


def unload_kernel(sizes, res, turned, cons_ref, face_ref, out, sem):
    nz, ny, nx = sizes
    plane, wide = nz * ny, ny + 3
    column = lax.broadcasted_iota(jnp.int32, (ny, nx), 1)
    ends = jnp.logical_or(column == 0, column >= nx - 2)
    copies = []
    for m in range(FIELDS):
        for z in range(nz):
            rows = pl.ds(m * plane + z * ny, ny)
            ring = turned[pl.ds((z + 1) * wide + 1, ny), :]
            out[rows, :] = jnp.where(
                ends, pltpu.roll(ring, (nx - 2 - 3 * m) % nx, 1), res[rows, :]
            )
        target, base = (cons_ref, m * plane) if m < 5 else (face_ref, (m - 5) * plane)
        copies.append(pltpu.make_async_copy(
            out.at[pl.ds(m * plane, plane)], target.at[pl.ds(base, plane)], sem.at[m]
        ))
        copies[-1].start()
    for copy in copies:
        copy.wait()


def on_device(sizes, density, velocity, pressure, field, corona):
    nz, ny, nx = density.shape
    gz, gy, gx = sizes
    plane = nz * ny
    hbm = pl.BlockSpec(memory_space=pltpu.HBM)
    vmem = pl.BlockSpec(memory_space=pltpu.VMEM)
    f32 = jnp.float32
    rows = FIELDS * max(nz, ny) + max(nz, ny)
    result, ends = pl.pallas_call(
        functools.partial(kernel, (nz, ny, nx, gz, gy, gx)),
        out_shape=(pltpu.VMEM((FIELDS * plane, nx), f32), pltpu.VMEM((128, 128), f32)),
        in_specs=[hbm] * 5,
        out_specs=(vmem, vmem),
        scratch_shapes=[
            pltpu.VMEM((FIELDS * plane, nx), f32),
            pltpu.VMEM((plane, nx), f32),
            pltpu.SMEM(corona.shape, jnp.int32),
            pltpu.VMEM((8, rows, nx), f32),
            pltpu.VMEM((8, rows, nx), f32),
            pltpu.VMEM((FIELDS * 128, nx), f32),
            pltpu.VMEM((FIELDS * 8, 128), f32),
            pltpu.VMEM((128, 128), f32),
            pltpu.VMEM((24, 128), f32),
            pltpu.VMEM((24, 128), f32),
            pltpu.VMEM((18, 8, 128), f32),
            pltpu.VMEM((18, 8, 128), f32),
            pltpu.VMEM((21, 128, nx), f32),
            pltpu.VMEM((128, 128), f32),
            pltpu.SemaphoreType.DMA((5,)),
            pltpu.SemaphoreType.DMA((27,)),
            pltpu.SemaphoreType.DMA((27,)),
            pltpu.SemaphoreType.REGULAR((9,)),
        ],
        compiler_params=pltpu.CompilerParams(
            collective_id=0, has_side_effects=True, vmem_limit_bytes=16 << 20
        ),
    )(
        *(
            pltpu.with_memory_space_constraint(x, pltpu.HBM)
            for x in (
                density.reshape(plane, nx),
                velocity.reshape(3 * plane, nx),
                pressure.reshape(plane, nx),
                field.reshape(3 * plane, nx),
                corona,
            )
        )
    )
    conserved, faces = pl.pallas_call(
        functools.partial(unload_kernel, (nz, ny, nx)),
        out_shape=(
            jax.ShapeDtypeStruct((5 * plane, nx), f32),
            jax.ShapeDtypeStruct((3 * plane, nx), f32),
        ),
        in_specs=[vmem, vmem],
        out_specs=(hbm, hbm),
        scratch_shapes=[
            pltpu.VMEM((FIELDS * plane, nx), f32),
            pltpu.SemaphoreType.DMA((FIELDS,)),
        ],
        compiler_params=pltpu.CompilerParams(vmem_limit_bytes=16 << 20),
    )(result, ends)
    return conserved.reshape(5, nz, ny, nx), faces.reshape(3, nz, ny, nx)


def solution(mesh):
    sizes = tuple(mesh.shape[axis] for axis in ("gz", "gy", "gx"))
    return jax.shard_map(
        functools.partial(on_device, sizes),
        mesh=mesh,
        in_specs=(
            P("gz", "gy", "gx"),
            P(None, "gz", "gy", "gx"),
            P("gz", "gy", "gx"),
            P(None, "gz", "gy", "gx"),
            P(),
        ),
        out_specs=(P(None, "gz", "gy", "gx"), P(None, "gz", "gy", "gx")),
        check_vma=False,
    )
```

```python
import functools

import jax
import jax.numpy as jnp
from jax import lax
from jax.experimental import pallas as pl
from jax.experimental.pallas import tpu as pltpu
from jax.sharding import PartitionSpec as P

COOL_STEPS = 8
adiabatic = 5.0 / 3.0
courant = 0.08
cool_rate = 0.03
gravity = 1.0

MESH = pl.DeviceIdType.MESH
DIRS = ((0, -1), (0, 1), (-1, 0), (1, 0), (-1, -1), (-1, 1), (1, -1), (1, 1))
ALL = ((0, 0),) + DIRS
SKIP = ((-1, -1, -1), (1, 1, 1))
FIELDS = 8
FZ, FY, FX = 5, 6, 7
TINY = 1e-36


def root(values):
    return values * lax.rsqrt(values)


def fast_speed(half_sound, half_squared, transverse_sq, half_inverse):
    both = half_squared * (2.0 * half_inverse)
    gap = half_sound - both
    inner = gap * gap + (4.0 * half_sound) * (transverse_sq * half_inverse)
    return root(half_sound + both + root(jnp.maximum(inner, TINY)))


def state_terms(cell, velocity, pressure, magnetic, axis):
    rho, half_inverse, half_sound, hydro, momenta = cell
    one, two = [c for c in range(3) if c != axis]
    normal = magnetic[axis]
    normal_sq = normal * normal
    transverse_sq = magnetic[one] * magnetic[one] + magnetic[two] * magnetic[two]
    half = 0.5 * (transverse_sq + normal_sq)
    energy = hydro + half
    tension = pressure + half - normal_sq
    align = velocity[one] * magnetic[one] + velocity[two] * magnetic[two]
    speed = fast_speed(half_sound, half, transverse_sq, half_inverse)
    va = velocity[axis]
    conserved = [rho] + list(momenta) + [energy]
    work = tension * va - normal * align
    return va, speed, conserved, tension, work, velocity, magnetic


def cell_terms(rho, velocity, pressure):
    half_inverse = 0.5 / rho
    momenta = [rho * v for v in velocity]
    kinetic = momenta[0] * velocity[0] + momenta[1] * velocity[1] + momenta[2] * velocity[2]
    hydro = pressure * (1.0 / (adiabatic - 1.0)) + 0.5 * kinetic
    return rho, half_inverse, adiabatic * pressure * half_inverse, hydro, momenta


def hll(lower, upper, axis, want=range(7)):
    low, high = lower[0] - lower[1], lower[0] + lower[1]
    slow = jnp.minimum(jnp.minimum(low, upper[0] - upper[1]), 0.0)
    fast = jnp.maximum(jnp.maximum(high, upper[0] + upper[1]), 0.0)
    inverse = 1.0 / (fast - slow)
    wl = fast * inverse
    wu = -slow * inverse
    wj = slow * wl
    al = wl * lower[0] - wj
    au = wu * upper[0] + wj
    normal = upper[6][axis]
    bl, bu = wl * normal, wu * normal
    others = [c for c in range(3) if c != axis]

    def carried(one, two):
        return al * one + au * two

    def member(m):
        if m == 0:
            return carried(lower[2][0], upper[2][0])
        if m <= 3:
            c = m - 1
            value = carried(lower[2][m], upper[2][m])
            if c == axis:
                return value + (wl * lower[3] + wu * upper[3])
            return value - (bl * lower[6][c] + bu * upper[6][c])
        if m == 4:
            return carried(lower[2][4], upper[2][4]) + (wl * lower[4] + wu * upper[4])
        c = others[m - 5]
        return carried(lower[6][c], upper[6][c]) - (bl * lower[5][c] + bu * upper[5][c])

    return {m: member(m) for m in want}


def kernel(
    sizes, rho_hbm, vel_hbm, pre_hbm, fld_hbm, corona_hbm, res, turned,
    stack, raw, marks, sbuf, rbuf, pad, ext, flat, xsend, xrecv, esend, erecv, flux, edge, load_sem, send_sem, recv_sem, ready,
):
    nz, ny, nx, gz, gy, gx = sizes
    plane = nz * ny
    wide = ny + 3
    iz, iy, ix = lax.axis_index("gz"), lax.axis_index("gy"), lax.axis_index("gx")
    left = lax.rem(ix + gx - 1, gx)
    right = lax.rem(ix + 1, gx)

    has_z = {-1: iz > 0, 0: None, 1: iz < gz - 1}
    has_y = {-1: iy > 0, 0: None, 1: iy < gy - 1}

    def exists(dz, dy):
        if dz == 0:
            return has_y[dy]
        if dy == 0:
            return has_z[dz]
        return jnp.logical_and(has_z[dz], has_y[dy])

    loads = [
        pltpu.make_async_copy(src, dst, load_sem.at[i])
        for i, (src, dst) in enumerate((
            (rho_hbm, stack.at[pl.ds(0, plane)]),
            (pre_hbm, raw),
            (corona_hbm, marks),
            (fld_hbm, stack.at[pl.ds(FZ * plane, 3 * plane)]),
            (vel_hbm, stack.at[pl.ds(plane, 3 * plane)]),
        ))
    ]
    for load in loads:
        load.start()

    def when(dz, dy, run):
        if dz == 0 and dy == 0:
            run()
        else:
            pl.when(exists(dz, dy))(run)

    def steps(dz, dy):
        return [dx for dx in (0, -1, 1) if (dz, dy, dx) not in SKIP and (dz, dy, dx) != (0, 0, 0)]

    def place(dz, dy, dx):
        where = {}
        if dz != 0:
            where["gz"] = iz + dz
        if dy != 0:
            where["gy"] = iy + dy
        if dx != 0:
            where["gx"] = left if dx < 0 else right
        return where

    barrier = pltpu.get_barrier_semaphore()
    for dz, dy in ALL:
        if dy >= 0:
            def greet():
                for dx in steps(dz, dy):
                    pl.semaphore_signal(
                        barrier, inc=1, device_id=place(dz, dy, dx), device_id_type=MESH
                    )
            when(dz, dy, greet)

    for load in loads[:3]:
        load.wait()
    for z in range(nz):
        rows = pl.ds(z * ny, ny)
        rho = stack[rows, :]
        start = raw[rows, :]
        p = start
        for _ in range(COOL_STEPS):
            p = p / (1.0 + cool_rate * jnp.sqrt(rho * p))
        mark = jnp.full(p.shape, marks[iz * nz + z], jnp.int32)
        stack[pl.ds(4 * plane + z * ny, ny), :] = jnp.where(mark == 1, p, start)

    for load in loads[3:]:
        load.wait()

    def y_rows(f, y):
        return stack[pl.ds(f * plane + y, nz, stride=ny), :]

    def z_rows(f, z):
        return stack[pl.ds(f * plane + z * ny, ny), :]

    def one_row(f, z, y):
        return stack[pl.ds(f * plane + z * ny + y, 1), :]

    zf, yf = FIELDS * ny, FIELDS * nz
    for f in range(FIELDS):
        for d, at in ((0, 0), (1, ny - 1)):
            sbuf[d, pl.ds(f * nz, nz), :] = y_rows(f, at)
        for d, at in ((2, 0), (3, nz - 1)):
            sbuf[d, pl.ds(f * ny, ny), :] = z_rows(f, at)
        for d in range(4, 8):
            dz, dy = DIRS[d]
            sbuf[d, pl.ds(f, 1), :] = one_row(f, 0 if dz < 0 else nz - 1, 0 if dy < 0 else ny - 1)
    sbuf[0, pl.ds(yf, nz), :] = y_rows(FY, 1)
    sbuf[2, pl.ds(zf, ny), :] = z_rows(FZ, 1)
    sbuf[5, pl.ds(FIELDS, 1), :] = one_row(FZ, 1, ny - 1)
    sbuf[6, pl.ds(FIELDS, 1), :] = one_row(FY, nz - 1, 1)
    size = (yf + nz, yf, zf + ny, zf, 16, 16, 16, 16)

    pl.semaphore_wait(
        barrier,
        2 + sum(
            exists(dz, dy).astype(jnp.int32) * len(steps(dz, dy)) for dz, dy in DIRS if dy <= 0
        ),
    )

    def ready_at(dz, dx):
        return ready.at[3 * (dz + 1) + dx + 1]

    for dz, dy in DIRS:
        if dy < 0:
            def answer():
                for dx in steps(dz, dy):
                    pl.semaphore_signal(
                        ready_at(dz, dx), inc=1, device_id=place(dz, dy, dx), device_id_type=MESH
                    )
            when(dz, dy, answer)

    def message(dz, dy, dx):
        d = ALL.index((dz, dy))
        if dx == 0:
            rows = pl.ds(0, size[d - 1])
            src, dst = sbuf.at[d - 1, rows], rbuf.at[d - 1, rows]
        elif d == 0:
            rows = pl.ds(0, 9) if dx < 0 else pl.ds(16, 8)
            src, dst = xsend.at[rows], xrecv.at[rows]
        else:
            at = 2 * d + (dx > 0)
            src, dst = esend.at[at, pl.ds(0, 1)], erecv.at[at, pl.ds(0, 1)]
        return pltpu.make_async_remote_copy(
            src_ref=src,
            dst_ref=dst,
            send_sem=send_sem.at[3 * d + dx + 1],
            recv_sem=recv_sem.at[3 * d + dx + 1],
            device_id=place(dz, dy, dx),
            device_id_type=MESH,
        )

    def post(want, sides):
        for dz, dy in ALL:
            if dy == want:
                def go():
                    for dx in steps(dz, dy):
                        if dx in sides:
                            if dy > 0:
                                pl.semaphore_wait(ready_at(-dz, -dx), 1)
                            message(dz, dy, dx).start()
                when(dz, dy, go)

    post(-1, (0,))
    lane = lax.broadcasted_iota(jnp.int32, (8, 128), 1)
    member = lax.broadcasted_iota(jnp.int32, (8, 128), 0)

    def end_lanes(parts, place_of):
        found = None
        for f, part in enumerate(parts):
            at = 8 * place_of(f)
            moved = pltpu.roll(part, (at + 3) % nx, 1)
            if found is None:
                found = moved
            else:
                found = jnp.where(jnp.logical_and(lane >= at, lane < at + 8), moved, found)
        return found

    def ends():
        for g in range(16):
            rows = [pad[pl.ds(f * 128 + 8 * g, 8), :] for f in range(FIELDS)]
            edge[pl.ds(8 * g, 8), :] = end_lanes(rows, lambda f: f)
        flat[...] = edge[...].T
        for row, at in enumerate((0, 1, 2, 5, 6, 7)):
            ext[pl.ds(at, FIELDS, stride=8), :] = flat[pl.ds(row, FIELDS, stride=8), :]

    for z in range(nz):
        own = end_lanes([z_rows(f, z) for f in range(FIELDS)], lambda f: FIELDS - 1 - f)
        lines = [z] + ([-1] if z == 0 else []) + ([nz, nz + 1] if z == nz - 1 else [])
        for to in lines:
            at = (to + 1) * wide
            edge[pl.ds(at + 1, ny), :] = own
            edge[pl.ds(at, 1), :] = own[:1]
            for beyond in range(ny + 1, min(wide, 128 - at)):
                edge[pl.ds(at + beyond, 1), :] = own[ny - 1:]
    flat[...] = edge[...].T
    zat = jnp.zeros((8, 128), jnp.int32) - 1
    for j in range(1, nz + 3):
        zat = zat + (lane >= j * wide).astype(jnp.int32)
    yat = lane - (zat + 1) * wide - 1
    far = 4 * 128
    low_y, high_y = jnp.where(has_y[-1], 0, -far), jnp.where(has_y[1], ny, far)
    low_z, high_z = jnp.where(has_z[-1], 0, -far), jnp.where(has_z[1], nz, far)

    def turn(values, by):
        return pltpu.roll(values, by % 128, 1)

    def slant(values, by, step):
        by = by % 128
        if by + (FIELDS - 1) * step > 128:
            values, by = turn(values, by), 0
        return pltpu.roll(values, by, 1, stride=step, stride_axis=0)

    def folded(values, extra, dz, dy, dx):
        y0, z0 = (0 if dy < 0 else ny - 1), (0 if dz < 0 else nz - 1)
        if dz == 0:
            from_, step, slot, next_ = y0 + 1, 1, yat + 1, FY
        elif dy == 0:
            from_, step, slot, next_ = (z0 + 1) * wide, wide, zat + 1, FZ
        else:
            from_, step, slot, next_ = (z0 + 1) * wide + y0 + 1, 1, lane, None
        picked = jnp.where(slot == member + 1, slant(values, step - from_, step), 0.0)
        row = jnp.sum(picked, axis=0, keepdims=True)
        if dx < 0:
            return jnp.where(slot[:1] == 0, turn(extra, -from_), row)
        if dz + dy < 0 and dz * dy == 0:
            second = values[FIELDS - 1 - next_:FIELDS - next_]
            return jnp.where(slot[:1] == 0, turn(second, -from_ - step), row)
        return row

    def unfolded(dz, dy, dx):
        row = erecv[2 * ALL.index((-dz, -dy)) + (dx < 0), pl.ds(0, 1), :]
        yt, zt = (-1 if dy < 0 else ny), (-1 if dz < 0 else nz)
        if dz == 0:
            to, step = yt + 1, 1
        elif dy == 0:
            to, step = (zt + 1) * wide, wide
        else:
            to, step = (zt + 1) * wide + yt + 1, 1
        out = slant(jnp.broadcast_to(row, (FIELDS, 128)), to - FIELDS * step, step)
        if dx < 0 and (dz, dy) in ((0, 1), (1, 0)):
            f, second = (FY, yat > ny) if dz == 0 else (FZ, zat > nz)
            chosen = jnp.logical_and(second, member == f)
            out = jnp.where(chosen, turn(row, to + step), out)
        return out, turn(row, to)

    to_left, to_right = flat[pl.ds(3, FIELDS, stride=8), :], flat[pl.ds(2, FIELDS, stride=8), :]
    extra = flat[pl.ds((FIELDS - 1 - FX) * 8 + 4, 1), :]
    for f in range(FIELDS):
        r = FIELDS - 1 - f
        xsend[pl.ds(f, 1), :] = to_left[r:r + 1]
        xsend[pl.ds(16 + f, 1), :] = to_right[r:r + 1]
    xsend[pl.ds(FIELDS, 1), :] = extra
    for dz, dy in DIRS:
        at = 2 * ALL.index((dz, dy))
        esend[at, pl.ds(0, 1), :] = folded(to_left, extra, dz, dy, -1)
        esend[at + 1, pl.ds(0, 1), :] = folded(to_right, extra, dz, dy, 1)

    post(-1, (-1, 1))
    post(0, (0, -1, 1))
    for f in range(FIELDS):
        for z in range(nz):
            pad[pl.ds(f * 128 + (z + 1) * wide + 1, ny), :] = z_rows(f, z)

    for d in range(4):
        dz, dy = DIRS[d]
        own = DIRS.index((-dz, -dy))
        step = nz if dz == 0 else ny

        @pl.when(jnp.logical_not(exists(-dz, -dy)))
        def _():
            for f in range(FIELDS):
                rbuf[d, pl.ds(f * step, step), :] = sbuf[own, pl.ds(f * step, step), :]
            if dz + dy < 0:
                f = FY if dz == 0 else FZ
                rbuf[d, pl.ds(FIELDS * step, step), :] = sbuf[own, pl.ds(f * step, step), :]

    def aside(values, by):
        return pltpu.roll(values, by % nx, 1)

    def tiers(values, by):
        return pltpu.roll(values, by % ny, 0)

    def keep(axis, start, count, stride, found):
        for m, value in found.items():
            flux[7 * axis + m, pl.ds(start, count, stride=stride), :] = value

    def start_of(z, y):
        return (z + 1) * wide + y + 1

    past = None
    for z in range(nz):
        rho, vel, pre = z_rows(0, z), [z_rows(1 + c, z) for c in range(3)], z_rows(4, z)
        faces = [z_rows(5 + c, z) for c in range(3)]
        cell = cell_terms(rho, vel, pre)
        centre = [
            0.5 * (faces[0] + z_rows(FZ, z + 1)) if z < nz - 1 else None,
            0.5 * (faces[1] + tiers(faces[1], -1)),
            0.5 * (faces[2] + aside(faces[2], -1)),
        ]
        if z > 0:
            lower = state_terms(past[0], past[1], past[2], [faces[0]] + past[3][1:], 0)
            upper = state_terms(cell, vel, pre, [faces[0]] + centre[1:], 0)
            keep(0, start_of(z, 0), ny, 1, hll(lower, upper, 0))
        if z < nz - 1:
            for axis, below in ((1, lambda v: tiers(v, 1)), (2, lambda v: aside(v, 1))):
                lrho, lvel = below(rho), [below(v) for v in vel]
                lcell = (
                    lrho, below(cell[1]), below(cell[2]), below(cell[3]),
                    [lrho * v for v in lvel],
                )
                lmag = [faces[c] if c == axis else below(centre[c]) for c in range(3)]
                umag = [faces[c] if c == axis else centre[c] for c in range(3)]
                lower = state_terms(lcell, lvel, below(pre), lmag, axis)
                upper = state_terms(cell, vel, pre, umag, axis)
                keep(axis, start_of(z, 0), ny, 1, hll(lower, upper, axis))
        past = (cell, vel, pre, centre)

    post(1, (0,))
    post(1, (-1, 1))

    for dz, dy in ALL:
        def sent():
            for dx in steps(dz, dy):
                message(dz, dy, dx).wait_send()
        when(dz, dy, sent)

    for d in range(8):
        dz, dy = DIRS[d]

        @pl.when(exists(-dz, -dy))
        def _():
            message(dz, dy, 0).wait_recv()

    for f in range(FIELDS):
        base = f * 128
        pad[pl.ds(base + wide, nz, stride=wide), :] = rbuf[1, pl.ds(f * nz, nz), :]
        pad[pl.ds(base + wide + ny + 1, nz, stride=wide), :] = rbuf[0, pl.ds(f * nz, nz), :]
        pad[pl.ds(base + 1, ny), :] = rbuf[3, pl.ds(f * ny, ny), :]
        pad[pl.ds(base + (nz + 1) * wide + 1, ny), :] = rbuf[2, pl.ds(f * ny, ny), :]
    pad[pl.ds(FY * 128 + wide + ny + 2, nz, stride=wide), :] = rbuf[0, pl.ds(yf, nz), :]
    pad[pl.ds(FZ * 128 + (nz + 2) * wide + 1, ny), :] = rbuf[2, pl.ds(zf, ny), :]

    def spot(z, y):
        return (z + 1) * wide + y + 1

    for d in range(4, 8):
        dz, dy = DIRS[d]
        zg, yg = (nz if dz < 0 else -1), (ny if dy < 0 else -1)
        zc, yc = min(max(zg, 0), nz - 1), min(max(yg, 0), ny - 1)
        ydir, zdir = DIRS.index((0, dy)), DIRS.index((dz, 0))

        def chosen(corner, along_y, along_z):
            edge_of = jnp.where(has_z[-dz], along_z, along_y)
            return jnp.where(jnp.logical_and(has_z[-dz], has_y[-dy]), corner, edge_of)

        pad[pl.ds(spot(zg, yg), FIELDS, stride=128), :] = chosen(
            rbuf[d, pl.ds(0, FIELDS), :],
            rbuf[ydir, pl.ds(zc, FIELDS, stride=nz), :],
            rbuf[zdir, pl.ds(yc, FIELDS, stride=ny), :],
        )
        if d == 5:
            pad[pl.ds(FZ * 128 + spot(nz + 1, -1), 1), :] = chosen(
                rbuf[d, pl.ds(FIELDS, 1), :],
                rbuf[ydir, pl.ds(FZ * nz + zc, 1), :],
                rbuf[zdir, pl.ds(zf + yc, 1), :],
            )
        if d == 6:
            pad[pl.ds(FY * 128 + spot(-1, ny + 1), 1), :] = chosen(
                rbuf[d, pl.ds(FIELDS, 1), :],
                rbuf[ydir, pl.ds(yf + zc, 1), :],
                rbuf[zdir, pl.ds(FY * ny + yc, 1), :],
            )

    ends()

    away = (wide, 1)

    def border(axis, start, count, stride, want):
        def load(f, at):
            return pad[pl.ds(f * 128 + at, count, stride=stride), :]

        def state(at):
            vel = [load(1 + c, at) for c in range(3)]
            pre = load(4, at)
            cell = cell_terms(load(0, at), vel, pre)
            centre = [None] * 3
            for c in range(3):
                if c != axis:
                    face = load(5 + c, at)
                    after = aside(face, -1) if c == 2 else load(5 + c, at + away[c])
                    centre[c] = 0.5 * (face + after)
            return cell, vel, pre, centre

        normal = load(5 + axis, start)
        cell, vel, pre, centre = state(start)
        if axis == 2:
            lvel = [aside(v, 1) for v in vel]
            lrho = aside(cell[0], 1)
            lcell = (
                lrho, aside(cell[1], 1), aside(cell[2], 1), aside(cell[3], 1),
                [lrho * v for v in lvel],
            )
            lpre = aside(pre, 1)
            lcentre = [aside(centre[0], 1), aside(centre[1], 1), None]
        else:
            lcell, lvel, lpre, lcentre = state(start - away[axis])
        lcentre[axis] = centre[axis] = normal
        lower = state_terms(lcell, lvel, lpre, lcentre, axis)
        upper = state_terms(cell, vel, pre, centre, axis)
        keep(axis, start, count, stride, hll(lower, upper, axis, want))

    def across(z):
        return start_of(z, 0), ny, 1

    def along(y):
        return start_of(0, y), nz, wide

    every = range(7)
    border(0, *across(0), every)
    border(0, *across(nz), every)
    border(0, *along(ny - 1), every)
    border(0, start_of(0, -1), nz + 1, wide, (5,))
    border(0, *along(ny), (5,))
    border(1, *along(0), every)
    border(1, *along(ny), every)
    border(1, *across(nz - 1), every)
    border(1, start_of(-1, 0), ny + 1, 1, (5,))
    border(1, *across(nz), (5,))
    border(2, *along(ny - 1), every)
    border(2, *across(nz - 1), every)
    border(2, *along(-1), (6,))
    border(2, *along(ny), (6,))
    border(2, *across(-1), (5,))
    border(2, *across(nz), (5,))

    for dz, dy in ALL:
        def arrived():
            for dx in steps(-dz, -dy):
                if dx != 0:
                    message(-dz, -dy, dx).wait_recv()
        when(dz, dy, arrived)

    slab = iz * nz - 1
    zglobal = zat[:8] + (slab + 1)
    height = (2 * zglobal + 1 - nz * gz).astype(jnp.float32) * (1.0 / (nz * gz))
    pull = -gravity * courant * height

    def gather(dx):
        out, extra = (0, 8) if dx > 0 else (16, 16)
        out, extra = xrecv[pl.ds(out, FIELDS), :], xrecv[pl.ds(extra, 1), :]
        in_y, in_z = {-1: yat < low_y, 1: yat >= high_y}, {-1: zat < low_z, 1: zat >= high_z}
        for dz, dy in DIRS:
            if (dz, dy, dx) not in SKIP:
                if dz == 0:
                    zone = in_y[dy]
                elif dy == 0:
                    zone = in_z[dz]
                else:
                    zone = jnp.logical_and(in_y[dy], in_z[dz])
                values, more = unfolded(dz, dy, dx)
                out = jnp.where(zone, values, out)
                extra = jnp.where(zone[:1], more, extra)
        return out, extra

    members, extra = gather(1)
    ext[pl.ds(3, FIELDS, stride=8), :] = members
    ext[pl.ds(4, FIELDS, stride=8), :] = gather(-1)[0]

    def up(values, axis):
        if axis == 2:
            return pltpu.roll(values, 7, 0)
        return pltpu.roll(values, 128 - (wide if axis == 0 else 1), 1)

    def down(values, axis):
        if axis == 2:
            return pltpu.roll(values, 1, 0)
        return pltpu.roll(values, wide if axis == 0 else 1, 1)

    def outer():
        now = [ext[pl.ds(8 * f, 8), :] for f in range(FIELDS)]
        rho, vel, pre, faces = now[0], now[1:4], now[4], now[5:8]
        centre = [
            0.5 * (faces[0] + up(faces[0], 0)),
            0.5 * (faces[1] + up(faces[1], 1)),
            0.5 * (faces[2] + jnp.where(member == 3, extra, up(faces[2], 2))),
        ]
        cell = cell_terms(rho, vel, pre)
        fluxes = []
        for axis in range(3):
            lrho, lvel = down(rho, axis), [down(v, axis) for v in vel]
            lcell = (
                lrho, down(cell[1], axis), down(cell[2], axis), down(cell[3], axis),
                [lrho * v for v in lvel],
            )
            lmag = [faces[c] if c == axis else down(centre[c], axis) for c in range(3)]
            umag = [faces[c] if c == axis else centre[c] for c in range(3)]
            lower = state_terms(lcell, lvel, down(pre, axis), lmag, axis)
            upper = state_terms(cell, vel, pre, umag, axis)
            fluxes.append(hll(lower, upper, axis))
        squared = centre[0] * centre[0] + centre[1] * centre[1] + centre[2] * centre[2]
        base = [rho] + list(cell[4]) + [cell[3] + 0.5 * squared]
        fz, fy, fx = fluxes

        def after(values):
            return up(values, 2)

        def before(values):
            return down(values, 2)

        outs = []
        for m in range(5):
            change = up(fz[m], 0) - fz[m] + up(fy[m], 1) - fy[m] + after(fx[m]) - fx[m]
            value = base[m] - courant * change
            if m == 1:
                value = value + rho * pull
            if m == 4:
                value = value + cell[4][0] * pull
            outs.append(value)
        ex = 0.25 * (fz[5] + down(fz[5], 1) - fy[5] - down(fy[5], 0))
        ey = 0.25 * (fx[5] + down(fx[5], 0) - fz[6] - before(fz[6]))
        ez = 0.25 * (fy[6] + before(fy[6]) - fx[6] - down(fx[6], 1))
        outs.append(faces[0] - courant * ((after(ey) - ey) - (up(ex, 1) - ex)))
        outs.append(faces[1] - courant * ((up(ex, 0) - ex) - (after(ez) - ez)))
        outs.append(faces[2] - courant * ((up(ez, 1) - ez) - (up(ey, 0) - ey)))
        return outs

    for m, value in enumerate(outer()):
        edge[pl.ds(3 * m, 2), :] = value[1:3]
        edge[pl.ds(3 * m + 2, 1), :] = value[5:6]
    turned[...] = edge[...].T

    def got(axis, m, at):
        return flux[7 * axis + m, pl.ds(at, ny), :]

    def ex_at(at):
        return 0.25 * (got(0, 5, at) + got(0, 5, at - 1) - got(1, 5, at) - got(1, 5, at - wide))

    def ey_at(at):
        one = got(0, 6, at)
        return 0.25 * (got(2, 5, at) + got(2, 5, at - wide) - one - aside(one, 1))

    def ez_at(at):
        one = got(1, 6, at)
        return 0.25 * (one + aside(one, 1) - got(2, 6, at) - got(2, 6, at - 1))

    ex_here, ey_here = ex_at(start_of(0, 0)), ey_at(start_of(0, 0))
    for z in range(nz):
        at = start_of(z, 0)
        rho, vel, pre = z_rows(0, z), [z_rows(1 + c, z) for c in range(3)], z_rows(4, z)
        faces = [z_rows(5 + c, z) for c in range(3)]
        above = pad[pl.ds(FZ * 128 + at + wide, ny), :]
        beside = pad[pl.ds(FY * 128 + at + 1, ny), :]
        centre = [
            0.5 * (faces[0] + above), 0.5 * (faces[1] + beside),
            0.5 * (faces[2] + aside(faces[2], -1)),
        ]
        cell = cell_terms(rho, vel, pre)
        squared = centre[0] * centre[0] + centre[1] * centre[1] + centre[2] * centre[2]
        start = [rho] + list(cell[4]) + [cell[3] + 0.5 * squared]
        level = jnp.zeros((ny, nx), jnp.int32) + (2 * (iz * nz + z) + 1 - nz * gz)
        force = -gravity * courant * (level.astype(jnp.float32) * (1.0 / (nz * gz)))
        values = []
        for m in range(5):
            fx, fy, fz = got(2, m, at), got(1, m, at), got(0, m, at)
            change = (
                aside(fx, -1) - fx + got(1, m, at + 1) - fy + got(0, m, at + wide) - fz
            )
            value = start[m] - courant * change
            if m == 1:
                value = value + rho * force
            if m == 4:
                value = value + cell[4][0] * force
            values.append(value)
        ex, ey, ez = ex_here, ey_here, ez_at(at)
        ex_here, ey_here = ex_at(at + wide), ey_at(at + wide)
        values.append(faces[0] - courant * ((aside(ey, -1) - ey) - (ex_at(at + 1) - ex)))
        values.append(faces[1] - courant * ((ex_here - ex) - (aside(ez, -1) - ez)))
        values.append(faces[2] - courant * ((ez_at(at + 1) - ez) - (ey_here - ey)))
        for m in range(FIELDS):
            res[pl.ds(m * plane + z * ny, ny), :] = values[m]


def unload_kernel(sizes, res, turned, cons_ref, face_ref, out, sem):
    nz, ny, nx = sizes
    plane, wide = nz * ny, ny + 3
    column = lax.broadcasted_iota(jnp.int32, (ny, nx), 1)
    ends = jnp.logical_or(column == 0, column >= nx - 2)
    copies = []
    for m in range(FIELDS):
        for z in range(nz):
            rows = pl.ds(m * plane + z * ny, ny)
            ring = turned[pl.ds((z + 1) * wide + 1, ny), :]
            out[rows, :] = jnp.where(
                ends, pltpu.roll(ring, (nx - 2 - 3 * m) % nx, 1), res[rows, :]
            )
        target, base = (cons_ref, m * plane) if m < 5 else (face_ref, (m - 5) * plane)
        copies.append(pltpu.make_async_copy(
            out.at[pl.ds(m * plane, plane)], target.at[pl.ds(base, plane)], sem.at[m]
        ))
        copies[-1].start()
    for copy in copies:
        copy.wait()


def on_device(sizes, density, velocity, pressure, field, corona):
    nz, ny, nx = density.shape
    gz, gy, gx = sizes
    plane = nz * ny
    hbm = pl.BlockSpec(memory_space=pltpu.HBM)
    vmem = pl.BlockSpec(memory_space=pltpu.VMEM)
    f32 = jnp.float32
    rows = FIELDS * max(nz, ny) + max(nz, ny)
    result, ends = pl.pallas_call(
        functools.partial(kernel, (nz, ny, nx, gz, gy, gx)),
        out_shape=(pltpu.VMEM((FIELDS * plane, nx), f32), pltpu.VMEM((128, 128), f32)),
        in_specs=[hbm] * 5,
        out_specs=(vmem, vmem),
        scratch_shapes=[
            pltpu.VMEM((FIELDS * plane, nx), f32),
            pltpu.VMEM((plane, nx), f32),
            pltpu.SMEM(corona.shape, jnp.int32),
            pltpu.VMEM((8, rows, nx), f32),
            pltpu.VMEM((8, rows, nx), f32),
            pltpu.VMEM((FIELDS * 128, nx), f32),
            pltpu.VMEM((FIELDS * 8, 128), f32),
            pltpu.VMEM((128, 128), f32),
            pltpu.VMEM((24, 128), f32),
            pltpu.VMEM((24, 128), f32),
            pltpu.VMEM((18, 8, 128), f32),
            pltpu.VMEM((18, 8, 128), f32),
            pltpu.VMEM((21, 128, nx), f32),
            pltpu.VMEM((128, 128), f32),
            pltpu.SemaphoreType.DMA((5,)),
            pltpu.SemaphoreType.DMA((27,)),
            pltpu.SemaphoreType.DMA((27,)),
            pltpu.SemaphoreType.REGULAR((9,)),
        ],
        compiler_params=pltpu.CompilerParams(
            collective_id=0, has_side_effects=True, vmem_limit_bytes=16 << 20
        ),
    )(
        *(
            pltpu.with_memory_space_constraint(x, pltpu.HBM)
            for x in (
                density.reshape(plane, nx),
                velocity.reshape(3 * plane, nx),
                pressure.reshape(plane, nx),
                field.reshape(3 * plane, nx),
                corona,
            )
        )
    )
    conserved, faces = pl.pallas_call(
        functools.partial(unload_kernel, (nz, ny, nx)),
        out_shape=(
            jax.ShapeDtypeStruct((5 * plane, nx), f32),
            jax.ShapeDtypeStruct((3 * plane, nx), f32),
        ),
        in_specs=[vmem, vmem],
        out_specs=(hbm, hbm),
        scratch_shapes=[
            pltpu.VMEM((FIELDS * plane, nx), f32),
            pltpu.SemaphoreType.DMA((FIELDS,)),
        ],
        compiler_params=pltpu.CompilerParams(vmem_limit_bytes=16 << 20),
    )(result, ends)
    return conserved.reshape(5, nz, ny, nx), faces.reshape(3, nz, ny, nx)


def solution(mesh):
    sizes = tuple(mesh.shape[axis] for axis in ("gz", "gy", "gx"))
    return jax.shard_map(
        functools.partial(on_device, sizes),
        mesh=mesh,
        in_specs=(
            P("gz", "gy", "gx"),
            P(None, "gz", "gy", "gx"),
            P("gz", "gy", "gx"),
            P(None, "gz", "gy", "gx"),
            P(),
        ),
        out_specs=(P(None, "gz", "gy", "gx"), P(None, "gz", "gy", "gx")),
        check_vma=False,
    )
```

```python
import functools

import jax
import jax.numpy as jnp
from jax import lax
from jax.experimental import pallas as pl
from jax.experimental.pallas import tpu as pltpu
from jax.sharding import PartitionSpec as P

COOL_STEPS = 8
adiabatic = 5.0 / 3.0
courant = 0.08
cool_rate = 0.03
gravity = 1.0

MESH = pl.DeviceIdType.MESH
DIRS = ((0, -1), (0, 1), (-1, 0), (1, 0), (-1, -1), (-1, 1), (1, -1), (1, 1))
ALL = ((0, 0),) + DIRS
SKIP = ((-1, -1, -1), (1, 1, 1))
FIELDS = 8
FZ, FY, FX = 5, 6, 7
TINY = 1e-36


def root(values):
    return values * lax.rsqrt(values)


def fast_speed(half_sound, half_squared, transverse_sq, half_inverse):
    both = half_squared * (2.0 * half_inverse)
    gap = half_sound - both
    inner = gap * gap + (4.0 * half_sound) * (transverse_sq * half_inverse)
    return root(half_sound + both + root(jnp.maximum(inner, TINY)))


def state_terms(cell, velocity, pressure, magnetic, axis):
    rho, half_inverse, half_sound, hydro, momenta = cell
    one, two = [c for c in range(3) if c != axis]
    normal = magnetic[axis]
    normal_sq = normal * normal
    transverse_sq = magnetic[one] * magnetic[one] + magnetic[two] * magnetic[two]
    half = 0.5 * (transverse_sq + normal_sq)
    energy = hydro + half
    tension = pressure + half - normal_sq
    align = velocity[one] * magnetic[one] + velocity[two] * magnetic[two]
    speed = fast_speed(half_sound, half, transverse_sq, half_inverse)
    va = velocity[axis]
    conserved = [rho] + list(momenta) + [energy]
    work = tension * va - normal * align
    return va, speed, conserved, tension, work, velocity, magnetic


def cell_terms(rho, velocity, pressure):
    half_inverse = 0.5 / rho
    momenta = [rho * v for v in velocity]
    kinetic = momenta[0] * velocity[0] + momenta[1] * velocity[1] + momenta[2] * velocity[2]
    hydro = pressure * (1.0 / (adiabatic - 1.0)) + 0.5 * kinetic
    return rho, half_inverse, adiabatic * pressure * half_inverse, hydro, momenta


def hll(lower, upper, axis, want=range(7)):
    low, high = lower[0] - lower[1], lower[0] + lower[1]
    slow = jnp.minimum(jnp.minimum(low, upper[0] - upper[1]), 0.0)
    fast = jnp.maximum(jnp.maximum(high, upper[0] + upper[1]), 0.0)
    inverse = 1.0 / (fast - slow)
    wl = fast * inverse
    wu = -slow * inverse
    wj = slow * wl
    al = wl * lower[0] - wj
    au = wu * upper[0] + wj
    normal = upper[6][axis]
    bl, bu = wl * normal, wu * normal
    others = [c for c in range(3) if c != axis]

    def carried(one, two):
        return al * one + au * two

    def member(m):
        if m == 0:
            return carried(lower[2][0], upper[2][0])
        if m <= 3:
            c = m - 1
            value = carried(lower[2][m], upper[2][m])
            if c == axis:
                return value + (wl * lower[3] + wu * upper[3])
            return value - (bl * lower[6][c] + bu * upper[6][c])
        if m == 4:
            return carried(lower[2][4], upper[2][4]) + (wl * lower[4] + wu * upper[4])
        c = others[m - 5]
        return carried(lower[6][c], upper[6][c]) - (bl * lower[5][c] + bu * upper[5][c])

    return {m: member(m) for m in want}


def kernel(
    sizes, rho_hbm, vel_hbm, pre_hbm, fld_hbm, corona_hbm, res, turned,
    stack, raw, marks, sbuf, rbuf, pad, ext, flat, xsend, xrecv, esend, erecv, flux, edge, rim, load_sem, send_sem, recv_sem, ready,
):
    nz, ny, nx, gz, gy, gx = sizes
    plane = nz * ny
    wide = ny + 3
    iz, iy, ix = lax.axis_index("gz"), lax.axis_index("gy"), lax.axis_index("gx")
    left = lax.rem(ix + gx - 1, gx)
    right = lax.rem(ix + 1, gx)

    has_z = {-1: iz > 0, 0: None, 1: iz < gz - 1}
    has_y = {-1: iy > 0, 0: None, 1: iy < gy - 1}

    def exists(dz, dy):
        if dz == 0:
            return has_y[dy]
        if dy == 0:
            return has_z[dz]
        return jnp.logical_and(has_z[dz], has_y[dy])

    loads = [
        pltpu.make_async_copy(src, dst, load_sem.at[i])
        for i, (src, dst) in enumerate((
            (rho_hbm, stack.at[pl.ds(0, plane)]),
            (pre_hbm, raw),
            (corona_hbm, marks),
            (fld_hbm, stack.at[pl.ds(FZ * plane, 3 * plane)]),
            (vel_hbm, stack.at[pl.ds(plane, 3 * plane)]),
        ))
    ]
    for load in loads:
        load.start()

    def when(dz, dy, run):
        if dz == 0 and dy == 0:
            run()
        else:
            pl.when(exists(dz, dy))(run)

    def steps(dz, dy):
        return [dx for dx in (0, -1, 1) if (dz, dy, dx) not in SKIP and (dz, dy, dx) != (0, 0, 0)]

    def place(dz, dy, dx):
        where = {}
        if dz != 0:
            where["gz"] = iz + dz
        if dy != 0:
            where["gy"] = iy + dy
        if dx != 0:
            where["gx"] = left if dx < 0 else right
        return where

    barrier = pltpu.get_barrier_semaphore()
    for dz, dy in ALL:
        if dy >= 0:
            def greet():
                for dx in steps(dz, dy):
                    pl.semaphore_signal(
                        barrier, inc=1, device_id=place(dz, dy, dx), device_id_type=MESH
                    )
            when(dz, dy, greet)

    for load in loads[:3]:
        load.wait()
    for z in range(nz):
        rows = pl.ds(z * ny, ny)
        rho = stack[rows, :]
        start = raw[rows, :]
        p = start
        for _ in range(COOL_STEPS):
            p = p / (1.0 + cool_rate * jnp.sqrt(rho * p))
        mark = jnp.full(p.shape, marks[iz * nz + z], jnp.int32)
        stack[pl.ds(4 * plane + z * ny, ny), :] = jnp.where(mark == 1, p, start)

    for load in loads[3:]:
        load.wait()

    def y_rows(f, y):
        return stack[pl.ds(f * plane + y, nz, stride=ny), :]

    def z_rows(f, z):
        return stack[pl.ds(f * plane + z * ny, ny), :]

    def one_row(f, z, y):
        return stack[pl.ds(f * plane + z * ny + y, 1), :]

    zf, yf = FIELDS * ny, FIELDS * nz
    for f in range(FIELDS):
        for d, at in ((0, 0), (1, ny - 1)):
            sbuf[d, pl.ds(f * nz, nz), :] = y_rows(f, at)
        for d, at in ((2, 0), (3, nz - 1)):
            sbuf[d, pl.ds(f * ny, ny), :] = z_rows(f, at)
        for d in range(4, 8):
            dz, dy = DIRS[d]
            sbuf[d, pl.ds(f, 1), :] = one_row(f, 0 if dz < 0 else nz - 1, 0 if dy < 0 else ny - 1)
    sbuf[0, pl.ds(yf, nz), :] = y_rows(FY, 1)
    sbuf[2, pl.ds(zf, ny), :] = z_rows(FZ, 1)
    sbuf[5, pl.ds(FIELDS, 1), :] = one_row(FZ, 1, ny - 1)
    sbuf[6, pl.ds(FIELDS, 1), :] = one_row(FY, nz - 1, 1)
    size = (yf + nz, yf, zf + ny, zf, 16, 16, 16, 16)

    pl.semaphore_wait(
        barrier,
        2 + sum(
            exists(dz, dy).astype(jnp.int32) * len(steps(dz, dy)) for dz, dy in DIRS if dy <= 0
        ),
    )

    def ready_at(dz, dx):
        return ready.at[3 * (dz + 1) + dx + 1]

    for dz, dy in DIRS:
        if dy < 0:
            def answer():
                for dx in steps(dz, dy):
                    pl.semaphore_signal(
                        ready_at(dz, dx), inc=1, device_id=place(dz, dy, dx), device_id_type=MESH
                    )
            when(dz, dy, answer)

    def message(dz, dy, dx):
        d = ALL.index((dz, dy))
        if dx == 0:
            rows = pl.ds(0, size[d - 1])
            src, dst = sbuf.at[d - 1, rows], rbuf.at[d - 1, rows]
        elif d == 0:
            rows = pl.ds(0, 9) if dx < 0 else pl.ds(16, 8)
            src, dst = xsend.at[rows], xrecv.at[rows]
        else:
            at = 2 * d + (dx > 0)
            src, dst = esend.at[at, pl.ds(0, 1)], erecv.at[at, pl.ds(0, 1)]
        return pltpu.make_async_remote_copy(
            src_ref=src,
            dst_ref=dst,
            send_sem=send_sem.at[3 * d + dx + 1],
            recv_sem=recv_sem.at[3 * d + dx + 1],
            device_id=place(dz, dy, dx),
            device_id_type=MESH,
        )

    def post(want, sides):
        for dz, dy in ALL:
            if dy == want:
                def go():
                    for dx in steps(dz, dy):
                        if dx in sides:
                            if dy > 0:
                                pl.semaphore_wait(ready_at(-dz, -dx), 1)
                            message(dz, dy, dx).start()
                when(dz, dy, go)

    post(-1, (0,))
    lane = lax.broadcasted_iota(jnp.int32, (8, 128), 1)
    member = lax.broadcasted_iota(jnp.int32, (8, 128), 0)

    def end_lanes(parts, place_of):
        found = None
        for f, part in enumerate(parts):
            at = 8 * place_of(f)
            moved = pltpu.roll(part, (at + 3) % nx, 1)
            if found is None:
                found = moved
            else:
                found = jnp.where(jnp.logical_and(lane >= at, lane < at + 8), moved, found)
        return found

    for z in range(nz):
        own = end_lanes([z_rows(f, z) for f in range(FIELDS)], lambda f: FIELDS - 1 - f)
        lines = [z] + ([-1] if z == 0 else []) + ([nz, nz + 1] if z == nz - 1 else [])
        for to in lines:
            at = (to + 1) * wide
            edge[pl.ds(at + 1, ny), :] = own
            edge[pl.ds(at, 1), :] = own[:1]
            for beyond in range(ny + 1, min(wide, 128 - at)):
                edge[pl.ds(at + beyond, 1), :] = own[ny - 1:]
    flat[...] = edge[...].T
    zat = jnp.zeros((8, 128), jnp.int32) - 1
    for j in range(1, nz + 3):
        zat = zat + (lane >= j * wide).astype(jnp.int32)
    yat = lane - (zat + 1) * wide - 1
    far = 4 * 128
    low_y, high_y = jnp.where(has_y[-1], 0, -far), jnp.where(has_y[1], ny, far)
    low_z, high_z = jnp.where(has_z[-1], 0, -far), jnp.where(has_z[1], nz, far)

    def turn(values, by):
        return pltpu.roll(values, by % 128, 1)

    def slant(values, by, step):
        by = by % 128
        if by + (FIELDS - 1) * step > 128:
            values, by = turn(values, by), 0
        return pltpu.roll(values, by, 1, stride=step, stride_axis=0)

    def folded(values, extra, dz, dy, dx):
        y0, z0 = (0 if dy < 0 else ny - 1), (0 if dz < 0 else nz - 1)
        if dz == 0:
            from_, step, slot, next_ = y0 + 1, 1, yat + 1, FY
        elif dy == 0:
            from_, step, slot, next_ = (z0 + 1) * wide, wide, zat + 1, FZ
        else:
            from_, step, slot, next_ = (z0 + 1) * wide + y0 + 1, 1, lane, None
        picked = jnp.where(slot == member + 1, slant(values, step - from_, step), 0.0)
        row = jnp.sum(picked, axis=0, keepdims=True)
        if dx < 0:
            return jnp.where(slot[:1] == 0, turn(extra, -from_), row)
        if dz + dy < 0 and dz * dy == 0:
            second = values[FIELDS - 1 - next_:FIELDS - next_]
            return jnp.where(slot[:1] == 0, turn(second, -from_ - step), row)
        return row

    def unfolded(dz, dy, dx):
        row = erecv[2 * ALL.index((-dz, -dy)) + (dx < 0), pl.ds(0, 1), :]
        yt, zt = (-1 if dy < 0 else ny), (-1 if dz < 0 else nz)
        if dz == 0:
            to, step = yt + 1, 1
        elif dy == 0:
            to, step = (zt + 1) * wide, wide
        else:
            to, step = (zt + 1) * wide + yt + 1, 1
        out = slant(jnp.broadcast_to(row, (FIELDS, 128)), to - FIELDS * step, step)
        if dx < 0 and (dz, dy) in ((0, 1), (1, 0)):
            f, second = (FY, yat > ny) if dz == 0 else (FZ, zat > nz)
            chosen = jnp.logical_and(second, member == f)
            out = jnp.where(chosen, turn(row, to + step), out)
        return out, turn(row, to)

    to_left, to_right = flat[pl.ds(3, FIELDS, stride=8), :], flat[pl.ds(2, FIELDS, stride=8), :]
    extra = flat[pl.ds((FIELDS - 1 - FX) * 8 + 4, 1), :]
    for f in range(FIELDS):
        r = FIELDS - 1 - f
        xsend[pl.ds(f, 1), :] = to_left[r:r + 1]
        xsend[pl.ds(16 + f, 1), :] = to_right[r:r + 1]
    xsend[pl.ds(FIELDS, 1), :] = extra
    for dz, dy in DIRS:
        at = 2 * ALL.index((dz, dy))
        esend[at, pl.ds(0, 1), :] = folded(to_left, extra, dz, dy, -1)
        esend[at + 1, pl.ds(0, 1), :] = folded(to_right, extra, dz, dy, 1)

    post(-1, (-1, 1))
    post(0, (0, -1, 1))
    for f in range(FIELDS):
        for z in range(nz):
            pad[pl.ds(f * 128 + (z + 1) * wide + 1, ny), :] = z_rows(f, z)

    for d in range(4):
        dz, dy = DIRS[d]
        own = DIRS.index((-dz, -dy))
        step = nz if dz == 0 else ny

        @pl.when(jnp.logical_not(exists(-dz, -dy)))
        def _():
            for f in range(FIELDS):
                rbuf[d, pl.ds(f * step, step), :] = sbuf[own, pl.ds(f * step, step), :]
            if dz + dy < 0:
                f = FY if dz == 0 else FZ
                rbuf[d, pl.ds(FIELDS * step, step), :] = sbuf[own, pl.ds(f * step, step), :]

    for z in range(nz):
        rim[pl.ds((z + 1) * wide + 1, ny), :] = end_lanes(
            [z_rows(f, z) for f in range(FIELDS)], lambda f: f
        )

    def aside(values, by):
        return pltpu.roll(values, by % nx, 1)

    def tiers(values, by):
        return pltpu.roll(values, by % ny, 0)

    def keep(axis, start, count, stride, found):
        for m, value in found.items():
            flux[7 * axis + m, pl.ds(start, count, stride=stride), :] = value

    def start_of(z, y):
        return (z + 1) * wide + y + 1

    past = None
    for z in range(nz):
        rho, vel, pre = z_rows(0, z), [z_rows(1 + c, z) for c in range(3)], z_rows(4, z)
        faces = [z_rows(5 + c, z) for c in range(3)]
        cell = cell_terms(rho, vel, pre)
        centre = [
            0.5 * (faces[0] + z_rows(FZ, z + 1)) if z < nz - 1 else None,
            0.5 * (faces[1] + tiers(faces[1], -1)),
            0.5 * (faces[2] + aside(faces[2], -1)),
        ]
        if z > 0:
            lower = state_terms(past[0], past[1], past[2], [faces[0]] + past[3][1:], 0)
            upper = state_terms(cell, vel, pre, [faces[0]] + centre[1:], 0)
            keep(0, start_of(z, 0), ny, 1, hll(lower, upper, 0))
        if z < nz - 1:
            for axis, below in ((1, lambda v: tiers(v, 1)), (2, lambda v: aside(v, 1))):
                lrho, lvel = below(rho), [below(v) for v in vel]
                lcell = (
                    lrho, below(cell[1]), below(cell[2]), below(cell[3]),
                    [lrho * v for v in lvel],
                )
                lmag = [faces[c] if c == axis else below(centre[c]) for c in range(3)]
                umag = [faces[c] if c == axis else centre[c] for c in range(3)]
                lower = state_terms(lcell, lvel, below(pre), lmag, axis)
                upper = state_terms(cell, vel, pre, umag, axis)
                keep(axis, start_of(z, 0), ny, 1, hll(lower, upper, axis))
        past = (cell, vel, pre, centre)

    post(1, (0,))
    post(1, (-1, 1))

    for dz, dy in ALL:
        def sent():
            for dx in steps(dz, dy):
                message(dz, dy, dx).wait_send()
        when(dz, dy, sent)

    for d in range(8):
        dz, dy = DIRS[d]

        @pl.when(exists(-dz, -dy))
        def _():
            message(dz, dy, 0).wait_recv()

    for f in range(FIELDS):
        base = f * 128
        pad[pl.ds(base + wide, nz, stride=wide), :] = rbuf[1, pl.ds(f * nz, nz), :]
        pad[pl.ds(base + wide + ny + 1, nz, stride=wide), :] = rbuf[0, pl.ds(f * nz, nz), :]
        pad[pl.ds(base + 1, ny), :] = rbuf[3, pl.ds(f * ny, ny), :]
        pad[pl.ds(base + (nz + 1) * wide + 1, ny), :] = rbuf[2, pl.ds(f * ny, ny), :]
    pad[pl.ds(FY * 128 + wide + ny + 2, nz, stride=wide), :] = rbuf[0, pl.ds(yf, nz), :]
    pad[pl.ds(FZ * 128 + (nz + 2) * wide + 1, ny), :] = rbuf[2, pl.ds(zf, ny), :]

    def spot(z, y):
        return (z + 1) * wide + y + 1

    for d in range(4, 8):
        dz, dy = DIRS[d]
        zg, yg = (nz if dz < 0 else -1), (ny if dy < 0 else -1)
        zc, yc = min(max(zg, 0), nz - 1), min(max(yg, 0), ny - 1)
        ydir, zdir = DIRS.index((0, dy)), DIRS.index((dz, 0))

        def chosen(corner, along_y, along_z):
            edge_of = jnp.where(has_z[-dz], along_z, along_y)
            return jnp.where(jnp.logical_and(has_z[-dz], has_y[-dy]), corner, edge_of)

        cells = chosen(
            rbuf[d, pl.ds(0, FIELDS), :],
            rbuf[ydir, pl.ds(zc, FIELDS, stride=nz), :],
            rbuf[zdir, pl.ds(yc, FIELDS, stride=ny), :],
        )
        pad[pl.ds(spot(zg, yg), FIELDS, stride=128), :] = cells
        mine = jnp.logical_and(lane >= 8 * member, lane < 8 * member + 8)
        rim[pl.ds(spot(zg, yg), 1), :] = jnp.sum(
            jnp.where(mine, slant(cells, 3, 8), 0.0), axis=0, keepdims=True
        )
        if d == 5:
            beyond = chosen(
                rbuf[d, pl.ds(FIELDS, 1), :],
                rbuf[ydir, pl.ds(FZ * nz + zc, 1), :],
                rbuf[zdir, pl.ds(zf + yc, 1), :],
            )
            pad[pl.ds(FZ * 128 + spot(nz + 1, -1), 1), :] = beyond
            rim[pl.ds(spot(nz + 1, -1), 1), :] = turn(beyond, 8 * FZ + 3)
        if d == 6:
            beyond = chosen(
                rbuf[d, pl.ds(FIELDS, 1), :],
                rbuf[ydir, pl.ds(yf + zc, 1), :],
                rbuf[zdir, pl.ds(FY * ny + yc, 1), :],
            )
            pad[pl.ds(FY * 128 + spot(-1, ny + 1), 1), :] = beyond
            rim[pl.ds(spot(-1, ny + 1), 1), :] = turn(beyond, 8 * FY + 3)

    for d, step, rows in (
        (1, nz, pl.ds(wide, nz, stride=wide)),
        (0, nz, pl.ds(wide + ny + 1, nz, stride=wide)),
        (3, ny, pl.ds(1, ny)),
        (2, ny, pl.ds((nz + 1) * wide + 1, ny)),
    ):
        rim[rows, :] = end_lanes(
            [rbuf[d, pl.ds(f * step, step), :] for f in range(FIELDS)], lambda f: f
        )
    rim[pl.ds(wide + ny + 2, nz, stride=wide), :] = turn(rbuf[0, pl.ds(yf, nz), :], 8 * FY + 3)
    rim[pl.ds((nz + 2) * wide + 1, ny), :] = turn(rbuf[2, pl.ds(zf, ny), :], 8 * FZ + 3)
    flat[...] = rim[...].T
    for row, at in enumerate((0, 1, 2, 5, 6, 7)):
        ext[pl.ds(at, FIELDS, stride=8), :] = flat[pl.ds(row, FIELDS, stride=8), :]

    away = (wide, 1)

    def border(axis, start, count, stride, want):
        def load(f, at):
            return pad[pl.ds(f * 128 + at, count, stride=stride), :]

        def state(at):
            vel = [load(1 + c, at) for c in range(3)]
            pre = load(4, at)
            cell = cell_terms(load(0, at), vel, pre)
            centre = [None] * 3
            for c in range(3):
                if c != axis:
                    face = load(5 + c, at)
                    after = aside(face, -1) if c == 2 else load(5 + c, at + away[c])
                    centre[c] = 0.5 * (face + after)
            return cell, vel, pre, centre

        normal = load(5 + axis, start)
        cell, vel, pre, centre = state(start)
        if axis == 2:
            lvel = [aside(v, 1) for v in vel]
            lrho = aside(cell[0], 1)
            lcell = (
                lrho, aside(cell[1], 1), aside(cell[2], 1), aside(cell[3], 1),
                [lrho * v for v in lvel],
            )
            lpre = aside(pre, 1)
            lcentre = [aside(centre[0], 1), aside(centre[1], 1), None]
        else:
            lcell, lvel, lpre, lcentre = state(start - away[axis])
        lcentre[axis] = centre[axis] = normal
        lower = state_terms(lcell, lvel, lpre, lcentre, axis)
        upper = state_terms(cell, vel, pre, centre, axis)
        keep(axis, start, count, stride, hll(lower, upper, axis, want))

    def across(z):
        return start_of(z, 0), ny, 1

    def along(y):
        return start_of(0, y), nz, wide

    every = range(7)
    border(0, *across(0), every)
    border(0, *across(nz), every)
    border(0, *along(ny - 1), every)
    border(0, start_of(0, -1), nz + 1, wide, (5,))
    border(0, *along(ny), (5,))
    border(1, *along(0), every)
    border(1, *along(ny), every)
    border(1, *across(nz - 1), every)
    border(1, start_of(-1, 0), ny + 1, 1, (5,))
    border(1, *across(nz), (5,))
    border(2, *along(ny - 1), every)
    border(2, *across(nz - 1), every)
    border(2, *along(-1), (6,))
    border(2, *along(ny), (6,))
    border(2, *across(-1), (5,))
    border(2, *across(nz), (5,))

    for dz, dy in ALL:
        def arrived():
            for dx in steps(-dz, -dy):
                if dx != 0:
                    message(-dz, -dy, dx).wait_recv()
        when(dz, dy, arrived)

    slab = iz * nz - 1
    zglobal = zat[:8] + (slab + 1)
    height = (2 * zglobal + 1 - nz * gz).astype(jnp.float32) * (1.0 / (nz * gz))
    pull = -gravity * courant * height

    def gather(dx):
        out, extra = (0, 8) if dx > 0 else (16, 16)
        out, extra = xrecv[pl.ds(out, FIELDS), :], xrecv[pl.ds(extra, 1), :]
        in_y, in_z = {-1: yat < low_y, 1: yat >= high_y}, {-1: zat < low_z, 1: zat >= high_z}
        for dz, dy in DIRS:
            if (dz, dy, dx) not in SKIP:
                if dz == 0:
                    zone = in_y[dy]
                elif dy == 0:
                    zone = in_z[dz]
                else:
                    zone = jnp.logical_and(in_y[dy], in_z[dz])
                values, more = unfolded(dz, dy, dx)
                out = jnp.where(zone, values, out)
                extra = jnp.where(zone[:1], more, extra)
        return out, extra

    members, extra = gather(1)
    ext[pl.ds(3, FIELDS, stride=8), :] = members
    ext[pl.ds(4, FIELDS, stride=8), :] = gather(-1)[0]

    def up(values, axis):
        if axis == 2:
            return pltpu.roll(values, 7, 0)
        return pltpu.roll(values, 128 - (wide if axis == 0 else 1), 1)

    def down(values, axis):
        if axis == 2:
            return pltpu.roll(values, 1, 0)
        return pltpu.roll(values, wide if axis == 0 else 1, 1)

    def outer():
        now = [ext[pl.ds(8 * f, 8), :] for f in range(FIELDS)]
        rho, vel, pre, faces = now[0], now[1:4], now[4], now[5:8]
        centre = [
            0.5 * (faces[0] + up(faces[0], 0)),
            0.5 * (faces[1] + up(faces[1], 1)),
            0.5 * (faces[2] + jnp.where(member == 3, extra, up(faces[2], 2))),
        ]
        cell = cell_terms(rho, vel, pre)
        fluxes = []
        for axis in range(3):
            lrho, lvel = down(rho, axis), [down(v, axis) for v in vel]
            lcell = (
                lrho, down(cell[1], axis), down(cell[2], axis), down(cell[3], axis),
                [lrho * v for v in lvel],
            )
            lmag = [faces[c] if c == axis else down(centre[c], axis) for c in range(3)]
            umag = [faces[c] if c == axis else centre[c] for c in range(3)]
            lower = state_terms(lcell, lvel, down(pre, axis), lmag, axis)
            upper = state_terms(cell, vel, pre, umag, axis)
            fluxes.append(hll(lower, upper, axis))
        squared = centre[0] * centre[0] + centre[1] * centre[1] + centre[2] * centre[2]
        base = [rho] + list(cell[4]) + [cell[3] + 0.5 * squared]
        fz, fy, fx = fluxes

        def after(values):
            return up(values, 2)

        def before(values):
            return down(values, 2)

        outs = []
        for m in range(5):
            change = up(fz[m], 0) - fz[m] + up(fy[m], 1) - fy[m] + after(fx[m]) - fx[m]
            value = base[m] - courant * change
            if m == 1:
                value = value + rho * pull
            if m == 4:
                value = value + cell[4][0] * pull
            outs.append(value)
        ex = 0.25 * (fz[5] + down(fz[5], 1) - fy[5] - down(fy[5], 0))
        ey = 0.25 * (fx[5] + down(fx[5], 0) - fz[6] - before(fz[6]))
        ez = 0.25 * (fy[6] + before(fy[6]) - fx[6] - down(fx[6], 1))
        outs.append(faces[0] - courant * ((after(ey) - ey) - (up(ex, 1) - ex)))
        outs.append(faces[1] - courant * ((up(ex, 0) - ex) - (after(ez) - ez)))
        outs.append(faces[2] - courant * ((up(ez, 1) - ez) - (up(ey, 0) - ey)))
        return outs

    for m, value in enumerate(outer()):
        edge[pl.ds(3 * m, 2), :] = value[1:3]
        edge[pl.ds(3 * m + 2, 1), :] = value[5:6]
    turned[...] = edge[...].T

    def got(axis, m, at):
        return flux[7 * axis + m, pl.ds(at, ny), :]

    def ex_at(at):
        return 0.25 * (got(0, 5, at) + got(0, 5, at - 1) - got(1, 5, at) - got(1, 5, at - wide))

    def ey_at(at):
        one = got(0, 6, at)
        return 0.25 * (got(2, 5, at) + got(2, 5, at - wide) - one - aside(one, 1))

    def ez_at(at):
        one = got(1, 6, at)
        return 0.25 * (one + aside(one, 1) - got(2, 6, at) - got(2, 6, at - 1))

    ex_here, ey_here = ex_at(start_of(0, 0)), ey_at(start_of(0, 0))
    for z in range(nz):
        at = start_of(z, 0)
        rho, vel, pre = z_rows(0, z), [z_rows(1 + c, z) for c in range(3)], z_rows(4, z)
        faces = [z_rows(5 + c, z) for c in range(3)]
        above = pad[pl.ds(FZ * 128 + at + wide, ny), :]
        beside = pad[pl.ds(FY * 128 + at + 1, ny), :]
        centre = [
            0.5 * (faces[0] + above), 0.5 * (faces[1] + beside),
            0.5 * (faces[2] + aside(faces[2], -1)),
        ]
        cell = cell_terms(rho, vel, pre)
        squared = centre[0] * centre[0] + centre[1] * centre[1] + centre[2] * centre[2]
        start = [rho] + list(cell[4]) + [cell[3] + 0.5 * squared]
        level = jnp.zeros((ny, nx), jnp.int32) + (2 * (iz * nz + z) + 1 - nz * gz)
        force = -gravity * courant * (level.astype(jnp.float32) * (1.0 / (nz * gz)))
        values = []
        for m in range(5):
            fx, fy, fz = got(2, m, at), got(1, m, at), got(0, m, at)
            change = (
                aside(fx, -1) - fx + got(1, m, at + 1) - fy + got(0, m, at + wide) - fz
            )
            value = start[m] - courant * change
            if m == 1:
                value = value + rho * force
            if m == 4:
                value = value + cell[4][0] * force
            values.append(value)
        ex, ey, ez = ex_here, ey_here, ez_at(at)
        ex_here, ey_here = ex_at(at + wide), ey_at(at + wide)
        values.append(faces[0] - courant * ((aside(ey, -1) - ey) - (ex_at(at + 1) - ex)))
        values.append(faces[1] - courant * ((ex_here - ex) - (aside(ez, -1) - ez)))
        values.append(faces[2] - courant * ((ez_at(at + 1) - ez) - (ey_here - ey)))
        for m in range(FIELDS):
            res[pl.ds(m * plane + z * ny, ny), :] = values[m]


def unload_kernel(sizes, res, turned, cons_ref, face_ref, out, sem):
    nz, ny, nx = sizes
    plane, wide = nz * ny, ny + 3
    column = lax.broadcasted_iota(jnp.int32, (ny, nx), 1)
    ends = jnp.logical_or(column == 0, column >= nx - 2)
    copies = []
    for m in range(FIELDS):
        for z in range(nz):
            rows = pl.ds(m * plane + z * ny, ny)
            ring = turned[pl.ds((z + 1) * wide + 1, ny), :]
            out[rows, :] = jnp.where(
                ends, pltpu.roll(ring, (nx - 2 - 3 * m) % nx, 1), res[rows, :]
            )
        target, base = (cons_ref, m * plane) if m < 5 else (face_ref, (m - 5) * plane)
        copies.append(pltpu.make_async_copy(
            out.at[pl.ds(m * plane, plane)], target.at[pl.ds(base, plane)], sem.at[m]
        ))
        copies[-1].start()
    for copy in copies:
        copy.wait()


def on_device(sizes, density, velocity, pressure, field, corona):
    nz, ny, nx = density.shape
    gz, gy, gx = sizes
    plane = nz * ny
    hbm = pl.BlockSpec(memory_space=pltpu.HBM)
    vmem = pl.BlockSpec(memory_space=pltpu.VMEM)
    f32 = jnp.float32
    rows = FIELDS * max(nz, ny) + max(nz, ny)
    result, ends = pl.pallas_call(
        functools.partial(kernel, (nz, ny, nx, gz, gy, gx)),
        out_shape=(pltpu.VMEM((FIELDS * plane, nx), f32), pltpu.VMEM((128, 128), f32)),
        in_specs=[hbm] * 5,
        out_specs=(vmem, vmem),
        scratch_shapes=[
            pltpu.VMEM((FIELDS * plane, nx), f32),
            pltpu.VMEM((plane, nx), f32),
            pltpu.SMEM(corona.shape, jnp.int32),
            pltpu.VMEM((8, rows, nx), f32),
            pltpu.VMEM((8, rows, nx), f32),
            pltpu.VMEM((FIELDS * 128, nx), f32),
            pltpu.VMEM((FIELDS * 8, 128), f32),
            pltpu.VMEM((128, 128), f32),
            pltpu.VMEM((24, 128), f32),
            pltpu.VMEM((24, 128), f32),
            pltpu.VMEM((18, 8, 128), f32),
            pltpu.VMEM((18, 8, 128), f32),
            pltpu.VMEM((21, 128, nx), f32),
            pltpu.VMEM((128, 128), f32),
            pltpu.VMEM((128, 128), f32),
            pltpu.SemaphoreType.DMA((5,)),
            pltpu.SemaphoreType.DMA((27,)),
            pltpu.SemaphoreType.DMA((27,)),
            pltpu.SemaphoreType.REGULAR((9,)),
        ],
        compiler_params=pltpu.CompilerParams(
            collective_id=0, has_side_effects=True, vmem_limit_bytes=16 << 20
        ),
    )(
        *(
            pltpu.with_memory_space_constraint(x, pltpu.HBM)
            for x in (
                density.reshape(plane, nx),
                velocity.reshape(3 * plane, nx),
                pressure.reshape(plane, nx),
                field.reshape(3 * plane, nx),
                corona,
            )
        )
    )
    conserved, faces = pl.pallas_call(
        functools.partial(unload_kernel, (nz, ny, nx)),
        out_shape=(
            jax.ShapeDtypeStruct((5 * plane, nx), f32),
            jax.ShapeDtypeStruct((3 * plane, nx), f32),
        ),
        in_specs=[vmem, vmem],
        out_specs=(hbm, hbm),
        scratch_shapes=[
            pltpu.VMEM((FIELDS * plane, nx), f32),
            pltpu.SemaphoreType.DMA((FIELDS,)),
        ],
        compiler_params=pltpu.CompilerParams(vmem_limit_bytes=16 << 20),
    )(result, ends)
    return conserved.reshape(5, nz, ny, nx), faces.reshape(3, nz, ny, nx)


def solution(mesh):
    sizes = tuple(mesh.shape[axis] for axis in ("gz", "gy", "gx"))
    return jax.shard_map(
        functools.partial(on_device, sizes),
        mesh=mesh,
        in_specs=(
            P("gz", "gy", "gx"),
            P(None, "gz", "gy", "gx"),
            P("gz", "gy", "gx"),
            P(None, "gz", "gy", "gx"),
            P(),
        ),
        out_specs=(P(None, "gz", "gy", "gx"), P(None, "gz", "gy", "gx")),
        check_vma=False,
    )
```

```python
import functools

import jax
import jax.numpy as jnp
from jax import lax
from jax.experimental import pallas as pl
from jax.experimental.pallas import tpu as pltpu
from jax.sharding import PartitionSpec as P

COOL_STEPS = 8
adiabatic = 5.0 / 3.0
courant = 0.08
cool_rate = 0.03
gravity = 1.0

MESH = pl.DeviceIdType.MESH
DIRS = ((0, -1), (0, 1), (-1, 0), (1, 0), (-1, -1), (-1, 1), (1, -1), (1, 1))
ALL = ((0, 0),) + DIRS
SKIP = ((-1, -1, -1), (1, 1, 1))
FIELDS = 8
FZ, FY, FX = 5, 6, 7
TINY = 1e-36


def root(values):
    return values * lax.rsqrt(values)


def fast_speed(half_sound, half_squared, transverse_sq, half_inverse):
    both = half_squared * (2.0 * half_inverse)
    gap = half_sound - both
    inner = gap * gap + (4.0 * half_sound) * (transverse_sq * half_inverse)
    return root(half_sound + both + root(jnp.maximum(inner, TINY)))


def state_terms(cell, velocity, pressure, magnetic, axis):
    rho, half_inverse, half_sound, hydro, momenta = cell
    one, two = [c for c in range(3) if c != axis]
    normal = magnetic[axis]
    normal_sq = normal * normal
    transverse_sq = magnetic[one] * magnetic[one] + magnetic[two] * magnetic[two]
    half = 0.5 * (transverse_sq + normal_sq)
    energy = hydro + half
    tension = pressure + half - normal_sq
    align = velocity[one] * magnetic[one] + velocity[two] * magnetic[two]
    speed = fast_speed(half_sound, half, transverse_sq, half_inverse)
    va = velocity[axis]
    conserved = [rho] + list(momenta) + [energy]
    work = tension * va - normal * align
    return va, speed, conserved, tension, work, velocity, magnetic


def cell_terms(rho, velocity, pressure):
    half_inverse = 0.5 / rho
    momenta = [rho * v for v in velocity]
    kinetic = momenta[0] * velocity[0] + momenta[1] * velocity[1] + momenta[2] * velocity[2]
    hydro = pressure * (1.0 / (adiabatic - 1.0)) + 0.5 * kinetic
    return rho, half_inverse, adiabatic * pressure * half_inverse, hydro, momenta


def hll(lower, upper, axis, want=range(7)):
    low, high = lower[0] - lower[1], lower[0] + lower[1]
    slow = jnp.minimum(jnp.minimum(low, upper[0] - upper[1]), 0.0)
    fast = jnp.maximum(jnp.maximum(high, upper[0] + upper[1]), 0.0)
    inverse = 1.0 / (fast - slow)
    wl = fast * inverse
    wu = -slow * inverse
    wj = slow * wl
    al = wl * lower[0] - wj
    au = wu * upper[0] + wj
    normal = upper[6][axis]
    bl, bu = wl * normal, wu * normal
    others = [c for c in range(3) if c != axis]

    def carried(one, two):
        return al * one + au * two

    def member(m):
        if m == 0:
            return carried(lower[2][0], upper[2][0])
        if m <= 3:
            c = m - 1
            value = carried(lower[2][m], upper[2][m])
            if c == axis:
                return value + (wl * lower[3] + wu * upper[3])
            return value - (bl * lower[6][c] + bu * upper[6][c])
        if m == 4:
            return carried(lower[2][4], upper[2][4]) + (wl * lower[4] + wu * upper[4])
        c = others[m - 5]
        return carried(lower[6][c], upper[6][c]) - (bl * lower[5][c] + bu * upper[5][c])

    return {m: member(m) for m in want}


def kernel(
    sizes, rho_hbm, vel_hbm, pre_hbm, fld_hbm, corona_hbm, res, turned,
    stack, raw, marks, sbuf, rbuf, pad, ext, flat, xsend, xrecv, esend, erecv, flux, edge, rim, load_sem, send_sem, recv_sem, ready,
):
    nz, ny, nx, gz, gy, gx = sizes
    plane = nz * ny
    wide = ny + 3
    iz, iy, ix = lax.axis_index("gz"), lax.axis_index("gy"), lax.axis_index("gx")
    left = lax.rem(ix + gx - 1, gx)
    right = lax.rem(ix + 1, gx)

    has_z = {-1: iz > 0, 0: None, 1: iz < gz - 1}
    has_y = {-1: iy > 0, 0: None, 1: iy < gy - 1}

    def exists(dz, dy):
        if dz == 0:
            return has_y[dy]
        if dy == 0:
            return has_z[dz]
        return jnp.logical_and(has_z[dz], has_y[dy])

    loads = [
        pltpu.make_async_copy(src, dst, load_sem.at[i])
        for i, (src, dst) in enumerate((
            (rho_hbm, stack.at[pl.ds(0, plane)]),
            (pre_hbm, raw),
            (corona_hbm, marks),
            (fld_hbm, stack.at[pl.ds(FZ * plane, 3 * plane)]),
            (vel_hbm, stack.at[pl.ds(plane, 3 * plane)]),
        ))
    ]
    for load in loads:
        load.start()

    def when(dz, dy, run):
        if dz == 0 and dy == 0:
            run()
        else:
            pl.when(exists(dz, dy))(run)

    def steps(dz, dy):
        return [dx for dx in (0, -1, 1) if (dz, dy, dx) not in SKIP and (dz, dy, dx) != (0, 0, 0)]

    def place(dz, dy, dx):
        where = {}
        if dz != 0:
            where["gz"] = iz + dz
        if dy != 0:
            where["gy"] = iy + dy
        if dx != 0:
            where["gx"] = left if dx < 0 else right
        return where

    barrier = pltpu.get_barrier_semaphore()
    for dz, dy in ALL:
        if dy >= 0:
            def greet():
                for dx in steps(dz, dy):
                    pl.semaphore_signal(
                        barrier, inc=1, device_id=place(dz, dy, dx), device_id_type=MESH
                    )
            when(dz, dy, greet)

    for load in loads[:3]:
        load.wait()
    for z in range(nz):
        rows = pl.ds(z * ny, ny)
        rho = stack[rows, :]
        start = raw[rows, :]
        p = start
        for _ in range(COOL_STEPS):
            p = p / (1.0 + cool_rate * jnp.sqrt(rho * p))
        mark = jnp.full(p.shape, marks[iz * nz + z], jnp.int32)
        stack[pl.ds(4 * plane + z * ny, ny), :] = jnp.where(mark == 1, p, start)

    for load in loads[3:]:
        load.wait()

    def y_rows(f, y):
        return stack[pl.ds(f * plane + y, nz, stride=ny), :]

    def z_rows(f, z):
        return stack[pl.ds(f * plane + z * ny, ny), :]

    def one_row(f, z, y):
        return stack[pl.ds(f * plane + z * ny + y, 1), :]

    zf, yf = FIELDS * ny, FIELDS * nz
    for f in range(FIELDS):
        for d, at in ((0, 0), (1, ny - 1)):
            sbuf[d, pl.ds(f * nz, nz), :] = y_rows(f, at)
        for d, at in ((2, 0), (3, nz - 1)):
            sbuf[d, pl.ds(f * ny, ny), :] = z_rows(f, at)
        for d in range(4, 8):
            dz, dy = DIRS[d]
            sbuf[d, pl.ds(f, 1), :] = one_row(f, 0 if dz < 0 else nz - 1, 0 if dy < 0 else ny - 1)
    sbuf[0, pl.ds(yf, nz), :] = y_rows(FY, 1)
    sbuf[2, pl.ds(zf, ny), :] = z_rows(FZ, 1)
    sbuf[5, pl.ds(FIELDS, 1), :] = one_row(FZ, 1, ny - 1)
    sbuf[6, pl.ds(FIELDS, 1), :] = one_row(FY, nz - 1, 1)
    size = (yf + nz, yf, zf + ny, zf, 16, 16, 16, 16)

    pl.semaphore_wait(
        barrier,
        2 + sum(
            exists(dz, dy).astype(jnp.int32) * len(steps(dz, dy)) for dz, dy in DIRS if dy <= 0
        ),
    )

    def ready_at(dz, dx):
        return ready.at[3 * (dz + 1) + dx + 1]

    for dz, dy in DIRS:
        if dy < 0:
            def answer():
                for dx in steps(dz, dy):
                    pl.semaphore_signal(
                        ready_at(dz, dx), inc=1, device_id=place(dz, dy, dx), device_id_type=MESH
                    )
            when(dz, dy, answer)

    def message(dz, dy, dx):
        d = ALL.index((dz, dy))
        if dx == 0:
            rows = pl.ds(0, size[d - 1])
            src, dst = sbuf.at[d - 1, rows], rbuf.at[d - 1, rows]
        elif d == 0:
            rows = pl.ds(0, 9) if dx < 0 else pl.ds(16, 8)
            src, dst = xsend.at[rows], xrecv.at[rows]
        else:
            at = 2 * d + (dx > 0)
            src, dst = esend.at[at, pl.ds(0, 1)], erecv.at[at, pl.ds(0, 1)]
        return pltpu.make_async_remote_copy(
            src_ref=src,
            dst_ref=dst,
            send_sem=send_sem.at[3 * d + dx + 1],
            recv_sem=recv_sem.at[3 * d + dx + 1],
            device_id=place(dz, dy, dx),
            device_id_type=MESH,
        )

    def post(want, sides):
        for dz, dy in ALL:
            if dy == want:
                def go():
                    for dx in steps(dz, dy):
                        if dx in sides:
                            if dy > 0:
                                pl.semaphore_wait(ready_at(-dz, -dx), 1)
                            message(dz, dy, dx).start()
                when(dz, dy, go)

    post(-1, (0,))
    lane = lax.broadcasted_iota(jnp.int32, (8, 128), 1)
    member = lax.broadcasted_iota(jnp.int32, (8, 128), 0)

    def end_lanes(parts, place_of):
        found = None
        for f, part in enumerate(parts):
            at = 8 * place_of(f)
            moved = pltpu.roll(part, (at + 3) % nx, 1)
            if found is None:
                found = moved
            else:
                found = jnp.where(jnp.logical_and(lane >= at, lane < at + 8), moved, found)
        return found

    for z in range(nz):
        own = end_lanes([z_rows(f, z) for f in range(FIELDS)], lambda f: FIELDS - 1 - f)
        lines = [z] + ([-1] if z == 0 else []) + ([nz, nz + 1] if z == nz - 1 else [])
        for to in lines:
            at = (to + 1) * wide
            edge[pl.ds(at + 1, ny), :] = own
            edge[pl.ds(at, 1), :] = own[:1]
            for beyond in range(ny + 1, min(wide, 128 - at)):
                edge[pl.ds(at + beyond, 1), :] = own[ny - 1:]
    flat[...] = edge[...].T
    zat = jnp.zeros((8, 128), jnp.int32) - 1
    for j in range(1, nz + 3):
        zat = zat + (lane >= j * wide).astype(jnp.int32)
    yat = lane - (zat + 1) * wide - 1
    far = 4 * 128
    low_y, high_y = jnp.where(has_y[-1], 0, -far), jnp.where(has_y[1], ny, far)
    low_z, high_z = jnp.where(has_z[-1], 0, -far), jnp.where(has_z[1], nz, far)

    def turn(values, by):
        return pltpu.roll(values, by % 128, 1)

    def slant(values, by, step):
        by = by % 128
        if by + (FIELDS - 1) * step > 128:
            values, by = turn(values, by), 0
        return pltpu.roll(values, by, 1, stride=step, stride_axis=0)

    def folded(values, extra, dz, dy, dx):
        y0, z0 = (0 if dy < 0 else ny - 1), (0 if dz < 0 else nz - 1)
        if dz == 0:
            from_, step, slot, next_ = y0 + 1, 1, yat + 1, FY
        elif dy == 0:
            from_, step, slot, next_ = (z0 + 1) * wide, wide, zat + 1, FZ
        else:
            from_, step, slot, next_ = (z0 + 1) * wide + y0 + 1, 1, lane, None
        picked = jnp.where(slot == member + 1, slant(values, step - from_, step), 0.0)
        row = jnp.sum(picked, axis=0, keepdims=True)
        if dx < 0:
            return jnp.where(slot[:1] == 0, turn(extra, -from_), row)
        if dz + dy < 0 and dz * dy == 0:
            second = values[FIELDS - 1 - next_:FIELDS - next_]
            return jnp.where(slot[:1] == 0, turn(second, -from_ - step), row)
        return row

    def unfolded(dz, dy, dx):
        row = erecv[2 * ALL.index((-dz, -dy)) + (dx < 0), pl.ds(0, 1), :]
        yt, zt = (-1 if dy < 0 else ny), (-1 if dz < 0 else nz)
        if dz == 0:
            to, step = yt + 1, 1
        elif dy == 0:
            to, step = (zt + 1) * wide, wide
        else:
            to, step = (zt + 1) * wide + yt + 1, 1
        out = slant(jnp.broadcast_to(row, (FIELDS, 128)), to - FIELDS * step, step)
        if dx < 0 and (dz, dy) in ((0, 1), (1, 0)):
            f, second = (FY, yat > ny) if dz == 0 else (FZ, zat > nz)
            chosen = jnp.logical_and(second, member == f)
            out = jnp.where(chosen, turn(row, to + step), out)
        return out, turn(row, to)

    to_left, to_right = flat[pl.ds(3, FIELDS, stride=8), :], flat[pl.ds(2, FIELDS, stride=8), :]
    extra = flat[pl.ds((FIELDS - 1 - FX) * 8 + 4, 1), :]
    for f in range(FIELDS):
        r = FIELDS - 1 - f
        xsend[pl.ds(f, 1), :] = to_left[r:r + 1]
        xsend[pl.ds(16 + f, 1), :] = to_right[r:r + 1]
    xsend[pl.ds(FIELDS, 1), :] = extra
    for dz, dy in DIRS:
        at = 2 * ALL.index((dz, dy))
        esend[at, pl.ds(0, 1), :] = folded(to_left, extra, dz, dy, -1)
        esend[at + 1, pl.ds(0, 1), :] = folded(to_right, extra, dz, dy, 1)

    post(-1, (-1, 1))
    post(0, (0, -1, 1))
    for f in range(FIELDS):
        for z in range(nz):
            pad[pl.ds(f * 128 + (z + 1) * wide + 1, ny), :] = z_rows(f, z)

    for d in range(4):
        dz, dy = DIRS[d]
        own = DIRS.index((-dz, -dy))
        step = nz if dz == 0 else ny

        @pl.when(jnp.logical_not(exists(-dz, -dy)))
        def _():
            for f in range(FIELDS):
                rbuf[d, pl.ds(f * step, step), :] = sbuf[own, pl.ds(f * step, step), :]
            if dz + dy < 0:
                f = FY if dz == 0 else FZ
                rbuf[d, pl.ds(FIELDS * step, step), :] = sbuf[own, pl.ds(f * step, step), :]

    for z in range(nz):
        rim[pl.ds((z + 1) * wide + 1, ny), :] = end_lanes(
            [z_rows(f, z) for f in range(FIELDS)], lambda f: f
        )

    def aside(values, by):
        return pltpu.roll(values, by % nx, 1)

    def tiers(values, by):
        return pltpu.roll(values, by % ny, 0)

    def keep(axis, start, count, stride, found):
        for m, value in found.items():
            flux[7 * axis + m, pl.ds(start, count, stride=stride), :] = value

    def start_of(z, y):
        return (z + 1) * wide + y + 1

    past = None
    for z in range(nz):
        rho, vel, pre = z_rows(0, z), [z_rows(1 + c, z) for c in range(3)], z_rows(4, z)
        faces = [z_rows(5 + c, z) for c in range(3)]
        cell = cell_terms(rho, vel, pre)
        centre = [
            0.5 * (faces[0] + z_rows(FZ, z + 1)) if z < nz - 1 else None,
            0.5 * (faces[1] + tiers(faces[1], -1)),
            0.5 * (faces[2] + aside(faces[2], -1)),
        ]
        if z > 0:
            lower = state_terms(past[0], past[1], past[2], [faces[0]] + past[3][1:], 0)
            upper = state_terms(cell, vel, pre, [faces[0]] + centre[1:], 0)
            keep(0, start_of(z, 0), ny, 1, hll(lower, upper, 0))
        if z < nz - 1:
            for axis, below in ((1, lambda v: tiers(v, 1)), (2, lambda v: aside(v, 1))):
                lrho, lvel = below(rho), [below(v) for v in vel]
                lcell = (
                    lrho, below(cell[1]), below(cell[2]), below(cell[3]),
                    [lrho * v for v in lvel],
                )
                lmag = [faces[c] if c == axis else below(centre[c]) for c in range(3)]
                umag = [faces[c] if c == axis else centre[c] for c in range(3)]
                lower = state_terms(lcell, lvel, below(pre), lmag, axis)
                upper = state_terms(cell, vel, pre, umag, axis)
                keep(axis, start_of(z, 0), ny, 1, hll(lower, upper, axis))
        past = (cell, vel, pre, centre)

    post(1, (0,))
    post(1, (-1, 1))

    for dz, dy in ALL:
        def sent():
            for dx in steps(dz, dy):
                message(dz, dy, dx).wait_send()
        when(dz, dy, sent)

    for d in range(8):
        dz, dy = DIRS[d]

        @pl.when(exists(-dz, -dy))
        def _():
            message(dz, dy, 0).wait_recv()

    for f in range(FIELDS):
        base = f * 128
        pad[pl.ds(base + wide, nz, stride=wide), :] = rbuf[1, pl.ds(f * nz, nz), :]
        pad[pl.ds(base + wide + ny + 1, nz, stride=wide), :] = rbuf[0, pl.ds(f * nz, nz), :]
        pad[pl.ds(base + 1, ny), :] = rbuf[3, pl.ds(f * ny, ny), :]
        pad[pl.ds(base + (nz + 1) * wide + 1, ny), :] = rbuf[2, pl.ds(f * ny, ny), :]
    pad[pl.ds(FY * 128 + wide + ny + 2, nz, stride=wide), :] = rbuf[0, pl.ds(yf, nz), :]
    pad[pl.ds(FZ * 128 + (nz + 2) * wide + 1, ny), :] = rbuf[2, pl.ds(zf, ny), :]

    def spot(z, y):
        return (z + 1) * wide + y + 1

    for d in range(4, 8):
        dz, dy = DIRS[d]
        zg, yg = (nz if dz < 0 else -1), (ny if dy < 0 else -1)
        zc, yc = min(max(zg, 0), nz - 1), min(max(yg, 0), ny - 1)
        ydir, zdir = DIRS.index((0, dy)), DIRS.index((dz, 0))

        def chosen(corner, along_y, along_z):
            edge_of = jnp.where(has_z[-dz], along_z, along_y)
            return jnp.where(jnp.logical_and(has_z[-dz], has_y[-dy]), corner, edge_of)

        cells = chosen(
            rbuf[d, pl.ds(0, FIELDS), :],
            rbuf[ydir, pl.ds(zc, FIELDS, stride=nz), :],
            rbuf[zdir, pl.ds(yc, FIELDS, stride=ny), :],
        )
        pad[pl.ds(spot(zg, yg), FIELDS, stride=128), :] = cells
        mine = jnp.logical_and(lane >= 8 * member, lane < 8 * member + 8)
        rim[pl.ds(spot(zg, yg), 1), :] = jnp.sum(
            jnp.where(mine, slant(cells, 3, 8), 0.0), axis=0, keepdims=True
        )
        if d == 5:
            beyond = chosen(
                rbuf[d, pl.ds(FIELDS, 1), :],
                rbuf[ydir, pl.ds(FZ * nz + zc, 1), :],
                rbuf[zdir, pl.ds(zf + yc, 1), :],
            )
            pad[pl.ds(FZ * 128 + spot(nz + 1, -1), 1), :] = beyond
            rim[pl.ds(spot(nz + 1, -1), 1), :] = turn(beyond, 8 * FZ + 3)
        if d == 6:
            beyond = chosen(
                rbuf[d, pl.ds(FIELDS, 1), :],
                rbuf[ydir, pl.ds(yf + zc, 1), :],
                rbuf[zdir, pl.ds(FY * ny + yc, 1), :],
            )
            pad[pl.ds(FY * 128 + spot(-1, ny + 1), 1), :] = beyond
            rim[pl.ds(spot(-1, ny + 1), 1), :] = turn(beyond, 8 * FY + 3)

    for d, step, rows in (
        (1, nz, pl.ds(wide, nz, stride=wide)),
        (0, nz, pl.ds(wide + ny + 1, nz, stride=wide)),
        (3, ny, pl.ds(1, ny)),
        (2, ny, pl.ds((nz + 1) * wide + 1, ny)),
    ):
        rim[rows, :] = end_lanes(
            [rbuf[d, pl.ds(f * step, step), :] for f in range(FIELDS)], lambda f: f
        )
    rim[pl.ds(wide + ny + 2, nz, stride=wide), :] = turn(rbuf[0, pl.ds(yf, nz), :], 8 * FY + 3)
    rim[pl.ds((nz + 2) * wide + 1, ny), :] = turn(rbuf[2, pl.ds(zf, ny), :], 8 * FZ + 3)
    flat[...] = rim[...].T
    for row, at in enumerate((0, 1, 2, 5, 6, 7)):
        ext[pl.ds(at, FIELDS, stride=8), :] = flat[pl.ds(row, FIELDS, stride=8), :]

    away = (wide, 1)

    def border(axis, start, count, stride, want):
        def load(f, at):
            return pad[pl.ds(f * 128 + at, count, stride=stride), :]

        def state(at):
            vel = [load(1 + c, at) for c in range(3)]
            pre = load(4, at)
            cell = cell_terms(load(0, at), vel, pre)
            centre = [None] * 3
            for c in range(3):
                if c != axis:
                    face = load(5 + c, at)
                    after = aside(face, -1) if c == 2 else load(5 + c, at + away[c])
                    centre[c] = 0.5 * (face + after)
            return cell, vel, pre, centre

        normal = load(5 + axis, start)
        cell, vel, pre, centre = state(start)
        if axis == 2:
            lvel = [aside(v, 1) for v in vel]
            lrho = aside(cell[0], 1)
            lcell = (
                lrho, aside(cell[1], 1), aside(cell[2], 1), aside(cell[3], 1),
                [lrho * v for v in lvel],
            )
            lpre = aside(pre, 1)
            lcentre = [aside(centre[0], 1), aside(centre[1], 1), None]
        else:
            lcell, lvel, lpre, lcentre = state(start - away[axis])
        lcentre[axis] = centre[axis] = normal
        lower = state_terms(lcell, lvel, lpre, lcentre, axis)
        upper = state_terms(cell, vel, pre, centre, axis)
        keep(axis, start, count, stride, hll(lower, upper, axis, want))

    def across(z):
        return start_of(z, 0), ny, 1

    def along(y):
        return start_of(0, y), nz, wide

    every = range(7)
    border(0, *across(0), every)
    border(0, *across(nz), every)
    border(0, *along(ny - 1), every)
    border(0, start_of(0, -1), nz + 1, wide, (5,))
    border(0, *along(ny), (5,))
    border(1, *along(0), every)
    border(1, *along(ny), every)
    border(1, *across(nz - 1), every)
    border(1, start_of(-1, 0), ny + 1, 1, (5,))
    border(1, *across(nz), (5,))
    border(2, *along(ny - 1), every)
    border(2, *across(nz - 1), every)
    border(2, *along(-1), (6,))
    border(2, *along(ny), (6,))
    border(2, *across(-1), (5,))
    border(2, *across(nz), (5,))

    for dz, dy in ALL:
        def arrived():
            for dx in steps(-dz, -dy):
                if dx != 0:
                    message(-dz, -dy, dx).wait_recv()
        when(dz, dy, arrived)

    slab = iz * nz - 1
    zglobal = zat[:8] + (slab + 1)
    height = (2 * zglobal + 1 - nz * gz).astype(jnp.float32) * (1.0 / (nz * gz))
    pull = -gravity * courant * height

    def gather(dx):
        out, extra = (0, 8) if dx > 0 else (16, 16)
        out, extra = xrecv[pl.ds(out, FIELDS), :], xrecv[pl.ds(extra, 1), :]
        in_y, in_z = {-1: yat < low_y, 1: yat >= high_y}, {-1: zat < low_z, 1: zat >= high_z}
        for dz, dy in DIRS:
            if (dz, dy, dx) not in SKIP:
                if dz == 0:
                    zone = in_y[dy]
                elif dy == 0:
                    zone = in_z[dz]
                else:
                    zone = jnp.logical_and(in_y[dy], in_z[dz])
                values, more = unfolded(dz, dy, dx)
                out = jnp.where(zone, values, out)
                extra = jnp.where(zone[:1], more, extra)
        return out, extra

    members, extra = gather(1)
    ext[pl.ds(3, FIELDS, stride=8), :] = members
    ext[pl.ds(4, FIELDS, stride=8), :] = gather(-1)[0]

    def up(values, axis):
        if axis == 2:
            return pltpu.roll(values, 7, 0)
        return pltpu.roll(values, 128 - (wide if axis == 0 else 1), 1)

    def down(values, axis):
        if axis == 2:
            return pltpu.roll(values, 1, 0)
        return pltpu.roll(values, wide if axis == 0 else 1, 1)

    def outer():
        now = [ext[pl.ds(8 * f, 8), :] for f in range(FIELDS)]
        rho, vel, pre, faces = now[0], now[1:4], now[4], now[5:8]
        centre = [
            0.5 * (faces[0] + up(faces[0], 0)),
            0.5 * (faces[1] + up(faces[1], 1)),
            0.5 * (faces[2] + jnp.where(member == 3, extra, up(faces[2], 2))),
        ]
        cell = cell_terms(rho, vel, pre)
        fluxes = []
        for axis in range(3):
            lrho, lvel = down(rho, axis), [down(v, axis) for v in vel]
            lcell = (
                lrho, down(cell[1], axis), down(cell[2], axis), down(cell[3], axis),
                [lrho * v for v in lvel],
            )
            lmag = [faces[c] if c == axis else down(centre[c], axis) for c in range(3)]
            umag = [faces[c] if c == axis else centre[c] for c in range(3)]
            lower = state_terms(lcell, lvel, down(pre, axis), lmag, axis)
            upper = state_terms(cell, vel, pre, umag, axis)
            fluxes.append(hll(lower, upper, axis))
        squared = centre[0] * centre[0] + centre[1] * centre[1] + centre[2] * centre[2]
        base = [rho] + list(cell[4]) + [cell[3] + 0.5 * squared]
        fz, fy, fx = fluxes

        def after(values):
            return up(values, 2)

        def before(values):
            return down(values, 2)

        outs = []
        for m in range(5):
            change = up(fz[m], 0) - fz[m] + up(fy[m], 1) - fy[m] + after(fx[m]) - fx[m]
            value = base[m] - courant * change
            if m == 1:
                value = value + rho * pull
            if m == 4:
                value = value + cell[4][0] * pull
            outs.append(value)
        ex = 0.25 * (fz[5] + down(fz[5], 1) - fy[5] - down(fy[5], 0))
        ey = 0.25 * (fx[5] + down(fx[5], 0) - fz[6] - before(fz[6]))
        ez = 0.25 * (fy[6] + before(fy[6]) - fx[6] - down(fx[6], 1))
        outs.append(faces[0] - courant * ((after(ey) - ey) - (up(ex, 1) - ex)))
        outs.append(faces[1] - courant * ((up(ex, 0) - ex) - (after(ez) - ez)))
        outs.append(faces[2] - courant * ((up(ez, 1) - ez) - (up(ey, 0) - ey)))
        return outs

    for m, value in enumerate(outer()):
        edge[pl.ds(3 * m, 2), :] = value[1:3]
        edge[pl.ds(3 * m + 2, 1), :] = value[5:6]
    turned[...] = edge[...].T

    def got(axis, m, at):
        return flux[7 * axis + m, pl.ds(at, ny), :]

    def ex_at(at):
        return 0.25 * (got(0, 5, at) + got(0, 5, at - 1) - got(1, 5, at) - got(1, 5, at - wide))

    def ey_at(at):
        one = got(0, 6, at)
        return 0.25 * (got(2, 5, at) + got(2, 5, at - wide) - one - aside(one, 1))

    def ez_at(at):
        one = got(1, 6, at)
        return 0.25 * (one + aside(one, 1) - got(2, 6, at) - got(2, 6, at - 1))

    ex_here, ey_here = ex_at(start_of(0, 0)), ey_at(start_of(0, 0))
    for z in range(nz):
        at = start_of(z, 0)
        rho, vel, pre = z_rows(0, z), [z_rows(1 + c, z) for c in range(3)], z_rows(4, z)
        faces = [z_rows(5 + c, z) for c in range(3)]
        above = pad[pl.ds(FZ * 128 + at + wide, ny), :]
        beside = pad[pl.ds(FY * 128 + at + 1, ny), :]
        centre = [
            0.5 * (faces[0] + above), 0.5 * (faces[1] + beside),
            0.5 * (faces[2] + aside(faces[2], -1)),
        ]
        cell = cell_terms(rho, vel, pre)
        squared = centre[0] * centre[0] + centre[1] * centre[1] + centre[2] * centre[2]
        start = [rho] + list(cell[4]) + [cell[3] + 0.5 * squared]
        level = jnp.zeros((ny, nx), jnp.int32) + (2 * (iz * nz + z) + 1 - nz * gz)
        force = -gravity * courant * (level.astype(jnp.float32) * (1.0 / (nz * gz)))
        values = []
        for m in range(5):
            fx, fy, fz = got(2, m, at), got(1, m, at), got(0, m, at)
            change = (
                aside(fx, -1) - fx + got(1, m, at + 1) - fy + got(0, m, at + wide) - fz
            )
            value = start[m] - courant * change
            if m == 1:
                value = value + rho * force
            if m == 4:
                value = value + cell[4][0] * force
            values.append(value)
        ex, ey, ez = ex_here, ey_here, ez_at(at)
        ex_here, ey_here = ex_at(at + wide), ey_at(at + wide)
        values.append(faces[0] - courant * ((aside(ey, -1) - ey) - (ex_at(at + 1) - ex)))
        values.append(faces[1] - courant * ((ex_here - ex) - (aside(ez, -1) - ez)))
        values.append(faces[2] - courant * ((ez_at(at + 1) - ez) - (ey_here - ey)))
        for m in range(FIELDS):
            res[pl.ds(m * plane + z * ny, ny), :] = values[m]


def unload_kernel(sizes, res, turned, cons_ref, face_ref, out, sem):
    nz, ny, nx = sizes
    plane, wide = nz * ny, ny + 3
    column = lax.broadcasted_iota(jnp.int32, (ny, nx), 1)
    ends = jnp.logical_or(column == 0, column >= nx - 2)
    copies = []
    for m in range(FIELDS):
        for z in range(nz):
            rows = pl.ds(m * plane + z * ny, ny)
            ring = turned[pl.ds((z + 1) * wide + 1, ny), :]
            out[rows, :] = jnp.where(
                ends, pltpu.roll(ring, (nx - 2 - 3 * m) % nx, 1), res[rows, :]
            )
        if m in (2, 4, 7):
            first = {2: 0, 4: 3, 7: 5}[m]
            count = (m + 1 - first) * plane
            target, base = (cons_ref, first * plane) if m < 5 else (face_ref, 0)
            copies.append(pltpu.make_async_copy(
                out.at[pl.ds(first * plane, count)], target.at[pl.ds(base, count)], sem.at[m]
            ))
            copies[-1].start()
    for copy in copies:
        copy.wait()


def on_device(sizes, density, velocity, pressure, field, corona):
    nz, ny, nx = density.shape
    gz, gy, gx = sizes
    plane = nz * ny
    hbm = pl.BlockSpec(memory_space=pltpu.HBM)
    vmem = pl.BlockSpec(memory_space=pltpu.VMEM)
    f32 = jnp.float32
    rows = FIELDS * max(nz, ny) + max(nz, ny)
    result, ends = pl.pallas_call(
        functools.partial(kernel, (nz, ny, nx, gz, gy, gx)),
        out_shape=(pltpu.VMEM((FIELDS * plane, nx), f32), pltpu.VMEM((128, 128), f32)),
        in_specs=[hbm] * 5,
        out_specs=(vmem, vmem),
        scratch_shapes=[
            pltpu.VMEM((FIELDS * plane, nx), f32),
            pltpu.VMEM((plane, nx), f32),
            pltpu.SMEM(corona.shape, jnp.int32),
            pltpu.VMEM((8, rows, nx), f32),
            pltpu.VMEM((8, rows, nx), f32),
            pltpu.VMEM((FIELDS * 128, nx), f32),
            pltpu.VMEM((FIELDS * 8, 128), f32),
            pltpu.VMEM((128, 128), f32),
            pltpu.VMEM((24, 128), f32),
            pltpu.VMEM((24, 128), f32),
            pltpu.VMEM((18, 8, 128), f32),
            pltpu.VMEM((18, 8, 128), f32),
            pltpu.VMEM((21, 128, nx), f32),
            pltpu.VMEM((128, 128), f32),
            pltpu.VMEM((128, 128), f32),
            pltpu.SemaphoreType.DMA((5,)),
            pltpu.SemaphoreType.DMA((27,)),
            pltpu.SemaphoreType.DMA((27,)),
            pltpu.SemaphoreType.REGULAR((9,)),
        ],
        compiler_params=pltpu.CompilerParams(
            collective_id=0, has_side_effects=True, vmem_limit_bytes=16 << 20
        ),
    )(
        *(
            pltpu.with_memory_space_constraint(x, pltpu.HBM)
            for x in (
                density.reshape(plane, nx),
                velocity.reshape(3 * plane, nx),
                pressure.reshape(plane, nx),
                field.reshape(3 * plane, nx),
                corona,
            )
        )
    )
    conserved, faces = pl.pallas_call(
        functools.partial(unload_kernel, (nz, ny, nx)),
        out_shape=(
            jax.ShapeDtypeStruct((5 * plane, nx), f32),
            jax.ShapeDtypeStruct((3 * plane, nx), f32),
        ),
        in_specs=[vmem, vmem],
        out_specs=(hbm, hbm),
        scratch_shapes=[
            pltpu.VMEM((FIELDS * plane, nx), f32),
            pltpu.SemaphoreType.DMA((FIELDS,)),
        ],
        compiler_params=pltpu.CompilerParams(vmem_limit_bytes=16 << 20),
    )(result, ends)
    return conserved.reshape(5, nz, ny, nx), faces.reshape(3, nz, ny, nx)


def solution(mesh):
    sizes = tuple(mesh.shape[axis] for axis in ("gz", "gy", "gx"))
    return jax.shard_map(
        functools.partial(on_device, sizes),
        mesh=mesh,
        in_specs=(
            P("gz", "gy", "gx"),
            P(None, "gz", "gy", "gx"),
            P("gz", "gy", "gx"),
            P(None, "gz", "gy", "gx"),
            P(),
        ),
        out_specs=(P(None, "gz", "gy", "gx"), P(None, "gz", "gy", "gx")),
        check_vma=False,
    )
```
